256 devices in a mesh: ctx: 16 (over z, core), exp: 16 (over x, y).
Axes of the slice: x: 4, y: 4, z: 8, core: 2. Of those that a mesh axis runs over, the one named last changes fastest.
Arguments:
- x_inner: bfloat16 [16384, 4096], P('ctx', 'exp'), may hold values from -6 to 6
- bc_input: bfloat16 [16384, 256], P('ctx'), may hold values from -6 to 6
- gate_input: bfloat16 [16384, 4096], P('ctx', 'exp'), may hold values from -22 to 22
- conv_weight: float32 [4, 4096], P(None, 'exp'), may hold values from -3 to 3
- bc_conv_weight: float32 [4, 256], replicated, may hold values from -3 to 3
- step_size: float32 [16384, 64], P('ctx', 'exp'), may hold values from 0.002 to 0.05
- log_decay: float32 [16384, 64], P('ctx', 'exp'), may hold values from -1 to 0
- skip_gain: float32 [64], P('exp'), may hold values from 0.5 to 1.5
- norm_gain: float32 [4096], P('exp'), may hold values from 0.25 to 1.75
- out_weight: bfloat16 [4096, 2048], P('exp'), may hold values from -0.09375 to 0.09375
- residual: bfloat16 [16384, 2048], P(('ctx', 'exp')), may hold values from -6 to 6
- moe_gain: float32 [2048], replicated, may hold values from 0.25 to 1.75
- expert_ids: int32 [16384, 4], P(('ctx', 'exp')), may hold values from 0 to 31, all different within a row; in each aligned block of 64 rows (0 to 63, 64 to 127, ...) at most 9 rows name the same one
- route_weights: float32 [16384, 4], P(('ctx', 'exp')), may hold values from 0.1 to 0.6
- gate_up_weight: bfloat16 [32, 2048, 1408], P('exp', 'ctx'), may hold values from -0.125 to 0.125
- down_weight: bfloat16 [32, 704, 2048], P('exp', None, 'ctx'), may hold values from -0.21875 to 0.21875
- out_grad: bfloat16 [16384, 2048], P(('ctx', 'exp')), may hold values from -6 to 6
Outputs:
- layer_output: bfloat16 [16384, 2048], P(('ctx', 'exp'))
- residual_grad: bfloat16 [16384, 2048], P(('ctx', 'exp'))
- route_grads: float32 [16384, 4], P(('ctx', 'exp'))
The draws below stay inside these ranges and needn't reach their ends.
Inputs may be any that keep to these rules, and one draw needn't show every extreme that they name: `expert_ids`: within the rows of one device (aligned blocks of 64 tokens) no expert is named by more than 9 rows, a bound that some block reaches; each row names 4 different experts.
All inputs are finite; a program needn't handle non-finite values.
Results may differ from the reference program's by a relative error of at most 0.03.
Values may be sent and summed in bfloat16 or wider, within the bound.
No kernel may reach another device: no remote copies, remote signals or barrier semaphores. Data moves between devices by JAX's collectives and lax.ppermute only.
A program may use at most 128 MiB of HBM per device.

```python
import math
import jax
import jax.numpy as jnp
import numpy as np
from jax import lax

D = 2048
HEADS = 64
HEAD_DIM = 64
STATE = 128
KERNEL = 4
SPAN = 128
MOE_FF = 704
TOP = 4
TOK_DEV = 64
INNER = 4096
ROWS_DEV = 1024
SEQUENCE_TOKENS = 16384
EXPERTS = 32
CAP = 9
N_EXP = 16


def draw_log_decay(key, part):
    random_subkeys = jax.random.split(key, 7)
    head_order = jax.random.permutation(random_subkeys[0], HEADS)
    slow_heads = head_order < HEADS // 2
    slow_rate = jnp.exp(jax.random.uniform(random_subkeys[1], (HEADS,), jnp.float32, jnp.log(0.1 / SEQUENCE_TOKENS), jnp.log(1.0 / SEQUENCE_TOKENS)))
    fast_rate = jnp.exp(jax.random.uniform(random_subkeys[2], (HEADS,), jnp.float32, jnp.log(1.0 / 50.0), jnp.log(1.0 / 30.0)))
    head_decay_rate = jnp.where(slow_heads, slow_rate, fast_rate)
    coarse_multiplier = jax.random.uniform(random_subkeys[3], (SEQUENCE_TOKENS, HEADS), jnp.float32, 0.5, 1.5)
    segments = SEQUENCE_TOKENS // ROWS_DEV
    device_multiplier = jnp.exp(jax.random.uniform(random_subkeys[4], (segments, HEADS), jnp.float32, -0.7, 0.7))
    device_multiplier = jnp.repeat(device_multiplier, ROWS_DEV, axis=0)
    spike_groups = jax.random.uniform(random_subkeys[5], (SEQUENCE_TOKENS, 1), jnp.float32) < 3.0 / SEQUENCE_TOKENS
    spike_loss_value = jnp.log(jax.random.uniform(random_subkeys[6], (SEQUENCE_TOKENS, 1), jnp.float32, 0.5, 0.8))
    return -head_decay_rate[None, :] * coarse_multiplier * device_multiplier + jnp.where(spike_groups, spike_loss_value, 0.0)


def draw_gate_input(key, part):
    random_subkeys = jax.random.split(key, 2)
    channel_ramp = jnp.exp(jnp.log(3.0) * jnp.arange(INNER, dtype=jnp.float32) / (INNER - 1))
    jitter = jax.random.uniform(random_subkeys[1], (INNER,), jnp.float32, 0.6, 1.4)
    base_values = jnp.clip(jax.random.normal(random_subkeys[0], (SEQUENCE_TOKENS, INNER), jnp.float32), -5.0, 5.0)
    return (base_values * (channel_ramp * jitter)[None, :]).astype(jnp.bfloat16)


def levels(key, extent, shards, smallest, high):
    level = 1.0
    for position, parts in shards:
        draws = jax.random.uniform(jax.random.fold_in(jax.random.fold_in(key, 6), position), (parts,), jnp.float32, smallest / len(shards), high / len(shards))
        level = level * jnp.repeat(jnp.exp(draws), extent[position] // parts).reshape((-1,) + (1,) * (len(extent) - 1 - position))
    return level


def shared_out(rng, own, number, rows, amount, top, bound, lean):
    ranking = jax.random.permutation(rng, amount)
    packed, ordinary = load_shares(amount, rows * top, bound, lean, True), load_shares(amount, rows * top, bound, lean, False)
    places = jnp.arange(amount)

    def named(sizes, turn):
        used = int((sizes > 0).sum())
        fixed = max(1, used // 4)
        passed = fixed + (places - fixed + turn * (used - fixed)) % max(1, amount - fixed)
        return jnp.zeros((amount,), jnp.int32).at[ranking[jnp.where(places < fixed, places, passed)]].set(jnp.asarray(sizes, jnp.int32))

    sizes = jnp.where(number % 4 == 0, named(packed, number // 4), named(ordinary, number - number // 4 - 1))
    mixed = jax.random.permutation(jax.random.fold_in(own, 3), amount)
    giver, taker = mixed[0:amount // 2 * 2:2], mixed[1:amount // 2 * 2:2]
    room = jnp.minimum(sizes[giver] - 1, bound - sizes[taker]) // 2
    room = jnp.where((giver == ranking[0]) | (taker == ranking[0]) | (sizes[taker] == 0), 0, jnp.maximum(room, 0))
    passed = jax.random.randint(jax.random.fold_in(own, 4), (amount // 2,), 0, 1 << 20) % (room + 1)
    sizes = sizes.at[giver].add(-passed).at[taker].add(passed)
    members = jnp.searchsorted(jnp.cumsum(sizes), jnp.arange(rows * top), side="right").astype(jnp.int32)
    grid = members.reshape(top, rows).T
    grid = grid[jax.random.permutation(jax.random.fold_in(own, 1), rows)]
    turn = jax.random.randint(jax.random.fold_in(own, 2), (rows, 1), 0, top)
    return jnp.take_along_axis(grid, (jnp.arange(top)[None, :] + turn) % top, axis=1)


def load_shares(amount, total, limit, slope, full):
    loads = [(1 << 20) // math.isqrt(standing ** slope) + 1 for standing in range(1, amount + 1)]
    largest = limit if full else min(limit, max(-(-total // amount), total * loads[0] // sum(loads)))
    least = 1 if total - largest >= amount - 1 else 0
    counts, spare = [largest] + [least] * (amount - 1), total - largest - least * (amount - 1)
    while spare > 0:
        candidates = [i for i in range(1, amount) if counts[i] < largest] or [i for i in range(1, amount) if counts[i] < limit]
        mass, remaining = sum([loads[i] for i in candidates]), spare
        for i in candidates:
            extra = min(limit - counts[i], max(1, remaining * loads[i] // mass), spare)
            counts[i] = counts[i] + extra
            spare = spare - extra
    return np.array(counts)


def normal_values(stream_key, dims, spread, bound, cuts=(), kind=jnp.bfloat16):
    drawn = jax.random.normal(stream_key, dims, jnp.float32) * spread
    if len(cuts) > 0:
        drawn = levels(stream_key, dims, cuts, -0.22, 0.18) * drawn
    return jnp.clip(drawn, min=-bound, max=bound).astype(kind)


def setup_inputs(seed: int = 0) -> dict:
    key_of = jax.random.split(jax.random.key(seed), 18)
    x_inner = normal_values(key_of[0], (SEQUENCE_TOKENS, INNER), 1.0, 6.0, ((0, 16), (1, 16)))
    bc_input = normal_values(key_of[1], (SEQUENCE_TOKENS, 2 * STATE), 1.0, 6.0, ((0, 16),))
    gate_input = draw_gate_input(jax.random.fold_in(key_of[17], 71), 0)
    conv_weight = normal_values(key_of[3], (KERNEL, INNER), KERNEL ** -0.5, 3.0, ((1, 16),), jnp.float32)
    bc_conv_weight = normal_values(key_of[4], (KERNEL, 2 * STATE), KERNEL ** -0.5, 3.0, (), jnp.float32)
    step_size = jnp.clip(jnp.exp(math.log(0.05) - 3.218876 * jax.random.uniform(key_of[5], (SEQUENCE_TOKENS, HEADS), jnp.float32) ** levels(key_of[5], (SEQUENCE_TOKENS, HEADS), ((0, 16), (1, 16)), -0.2, 0.2)), 0.002, 0.05)
    log_decay = draw_log_decay(jax.random.fold_in(key_of[17], 71), 0)
    skip_gain = jnp.clip(0.5 + 1.0 * jax.random.uniform(key_of[7], (HEADS,), jnp.float32) ** levels(key_of[7], (HEADS,), ((0, 16),), -0.2, 0.2), 0.5, 1.5)
    norm_gain = jnp.clip(1.0 + 0.15 * jax.random.normal(key_of[8], (INNER,), jnp.float32), 0.25, 1.75)
    out_weight = normal_values(key_of[9], (INNER, D), INNER ** -0.5, 0.09375, ((0, 16),))
    residual = normal_values(key_of[10], (SEQUENCE_TOKENS, D), 1.0, 6.0, ((0, 256),))
    moe_gain = jnp.clip(1.0 + 0.15 * jax.random.normal(key_of[11], (D,), jnp.float32), 0.25, 1.75)
    expert_ids_keys = jax.random.split(jax.random.fold_in(key_of[12], 1), SEQUENCE_TOKENS // TOK_DEV)
    expert_ids_turns = jax.random.permutation(jax.random.fold_in(key_of[12], 3), SEQUENCE_TOKENS // TOK_DEV)
    expert_ids = jax.vmap(lambda own, number: shared_out(jax.random.fold_in(key_of[12], 2), own, number, TOK_DEV, EXPERTS, TOP, CAP, 2))(expert_ids_keys, expert_ids_turns).reshape((SEQUENCE_TOKENS, TOP))
    route_weights = jnp.clip(jnp.exp(math.log(0.6) - 1.7917595 * jax.random.uniform(key_of[13], (SEQUENCE_TOKENS, TOP), jnp.float32) ** levels(key_of[13], (SEQUENCE_TOKENS, TOP), ((0, 256),), -0.2, 0.2)), 0.1, 0.6)
    gate_up_weight = normal_values(key_of[14], (EXPERTS, D, 2 * MOE_FF), D ** -0.5, 0.125, ((0, 16), (1, 16)))
    down_weight = normal_values(key_of[15], (EXPERTS, MOE_FF, D), MOE_FF ** -0.5, 0.21875, ((0, 16), (2, 16)))
    out_grad = normal_values(key_of[16], (SEQUENCE_TOKENS, D), 1.0, 6.0, ((0, 256),))
    return {"x_inner": x_inner, "bc_input": bc_input, "gate_input": gate_input, "conv_weight": conv_weight, "bc_conv_weight": bc_conv_weight, "step_size": step_size, "log_decay": log_decay, "skip_gain": skip_gain, "norm_gain": norm_gain, "out_weight": out_weight, "residual": residual, "moe_gain": moe_gain, "expert_ids": expert_ids, "route_weights": route_weights, "gate_up_weight": gate_up_weight, "down_weight": down_weight, "out_grad": out_grad}


def causal_conv(values, weight):
    kernel_len = weight.shape[0]
    row_total = values.shape[0]
    padded = jnp.pad(values.astype(jnp.float32), ((kernel_len - 1, 0), (0, 0)))
    summed = jnp.zeros((row_total, values.shape[1]), jnp.float32)
    for offset in range(kernel_len):
        summed = summed + weight[offset][None, :] * padded[offset:offset + row_total]
    return summed

def rounded(values):
    return lax.optimization_barrier(values.astype(jnp.bfloat16)).astype(jnp.float32)

def reference(x_inner, bc_input, gate_input, conv_weight, bc_conv_weight, step_size, log_decay, skip_gain, norm_gain, out_weight, residual, moe_gain, expert_ids, route_weights, gate_up_weight, down_weight, out_grad):
    high = lax.Precision.HIGHEST
    conv_x = jax.nn.silu(causal_conv(x_inner, conv_weight)).astype(jnp.bfloat16)
    conv_bc = jax.nn.silu(causal_conv(bc_input, bc_conv_weight)).astype(jnp.bfloat16)
    block_count = SEQUENCE_TOKENS // SPAN
    x_blocks = conv_x.reshape(block_count, SPAN, HEADS, HEAD_DIM)
    b_blocks = conv_bc[:, :STATE].reshape(block_count, SPAN, STATE)
    c_blocks = conv_bc[:, STATE:].reshape(block_count, SPAN, STATE)
    step_blocks = step_size.reshape(block_count, SPAN, HEADS)
    decay_blocks = log_decay.reshape(block_count, SPAN, HEADS)
    causal_mask = (jnp.arange(SPAN)[:, None] >= jnp.arange(SPAN)[None, :])[:, :, None]

    def one_block(held_state, inputs):
        x_block, b_block, c_block, step_block, decay_block = inputs
        cumulative = jnp.cumsum(decay_block, axis=0)
        x_float = x_block.astype(jnp.float32)
        scores = jnp.dot(c_block, b_block.T, preferred_element_type=jnp.float32)
        gap_matrix = cumulative[:, None, :] - cumulative[None, :, :]
        weights = jnp.where(causal_mask, jnp.exp(jnp.where(causal_mask, gap_matrix, 0.0)) * scores[:, :, None] * step_block[None, :, :], 0.0)
        within = jnp.einsum('tsh,shp->thp', rounded(weights), x_float, precision=high)
        entering = rounded(held_state)
        carried = jnp.einsum('tn,hnp->thp', c_block.astype(jnp.float32), entering, precision=high) * jnp.exp(cumulative)[:, :, None]
        tail_scale = jnp.exp(cumulative[-1:, :] - cumulative) * step_block
        scaled_b = rounded(b_block[:, None, :].astype(jnp.float32) * tail_scale[:, :, None])
        block_state = jnp.einsum('lhn,lhp->hnp', scaled_b, x_float, precision=high)
        mixer_out = within + carried + skip_gain[None, :, None] * x_float
        next_state = jnp.exp(cumulative[-1])[:, None, None] * held_state + block_state
        return (next_state, mixer_out)
    last_state, outputs = lax.scan(one_block, jnp.zeros((HEADS, STATE, HEAD_DIM), jnp.float32), (x_blocks, b_blocks, c_blocks, step_blocks, decay_blocks))
    mixer_out = outputs.reshape(SEQUENCE_TOKENS, INNER)
    gated = mixer_out * jax.nn.silu(gate_input.astype(jnp.float32))
    squares = lax.optimization_barrier(jnp.sum(gated * gated, axis=1))
    scaled = (gated * norm_gain[None, :]).astype(jnp.bfloat16)
    group_width = INNER // N_EXP
    summed = jnp.zeros((SEQUENCE_TOKENS, D), jnp.float32)
    for owner_index in range(N_EXP):
        partial_sum = jnp.dot(scaled[:, owner_index * group_width:(owner_index + 1) * group_width], out_weight[owner_index * group_width:(owner_index + 1) * group_width], preferred_element_type=jnp.float32)
        summed = summed + rounded(partial_sum)
    hidden_state = (residual.astype(jnp.float32) + summed * lax.rsqrt(squares / INNER + 1e-05)[:, None]).astype(jnp.bfloat16)
    hidden_f = hidden_state.astype(jnp.float32)
    inv_rms = lax.rsqrt(lax.optimization_barrier(jnp.mean(hidden_f * hidden_f, axis=1)) + 1e-06)
    normed = (hidden_f * inv_rms[:, None] * moe_gain[None, :]).astype(jnp.bfloat16)
    pair_count = SEQUENCE_TOKENS * TOP
    flat_ids = expert_ids.reshape(pair_count).astype(jnp.int32)
    grad_f = out_grad.astype(jnp.float32)
    pair_grads = (route_weights[:, :, None] * grad_f[:, None, :]).astype(jnp.bfloat16).reshape(pair_count, D)
    most_rows = CAP * (SEQUENCE_TOKENS // TOK_DEV)

    def one_expert(carry, inputs):
        outs_all, grads_all = carry
        gu_weight, dn_weight, expert = inputs
        picked = jnp.nonzero(flat_ids == expert, size=most_rows, fill_value=pair_count)[0].astype(jnp.int32)
        safe_index = jnp.minimum(picked, pair_count - 1)
        rows_in = normed[safe_index // TOP]
        projected = jnp.dot(rows_in, gu_weight, preferred_element_type=jnp.float32)
        pre_gate = projected[:, :MOE_FF]
        pre_up = projected[:, MOE_FF:]
        activated = (jax.nn.silu(pre_gate) * pre_up).astype(jnp.bfloat16)
        expert_out = jnp.dot(activated, dn_weight, preferred_element_type=jnp.float32).astype(jnp.bfloat16)
        grads_in = pair_grads[safe_index]
        hidden_grad = jnp.dot(grads_in, dn_weight.T, preferred_element_type=jnp.float32)
        sigmoid_gate = jax.nn.sigmoid(pre_gate)
        grad_gate = hidden_grad * pre_up * sigmoid_gate * (1.0 + pre_gate * (1.0 - sigmoid_gate))
        grad_up = hidden_grad * jax.nn.silu(pre_gate)
        grad_both = jnp.concatenate([grad_gate, grad_up], axis=1).astype(jnp.bfloat16)
        grad_rows = jnp.dot(grad_both, gu_weight.T, preferred_element_type=jnp.float32).astype(jnp.bfloat16)
        outs_all = outs_all.at[picked].set(expert_out, mode='drop')
        grads_all = grads_all.at[picked].set(grad_rows, mode='drop')
        return ((outs_all, grads_all), None)
    start_outs = jnp.zeros((pair_count, D), jnp.bfloat16)
    start_grads = jnp.zeros((pair_count, D), jnp.bfloat16)
    (outs_all, grads_all), unused = lax.scan(one_expert, (start_outs, start_grads), (gate_up_weight, down_weight, jnp.arange(EXPERTS, dtype=jnp.int32)))
    outs_pairs = outs_all.reshape(SEQUENCE_TOKENS, TOP, D).astype(jnp.float32)
    layer_output = (hidden_f + lax.optimization_barrier(jnp.sum(route_weights[:, :, None] * outs_pairs, axis=1))).astype(jnp.bfloat16)
    route_grads = lax.optimization_barrier(jnp.sum(grad_f[:, None, :] * outs_pairs, axis=2))
    normed_grad = lax.optimization_barrier(jnp.sum(grads_all.reshape(SEQUENCE_TOKENS, TOP, D).astype(jnp.float32), axis=1))
    unit_rows = hidden_f * inv_rms[:, None]
    unit_grad = normed_grad * moe_gain[None, :]
    residual_grad = (grad_f + inv_rms[:, None] * (unit_grad - unit_rows * lax.optimization_barrier(jnp.mean(unit_grad * unit_rows, axis=1, keepdims=True)))).astype(jnp.bfloat16)
    return (layer_output, residual_grad, route_grads)
```

```python
import jax
import jax.numpy as jnp
from jax import lax
from jax.experimental import pallas as pl
from jax.experimental.pallas import tpu as pltpu
from jax.sharding import Mesh
from jax.sharding import PartitionSpec as P

F32 = jnp.float32
BF16 = jnp.bfloat16
HIGH = lax.Precision.HIGHEST
SPAN = 128
CAP = 9
LANES = 128


def mm(a, b, dims, precision=None):
    return lax.dot_general(a, b, (dims, ((), ())), precision=precision, preferred_element_type=F32)


NN = ((1,), (0,))
NT = ((1,), (1,))
TN = ((0,), (0,))


def silu(v):
    return v * (1.0 / (1.0 + jnp.exp(-v)))


def call(kernel, outs, scratch=()):
    return pl.pallas_call(
        kernel,
        out_shape=outs,
        scratch_shapes=list(scratch),
        compiler_params=pltpu.CompilerParams(vmem_limit_bytes=58 << 20),
    )


def spread(values, first, heads, head_width):
    rows = values.shape[0]
    per = LANES // head_width
    lane = lax.broadcasted_iota(jnp.int32, (rows, LANES), 1)
    parts = []
    for group in range(heads // per):
        out = jnp.broadcast_to(values[:, first + group * per : first + group * per + 1], (rows, LANES))
        for i in range(1, per):
            col = first + group * per + i
            out = jnp.where(
                lane < i * head_width, out, jnp.broadcast_to(values[:, col : col + 1], (rows, LANES))
            )
        parts.append(out)
    return jnp.concatenate(parts, axis=1)


def mixer_local(x_inner, bc_input, rim, weight, sl, slt, skip_row, heads, ctx_count):
    rows, channels = x_inner.shape
    state_size = bc_input.shape[1] // 2
    width = channels + 2 * state_size
    head_width = channels // heads
    blocks = rows // SPAN
    chunk = state_size // ctx_count
    kernel_len = weight.shape[0]

    def kernel(x_ref, bc_ref, rim_ref, w_ref, sl_ref, slt_ref, skip_ref, y_ref, c_ref, e_ref, send_ref, pad_ref, held_ref, tot_ref):
        row_i = lax.broadcasted_iota(jnp.int32, (SPAN, SPAN), 0)
        col_i = lax.broadcasted_iota(jnp.int32, (SPAN, SPAN), 1)
        causal = row_i >= col_i
        lower = jnp.where(causal, 1.0, 0.0).astype(F32)
        upper = jnp.where(row_i <= col_i, 1.0, 0.0).astype(F32)
        lane = lax.broadcasted_iota(jnp.int32, (SPAN, LANES), 1)
        pad_ref[0:8, :] = rim_ref[...].astype(F32)
        held_ref[...] = jnp.zeros_like(held_ref)
        tot_ref[...] = jnp.zeros_like(tot_ref)

        def block(j, carry):
            at = pl.multiple_of(j * SPAN, SPAN)
            pad_ref[8:, :channels] = x_ref[pl.ds(at, SPAN), :].astype(F32)
            pad_ref[8:, channels:] = bc_ref[pl.ds(at, SPAN), :].astype(F32)
            summed = jnp.zeros((SPAN, width), F32)
            for k in range(kernel_len):
                begin = 8 - kernel_len + 1 + k
                summed = summed + w_ref[k : k + 1, :] * pad_ref[begin : begin + SPAN, :]
            tail_rows = pad_ref[SPAN : SPAN + 8, :]
            pad_ref[0:8, :] = tail_rows
            conv = silu(summed).astype(BF16)
            x_b = conv[:, :channels]
            b_b = conv[:, channels : channels + state_size]
            c_b = conv[:, channels + state_size :]
            x_f = x_b.astype(F32)
            sl_b = sl_ref[pl.ds(at, SPAN), :]
            cum = mm(lower, sl_b, NN, HIGH)
            slt_b = slt_ref[:, pl.ds(at, SPAN)]
            cum_t = mm(slt_b, upper, NN, HIGH)
            scores = mm(c_b, b_b, NT)
            within = []
            per = LANES // head_width
            for group in range(channels // LANES):
                x_g = x_b[:, group * LANES : (group + 1) * LANES]
                out = None
                for i in range(per):
                    h = group * per + i
                    gap = cum[:, heads + h : heads + h + 1] - cum_t[heads + h : heads + h + 1, :]
                    w = jnp.exp(jnp.where(causal, gap, -1e30)) * scores * slt_b[h : h + 1, :]
                    y_h = mm(w.astype(BF16), x_g, NN)
                    out = y_h if out is None else jnp.where(lane < i * head_width, out, y_h)
                within.append(out)
            within = jnp.concatenate(within, axis=1)
            held = held_ref[...]
            carried = mm(c_b, held.astype(BF16), NN) * spread(jnp.exp(cum), heads, heads, head_width)
            y_ref[pl.ds(at, SPAN), :] = within + carried + skip_ref[...] * x_f
            c_ref[pl.ds(at, SPAN), :] = c_b
            tot = tot_ref[0:1, :]
            e_ref[pl.ds(at, SPAN), :] = jnp.exp(jnp.minimum(tot + cum, 0.0))
            last = cum[SPAN - 1 : SPAN, :]
            tail = spread(jnp.exp(jnp.minimum(last - cum, 0.0)), heads, heads, head_width)
            step = spread(sl_b, 0, heads, head_width)
            x_t = (x_f * tail * step).astype(BF16)
            decay = spread(jnp.exp(jnp.minimum(last, 0.0)), heads, heads, head_width)
            held_ref[...] = decay * held + mm(b_b, x_t, TN)
            tot_ref[0:1, :] = tot + last
            return carry

        lax.fori_loop(0, blocks, block, 0)
        held = held_ref[...]
        total = spread(tot_ref[...], heads, heads, head_width)[0:1, :]
        hi = total.astype(BF16).astype(F32)
        mid = (total - hi).astype(BF16).astype(F32)
        low = total - hi - mid
        pick = lax.broadcasted_iota(jnp.int32, (8, channels), 0)
        extra = jnp.where(pick == 0, hi, jnp.where(pick == 1, mid, jnp.where(pick == 2, low, 0.0)))
        for d in range(ctx_count):
            part = jnp.concatenate([held[d * chunk : (d + 1) * chunk], extra], axis=0)
            send_ref[d] = part.astype(BF16)

    return call(
        kernel,
        (
            jax.ShapeDtypeStruct((rows, channels), F32),
            jax.ShapeDtypeStruct((rows, state_size), BF16),
            jax.ShapeDtypeStruct((rows, 2 * heads), F32),
            jax.ShapeDtypeStruct((ctx_count, chunk + 8, channels), BF16),
        ),
        (
            pltpu.VMEM((SPAN + 8, width), F32),
            pltpu.VMEM((state_size, channels), F32),
            pltpu.VMEM((8, 2 * heads), F32),
        ),
    )(x_inner, bc_input, rim, weight, sl, slt, skip_row)


def state_scan(received, chunk):
    count, _, channels = received.shape

    def kernel(r_ref, o_ref):
        arriving = jnp.zeros((chunk, channels), F32)
        for s in range(count):
            part = r_ref[s].astype(F32)
            o_ref[s] = arriving
            total = part[chunk : chunk + 1] + part[chunk + 1 : chunk + 2] + part[chunk + 2 : chunk + 3]
            arriving = jnp.exp(jnp.minimum(total, 0.0)) * arriving + part[:chunk]

    return call(kernel, jax.ShapeDtypeStruct((count, chunk, channels), F32))(received)


def gate_rows(y_local, c_rows, e_rows, arriving, gate_input, heads, x_count, y_count):
    rows, channels = y_local.shape
    head_width = channels // heads
    own = rows // (x_count * y_count)

    def kernel(y_ref, c_ref, e_ref, a_ref, g_ref, o_ref):
        state = a_ref[...].astype(BF16)
        for x in range(x_count):
            at = x * y_count * own
            size = y_count * own
            carried = mm(c_ref[at : at + size, :], state, NN) * spread(
                e_ref[at : at + size, :], heads, heads, head_width
            )
            gated = (y_ref[at : at + size, :] + carried) * silu(g_ref[at : at + size, :].astype(F32))
            for y in range(y_count):
                o_ref[y, x * own : (x + 1) * own, :] = gated[y * own : (y + 1) * own].astype(BF16)

    return call(kernel, jax.ShapeDtypeStruct((y_count, x_count * own, channels), BF16))(
        y_local, c_rows, e_rows, arriving, gate_input
    )


def project(gated, pieces, where, x_count):
    y_count, rows, channels = gated.shape
    out_width = pieces[0].shape[1]
    own = rows // x_count

    def kernel(where_ref, g_ref, *refs):
        o_ref = refs[-1]
        w_refs = refs[:-1]
        total = jnp.zeros((rows, out_width), F32)
        first = 0
        squares = jnp.zeros((rows, 1), F32)
        for y in range(y_count):
            part = g_ref[y].astype(F32)
            squares = squares + jnp.sum(part * part, axis=1, keepdims=True)
        for i, w_ref in enumerate(w_refs):
            size = w_ref.shape[0]
            lhs = g_ref[where_ref[i]]
            total = total + mm(lhs[:, first : first + size], w_ref[...], NN)
            first = (first + size) % channels
        hi = squares.astype(BF16).astype(F32)
        mid = (squares - hi).astype(BF16).astype(F32)
        low = squares - hi - mid
        lane = lax.broadcasted_iota(jnp.int32, (rows, LANES), 1)
        extra = jnp.where(lane == 0, hi, jnp.where(lane == 1, mid, jnp.where(lane == 2, low, 0.0)))
        for x in range(x_count):
            o_ref[x, :, :out_width] = total[x * own : (x + 1) * own].astype(BF16)
            o_ref[x, :, out_width:] = extra[x * own : (x + 1) * own].astype(BF16)

    vmem = pl.BlockSpec(memory_space=pltpu.VMEM)
    return pl.pallas_call(
        kernel,
        out_shape=jax.ShapeDtypeStruct((x_count, own, out_width + LANES), BF16),
        in_specs=[pl.BlockSpec(memory_space=pltpu.SMEM), vmem] + [vmem] * len(pieces),
        out_specs=vmem,
        compiler_params=pltpu.CompilerParams(vmem_limit_bytes=58 << 20),
    )(where, gated, *pieces)


def expert_of(row, owners, local_count):
    dest = (row * 7282) >> 16
    core = dest // owners
    return local_count * (dest - core * owners) + core, row - dest * CAP


def routing_rows(ids, expert_total, owners, local_count):
    tokens, top = ids.shape
    slots = expert_total * CAP
    member = jnp.zeros((tokens, expert_total), F32)
    for k in range(top):
        lane = lax.broadcasted_iota(jnp.int32, (tokens, expert_total), 1)
        member = member + jnp.where(lane == ids[:, k : k + 1], 1.0, 0.0)
    member = member.astype(BF16)
    earlier = lax.broadcasted_iota(jnp.int32, (tokens, tokens), 0) > lax.broadcasted_iota(
        jnp.int32, (tokens, tokens), 1
    )
    rank = mm(jnp.where(earlier, 1.0, 0.0).astype(BF16), member, NN)
    row = lax.broadcasted_iota(jnp.int32, (slots, expert_total), 0)
    expert, _ = expert_of(row, owners, local_count)
    spreading = jnp.where(
        expert == lax.broadcasted_iota(jnp.int32, (slots, expert_total), 1), 1.0, 0.0
    ).astype(BF16)
    hit = mm(spreading, member, NT)
    rank_of = mm(spreading, rank.astype(BF16), NT)
    _, slot = expert_of(lax.broadcasted_iota(jnp.int32, (slots, tokens), 0), owners, local_count)
    return jnp.where(rank_of == slot.astype(F32), hit, 0.0).astype(BF16)


def slot_masks(ids, expert_total, owners, local_count):
    tokens, top = ids.shape
    slots = expert_total * CAP
    lane = lax.broadcasted_iota(jnp.int32, (tokens, expert_total), 1)
    member = jnp.zeros((tokens, expert_total), F32)
    for k in range(top):
        member = member + jnp.where(lane == ids[:, k : k + 1], 1.0, 0.0)
    member = member.astype(BF16)
    earlier = lax.broadcasted_iota(jnp.int32, (tokens, tokens), 0) > lax.broadcasted_iota(
        jnp.int32, (tokens, tokens), 1
    )
    rank = mm(jnp.where(earlier, 1.0, 0.0).astype(BF16), member, NN)
    row = lax.broadcasted_iota(jnp.int32, (expert_total, slots), 1)
    expert, _ = expert_of(row, owners, local_count)
    spreading = jnp.where(
        expert == lax.broadcasted_iota(jnp.int32, (expert_total, slots), 0), 1.0, 0.0
    ).astype(BF16)
    rank_of = mm(rank.astype(BF16), spreading, NN)
    expert, slot = expert_of(lax.broadcasted_iota(jnp.int32, (tokens, slots), 1), owners, local_count)
    fits = rank_of == slot.astype(F32)
    return [fits & (expert == ids[:, k : k + 1]) for k in range(top)]


def to_tiles(scratch, rows, value, first=0):
    count = scratch.shape[0] // rows
    for i in range(value.shape[1] // LANES):
        scratch[pl.ds(first + i, rows, stride=count), :] = value[:, i * LANES : (i + 1) * LANES]


def dispatch_grads(ids, out_grad, expert_total, owners, local_count):
    tokens, width = out_grad.shape
    slots = expert_total * CAP
    count = width // LANES

    def kernel(i_ref, g_ref, o_ref, s_ref):
        pick = routing_rows(i_ref[...], expert_total, owners, local_count)
        to_tiles(s_ref, slots, mm(pick, g_ref[...], NN))
        o_ref[...] = s_ref[...].astype(BF16)

    return call(
        kernel,
        jax.ShapeDtypeStruct((slots * count, LANES), BF16),
        (pltpu.VMEM((slots * count, LANES), F32),),
    )(ids, out_grad)


def normalise(parts, residual, moe_gain, ids, inner_total, expert_total, owners, local_count):
    x_count, tokens, _ = parts.shape
    width = residual.shape[1]
    slots = expert_total * CAP
    count = width // LANES

    def kernel(p_ref, r_ref, m_ref, i_ref, o_ref, h_ref, v_ref, s_ref):
        summed = p_ref[0].astype(F32)
        for x in range(1, x_count):
            summed = summed + p_ref[x].astype(F32)
        squares = summed[:, width : width + 1] + summed[:, width + 1 : width + 2] + summed[:, width + 2 : width + 3]
        hidden = r_ref[...].astype(F32) + summed[:, :width] * lax.rsqrt(squares / inner_total + 1e-05)
        hidden = hidden.astype(BF16)
        h_ref[...] = hidden
        hidden = hidden.astype(F32)
        inv = lax.rsqrt(jnp.mean(hidden * hidden, axis=1, keepdims=True) + 1e-06)
        v_ref[...] = jnp.broadcast_to(inv, (tokens, LANES))
        normed = (hidden * inv * m_ref[...]).astype(BF16)
        pick = routing_rows(i_ref[...], expert_total, owners, local_count)
        to_tiles(s_ref, slots, mm(pick, normed, NN))
        o_ref[...] = s_ref[...].astype(BF16)

    return call(
        kernel,
        (
            jax.ShapeDtypeStruct((slots * count, LANES), BF16),
            jax.ShapeDtypeStruct((tokens, width), BF16),
            jax.ShapeDtypeStruct((tokens, LANES), F32),
        ),
        (pltpu.VMEM((slots * count, LANES), F32),),
    )(parts, residual, moe_gain, ids)


def gate_up_of(ref, lead, ff_tiles, rows):
    tiles = [ref[lead + (slice(i * rows, (i + 1) * rows), slice(None))] for i in range(ff_tiles)]
    return jnp.concatenate(tiles, axis=1)


def experts(rows_in, grads_in, weights, ff_width, gu_rows):
    count = weights.shape[0] * weights.shape[1]
    z_count, cores = weights.shape[:2]
    slots = rows_in.shape[0] // count
    ff_tiles = 2 * ff_width // LANES
    block = gu_rows // ff_tiles

    def kernel(x_ref, g_ref, w_ref, o_ref, b_ref, x_s, g_s):
        x_s[...] = x_ref[...].astype(F32)
        g_s[...] = g_ref[...].astype(F32)
        projected = jnp.zeros((slots, 2 * ff_width), F32)
        hidden_grad = jnp.zeros((slots, ff_width), F32)

        def columns(ref, z):
            return jnp.concatenate(
                [ref[pl.ds(z * cores + c, slots, stride=count), :].astype(BF16) for c in range(cores)],
                axis=1,
            )

        def gate_up(z):
            return jnp.concatenate([gate_up_of(w_ref, (z, c), ff_tiles, block) for c in range(cores)], axis=0)

        def down(z):
            return jnp.concatenate([w_ref[z, c, gu_rows:, :] for c in range(cores)], axis=1)

        for z in range(z_count):
            projected = projected + mm(columns(x_s, z), gate_up(z), NN)
            hidden_grad = hidden_grad + mm(columns(g_s, z), down(z), NT)
        pre_gate = projected[:, :ff_width]
        pre_up = projected[:, ff_width:]
        sig = 1.0 / (1.0 + jnp.exp(-pre_gate))
        act = pre_gate * sig
        activated = (act * pre_up).astype(BF16)
        grad_gate = hidden_grad * pre_up * sig * (1.0 + pre_gate * (1.0 - sig))
        grad_up = hidden_grad * act
        grad_both = jnp.concatenate([grad_gate, grad_up], axis=1).astype(BF16)
        for z in range(z_count):
            to_tiles(x_s, slots, mm(activated, down(z), NN), z * cores)
            to_tiles(g_s, slots, mm(grad_both, gate_up(z), NT), z * cores)
        o_ref[...] = x_s[...].astype(BF16)
        b_ref[...] = g_s[...].astype(BF16)

    shape = jax.ShapeDtypeStruct(rows_in.shape, BF16)
    return call(kernel, (shape, shape), (pltpu.VMEM(rows_in.shape, F32), pltpu.VMEM(rows_in.shape, F32)))(
        rows_in, grads_in, weights
    )


def combine(outs_back, grads_back, hidden, inv_rms, out_grad, moe_gain, ids, route_weights, expert_total, owners, local_count):
    tokens, width = hidden.shape
    top = ids.shape[1]
    count = width // LANES
    slots = expert_total * CAP

    def kernel(o_ref, b_ref, h_ref, v_ref, g_ref, m_ref, i_ref, w_ref, layer_ref, res_ref, route_ref, o_s, b_s):
        o_s[...] = o_ref[...].astype(F32)
        b_s[...] = b_ref[...].astype(F32)
        masks = slot_masks(i_ref[...], expert_total, owners, local_count)
        weight = jnp.zeros((tokens, slots), F32)
        for k in range(top):
            weight = weight + jnp.where(masks[k], w_ref[:, k : k + 1], 0.0)
        hi = weight.astype(BF16)
        both = jnp.concatenate([hi, (weight - hi.astype(F32)).astype(BF16)], axis=0)

        def rows_of(ref):
            return jnp.concatenate(
                [ref[pl.ds(i, slots, stride=count), :].astype(BF16) for i in range(count)], axis=1
            )

        hidden = h_ref[...].astype(F32)
        grad = g_ref[...]
        outs = rows_of(o_s)
        mixed = mm(both, outs, NN)
        layer_ref[...] = (hidden + (mixed[:tokens] + mixed[tokens:])).astype(BF16)
        dots = mm(grad, outs, NT)
        lane = lax.broadcasted_iota(jnp.int32, (tokens, top), 1)
        route = jnp.zeros((tokens, top), F32)
        for k in range(top):
            one = jnp.sum(jnp.where(masks[k], dots, 0.0), axis=1, keepdims=True)
            route = jnp.where(lane == k, one, route)
        route_ref[...] = route
        mixed = mm(both, rows_of(b_s), NN)
        inv = v_ref[:, 0:1]
        unit_grad = (mixed[:tokens] + mixed[tokens:]) * m_ref[...]
        unit_rows = hidden * inv
        mean = jnp.mean(unit_grad * unit_rows, axis=1, keepdims=True)
        res_ref[...] = (grad.astype(F32) + inv * (unit_grad - unit_rows * mean)).astype(BF16)

    shape = jax.ShapeDtypeStruct((tokens, width), BF16)
    return call(
        kernel,
        (shape, shape, jax.ShapeDtypeStruct((tokens, top), F32)),
        (pltpu.VMEM((slots * count, LANES), F32), pltpu.VMEM((slots * count, LANES), F32)),
    )(outs_back, grads_back, hidden, inv_rms, out_grad, moe_gain, ids, route_weights)


def ring_route(count, shift):
    return [(i, (i + shift) % count) for i in range(count)]


def local(
    x_inner,
    bc_input,
    gate_input,
    conv_weight,
    bc_conv_weight,
    step_size,
    log_decay,
    skip_gain,
    norm_gain,
    out_weight,
    residual,
    moe_gain,
    expert_ids,
    route_weights,
    gate_up_weight,
    down_weight,
    out_grad,
):
    ctx = ("z", "core")
    ctx_count = lax.axis_size("z") * lax.axis_size("core")
    x_count, y_count = lax.axis_size("x"), lax.axis_size("y")
    owners = x_count * y_count
    heads = step_size.shape[1]
    channels = x_inner.shape[1]
    head_width = channels // heads
    state_size = bc_input.shape[1] // 2
    local_count, d_local, ff_both = gate_up_weight.shape
    ff_width = down_weight.shape[1]
    expert_total = local_count * owners
    tokens, width = residual.shape
    exchange = ("core", "x", "y")

    last = jnp.concatenate([x_inner[-8:], bc_input[-8:]], axis=1)
    rim = lax.ppermute(last, ctx, [(i, i + 1) for i in range(ctx_count - 1)])

    tiles = ff_both // LANES
    packed = jnp.concatenate(
        [
            gate_up_weight.reshape(local_count, d_local, tiles, LANES).transpose(0, 2, 1, 3).reshape(local_count, tiles * d_local, LANES),
            down_weight,
        ],
        axis=1,
    )
    swapped = lax.all_to_all(packed, "core", split_axis=0, concat_axis=0, tiled=True)
    weights = lax.all_gather(swapped, "z", axis=0, tiled=False)

    folded = (out_weight.astype(F32) * norm_gain[:, None]).astype(BF16)
    half = folded.shape[0] // 2
    from_prev = lax.ppermute(folded, "y", ring_route(y_count, 1))
    from_next = lax.ppermute(folded, "y", ring_route(y_count, -1))
    far_a = lax.ppermute(from_prev[:half], "y", ring_route(y_count, 1))
    far_b = lax.ppermute(from_next[half:], "y", ring_route(y_count, -1))
    y_at = lax.axis_index("y")
    where = jnp.stack([y_at, (y_at + y_count - 1) % y_count, (y_at + 1) % y_count, (y_at + 2) % y_count, (y_at + 2) % y_count]).astype(jnp.int32)

    sent_grads = dispatch_grads(expert_ids, out_grad, expert_total, owners, local_count)
    grads_in = lax.all_to_all(
        sent_grads.reshape(expert_total, -1, LANES), exchange, split_axis=0, concat_axis=0, tiled=True
    )

    sl = jnp.concatenate([step_size, log_decay], axis=1)
    joint = jnp.concatenate([conv_weight, bc_conv_weight], axis=1)
    skip_row = jnp.repeat(skip_gain, head_width)[None, :]
    y_local, c_rows, e_rows, sent = mixer_local(
        x_inner, bc_input, rim, joint, sl, sl.T, skip_row, heads, ctx_count
    )
    received = lax.all_to_all(sent, ctx, split_axis=0, concat_axis=0, tiled=True)
    scanned = state_scan(received, state_size // ctx_count)
    arriving = lax.all_to_all(scanned, ctx, split_axis=0, concat_axis=0, tiled=True).reshape(state_size, channels)
    gated = gate_rows(y_local, c_rows, e_rows, arriving, gate_input, heads, x_count, y_count)
    gated = lax.all_to_all(gated, "y", split_axis=0, concat_axis=0, tiled=True)
    parts = project(gated, [folded, from_prev, from_next, far_a, far_b], where, x_count)
    parts = lax.all_to_all(parts, "x", split_axis=0, concat_axis=0, tiled=True)
    sent_rows, hidden, inv_rms = normalise(
        parts, residual, moe_gain[None, :], expert_ids, channels * owners, expert_total, owners, local_count
    )
    rows_in = lax.all_to_all(
        sent_rows.reshape(expert_total, -1, LANES), exchange, split_axis=0, concat_axis=0, tiled=True
    )
    outs, grads = experts(
        rows_in.reshape(-1, LANES), grads_in.reshape(-1, LANES), weights, ff_width, tiles * d_local
    )
    outs_back = lax.all_to_all(
        outs.reshape(expert_total, -1, LANES), exchange, split_axis=0, concat_axis=0, tiled=True
    )
    grads_back = lax.all_to_all(
        grads.reshape(expert_total, -1, LANES), exchange, split_axis=0, concat_axis=0, tiled=True
    )
    return combine(
        outs_back.reshape(-1, LANES),
        grads_back.reshape(-1, LANES),
        hidden,
        inv_rms,
        out_grad,
        moe_gain[None, :],
        expert_ids,
        route_weights,
        expert_total,
        owners,
        local_count,
    )


def solution(mesh):
    ctx_count, exp_count = mesh.devices.shape
    side = int(round(exp_count**0.5))
    devices = mesh.devices.reshape(ctx_count // 2, 2, side, exp_count // side)
    fine = Mesh(devices, ("z", "core", "x", "y"))
    ctx, exp = ("z", "core"), ("x", "y")
    token = P(ctx + exp, None)
    return jax.shard_map(
        local,
        mesh=fine,
        in_specs=(
            P(ctx, exp),
            P(ctx, None),
            P(ctx, exp),
            P(None, exp),
            P(),
            P(ctx, exp),
            P(ctx, exp),
            P(exp),
            P(exp),
            P(exp, None),
            token,
            P(),
            token,
            token,
            P(exp, ctx, None),
            P(exp, None, ctx),
            token,
        ),
        out_specs=(token, token, token),
        check_vma=False,
    )
```

```python
import jax
import jax.numpy as jnp
from jax import lax
from jax.experimental import pallas as pl
from jax.experimental.pallas import tpu as pltpu
from jax.sharding import Mesh
from jax.sharding import PartitionSpec as P

F32 = jnp.float32
BF16 = jnp.bfloat16
HIGH = lax.Precision.HIGHEST
SPAN = 128
CAP = 9
LANES = 128


def mm(a, b, dims, precision=None):
    return lax.dot_general(a, b, (dims, ((), ())), precision=precision, preferred_element_type=F32)


NN = ((1,), (0,))
NT = ((1,), (1,))
TN = ((0,), (0,))


def silu(v):
    return v * (1.0 / (1.0 + jnp.exp(-v)))


def call(kernel, outs, scratch=()):
    return pl.pallas_call(
        kernel,
        out_shape=outs,
        scratch_shapes=list(scratch),
        compiler_params=pltpu.CompilerParams(vmem_limit_bytes=58 << 20),
    )


def spread(values, first, heads, head_width):
    rows = values.shape[0]
    per = LANES // head_width
    lane = lax.broadcasted_iota(jnp.int32, (rows, LANES), 1)
    parts = []
    for group in range(heads // per):
        out = jnp.broadcast_to(values[:, first + group * per : first + group * per + 1], (rows, LANES))
        for i in range(1, per):
            col = first + group * per + i
            out = jnp.where(
                lane < i * head_width, out, jnp.broadcast_to(values[:, col : col + 1], (rows, LANES))
            )
        parts.append(out)
    return jnp.concatenate(parts, axis=1)


def columns_of(transposed, eye):
    return mm(eye, transposed, NT, HIGH)


def mixer_state(x_inner, bc_input, rim, conv_weight, bc_weight, step_t, decay_t, ctx_count):
    rows, channels = x_inner.shape
    heads = step_t.shape[0]
    state_size = bc_input.shape[1] // 2
    width = channels + 2 * state_size
    head_width = channels // heads
    blocks = rows // SPAN
    chunk = state_size // ctx_count
    kernel_len = conv_weight.shape[0]

    def kernel(x_ref, bc_ref, rim_ref, wx_ref, wb_ref, step_ref, ld_ref, conv_ref, in_ref, send_ref, pad_ref, held_ref, tot_ref):
        row_i = lax.broadcasted_iota(jnp.int32, (SPAN, SPAN), 0)
        col_i = lax.broadcasted_iota(jnp.int32, (SPAN, SPAN), 1)
        later = jnp.where(row_i < col_i, 1.0, 0.0).astype(F32)
        eye = jnp.where(row_i == col_i, 1.0, 0.0).astype(F32)
        ones = jnp.ones((SPAN, SPAN), F32)
        weight = jnp.concatenate([wx_ref[...], wb_ref[...]], axis=1)
        pad_ref[0:8, :] = rim_ref[...].astype(F32)
        held_ref[...] = jnp.zeros_like(held_ref)
        tot_ref[...] = jnp.zeros_like(tot_ref)

        def block(j, carry):
            at = pl.multiple_of(j * SPAN, SPAN)
            pad_ref[8:, :channels] = x_ref[pl.ds(at, SPAN), :].astype(F32)
            pad_ref[8:, channels:] = bc_ref[pl.ds(at, SPAN), :].astype(F32)
            summed = jnp.zeros((SPAN, width), F32)
            for k in range(kernel_len):
                begin = 8 - kernel_len + 1 + k
                summed = summed + weight[k : k + 1, :] * pad_ref[begin : begin + SPAN, :]
            tail_rows = pad_ref[SPAN : SPAN + 8, :]
            pad_ref[0:8, :] = tail_rows
            conv = silu(summed).astype(BF16)
            conv_ref[pl.ds(at, SPAN), :] = conv
            x_f = conv[:, :channels].astype(F32)
            b_b = conv[:, channels : channels + state_size]
            ld_b = ld_ref[:, pl.ds(at, SPAN)]
            left = mm(later, ld_b, NT, HIGH)
            step = columns_of(step_ref[:, pl.ds(at, SPAN)], eye)
            tail = spread(jnp.exp(jnp.minimum(left, 0.0)) * step, 0, heads, head_width)
            x_t = (x_f * tail).astype(BF16)
            last = mm(ones, ld_b, NT, HIGH)
            decay = spread(jnp.exp(jnp.minimum(last, 0.0)), 0, heads, head_width)
            held = held_ref[...]
            in_ref[pl.ds(at, SPAN), :] = held.astype(BF16)
            held_ref[...] = decay * held + mm(b_b, x_t, TN)
            tot_ref[...] = tot_ref[...] + last[0:8, :]
            return carry

        lax.fori_loop(0, blocks, block, 0)
        held = held_ref[...]
        total = spread(tot_ref[...], 0, heads, head_width)[0:1, :]
        hi = total.astype(BF16).astype(F32)
        mid = (total - hi).astype(BF16).astype(F32)
        low = total - hi - mid
        pick = lax.broadcasted_iota(jnp.int32, (8, channels), 0)
        extra = jnp.where(pick == 0, hi, jnp.where(pick == 1, mid, jnp.where(pick == 2, low, 0.0)))
        for d in range(ctx_count):
            part = jnp.concatenate([held[d * chunk : (d + 1) * chunk], extra], axis=0)
            send_ref[d] = part.astype(BF16)

    return call(
        kernel,
        (
            jax.ShapeDtypeStruct((rows, width), BF16),
            jax.ShapeDtypeStruct((blocks * state_size, channels), BF16),
            jax.ShapeDtypeStruct((ctx_count, chunk + 8, channels), BF16),
        ),
        (
            pltpu.VMEM((SPAN + 8, width), F32),
            pltpu.VMEM((state_size, channels), F32),
            pltpu.VMEM((8, heads), F32),
        ),
    )(x_inner, bc_input, rim, conv_weight, bc_weight, step_t, decay_t)


def mixer_rows(conv, entering, step_t, decay_t, skip_gain, channels):
    rows = conv.shape[0]
    heads = step_t.shape[0]
    state_size = (conv.shape[1] - channels) // 2
    head_width = channels // heads
    blocks = rows // SPAN

    def kernel(skip_ref, conv_ref, in_ref, step_ref, ld_ref, y_ref, e_ref, tot_ref):
        row_i = lax.broadcasted_iota(jnp.int32, (SPAN, SPAN), 0)
        col_i = lax.broadcasted_iota(jnp.int32, (SPAN, SPAN), 1)
        causal = row_i >= col_i
        lower = jnp.where(causal, 1.0, 0.0).astype(F32)
        upper = jnp.where(row_i <= col_i, 1.0, 0.0).astype(F32)
        lane = lax.broadcasted_iota(jnp.int32, (SPAN, LANES), 1)
        lane_row = lax.broadcasted_iota(jnp.int32, (1, LANES), 1)
        per = LANES // head_width
        skip = []
        for group in range(channels // LANES):
            out = jnp.full((1, LANES), skip_ref[group * per], F32)
            for i in range(1, per):
                out = jnp.where(lane_row < i * head_width, out, skip_ref[group * per + i])
            skip.append(out)
        skip = jnp.concatenate(skip, axis=1)
        tot_ref[...] = jnp.zeros_like(tot_ref)

        def block(j, carry):
            at = pl.multiple_of(j * SPAN, SPAN)
            x_b = conv_ref[pl.ds(at, SPAN), :channels]
            b_b = conv_ref[pl.ds(at, SPAN), channels : channels + state_size]
            c_b = conv_ref[pl.ds(at, SPAN), channels + state_size :]
            ld_b = ld_ref[:, pl.ds(at, SPAN)]
            step_b = step_ref[:, pl.ds(at, SPAN)]
            cum = mm(lower, ld_b, NT, HIGH)
            cum_t = mm(ld_b, upper, NN, HIGH)
            scores = mm(c_b, b_b, NT)
            within = []
            for group in range(channels // LANES):
                x_g = x_b[:, group * LANES : (group + 1) * LANES]
                out = None
                for i in range(per):
                    h = group * per + i
                    gap = cum[:, h : h + 1] - cum_t[h : h + 1, :]
                    w = jnp.exp(jnp.where(causal, gap, -1e30)) * scores * step_b[h : h + 1, :]
                    y_h = mm(w.astype(BF16), x_g, NN)
                    out = y_h if out is None else jnp.where(lane < i * head_width, out, y_h)
                within.append(out)
            within = jnp.concatenate(within, axis=1)
            carried = mm(c_b, in_ref[pl.ds(at, SPAN), :], NN) * spread(jnp.exp(cum), 0, heads, head_width)
            y_ref[pl.ds(at, SPAN), :] = within + carried + skip * x_b.astype(F32)
            tot = tot_ref[0:1, :]
            e_ref[pl.ds(at, SPAN), :] = jnp.exp(jnp.minimum(tot + cum, 0.0))
            tot_ref[...] = tot_ref[...] + cum[SPAN - 1 : SPAN, :]
            return carry

        lax.fori_loop(0, blocks, block, 0)

    vmem = pl.BlockSpec(memory_space=pltpu.VMEM)
    return pl.pallas_call(
        kernel,
        out_shape=(
            jax.ShapeDtypeStruct((rows, channels), F32),
            jax.ShapeDtypeStruct((rows, heads), F32),
        ),
        in_specs=[pl.BlockSpec(memory_space=pltpu.SMEM)] + [vmem] * 4,
        out_specs=(vmem, vmem),
        scratch_shapes=[pltpu.VMEM((8, heads), F32)],
        compiler_params=pltpu.CompilerParams(vmem_limit_bytes=58 << 20),
    )(skip_gain, conv, entering, step_t, decay_t)


def state_scan(received, chunk):
    count, _, channels = received.shape

    def kernel(r_ref, o_ref):
        arriving = jnp.zeros((chunk, channels), F32)
        for s in range(count):
            part = r_ref[s].astype(F32)
            o_ref[s] = arriving
            total = part[chunk : chunk + 1] + part[chunk + 1 : chunk + 2] + part[chunk + 2 : chunk + 3]
            arriving = jnp.exp(jnp.minimum(total, 0.0)) * arriving + part[:chunk]

    return call(kernel, jax.ShapeDtypeStruct((count, chunk, channels), F32))(received)


def gate_rows(y_local, conv, e_rows, arriving, gate_input, x_count, y_count):
    rows, channels = y_local.shape
    heads = e_rows.shape[1]
    state_size = arriving.shape[0]
    head_width = channels // heads
    own = rows // (x_count * y_count)

    def kernel(y_ref, c_ref, e_ref, a_ref, g_ref, o_ref):
        state = a_ref[...].astype(BF16)
        for x in range(x_count):
            at = x * y_count * own
            size = y_count * own
            carried = mm(c_ref[at : at + size, channels + state_size :], state, NN) * spread(
                e_ref[at : at + size, :], 0, heads, head_width
            )
            gated = (y_ref[at : at + size, :] + carried) * silu(g_ref[at : at + size, :].astype(F32))
            for y in range(y_count):
                o_ref[y, x * own : (x + 1) * own, :] = gated[y * own : (y + 1) * own].astype(BF16)

    return call(kernel, jax.ShapeDtypeStruct((y_count, x_count * own, channels), BF16))(
        y_local, conv, e_rows, arriving, gate_input
    )


def project(gated, pieces, where, x_count):
    y_count, rows, channels = gated.shape
    out_width = pieces[0].shape[1]
    own = rows // x_count

    def kernel(where_ref, g_ref, *refs):
        o_ref = refs[-1]
        w_refs = refs[:-1]
        total = jnp.zeros((rows, out_width), F32)
        first = 0
        squares = jnp.zeros((rows, 1), F32)
        for y in range(y_count):
            part = g_ref[y].astype(F32)
            squares = squares + jnp.sum(part * part, axis=1, keepdims=True)
        for i, w_ref in enumerate(w_refs):
            size = w_ref.shape[0]
            lhs = g_ref[where_ref[i]]
            total = total + mm(lhs[:, first : first + size], w_ref[...], NN)
            first = (first + size) % channels
        hi = squares.astype(BF16).astype(F32)
        mid = (squares - hi).astype(BF16).astype(F32)
        low = squares - hi - mid
        lane = lax.broadcasted_iota(jnp.int32, (rows, LANES), 1)
        extra = jnp.where(lane == 0, hi, jnp.where(lane == 1, mid, jnp.where(lane == 2, low, 0.0)))
        for x in range(x_count):
            o_ref[x, :, :out_width] = total[x * own : (x + 1) * own].astype(BF16)
            o_ref[x, :, out_width:] = extra[x * own : (x + 1) * own].astype(BF16)

    vmem = pl.BlockSpec(memory_space=pltpu.VMEM)
    return pl.pallas_call(
        kernel,
        out_shape=jax.ShapeDtypeStruct((x_count, own, out_width + LANES), BF16),
        in_specs=[pl.BlockSpec(memory_space=pltpu.SMEM), vmem] + [vmem] * len(pieces),
        out_specs=vmem,
        compiler_params=pltpu.CompilerParams(vmem_limit_bytes=58 << 20),
    )(where, gated, *pieces)


def expert_of(row, owners, local_count):
    dest = (row * 7282) >> 16
    core = dest // owners
    return local_count * (dest - core * owners) + core, row - dest * CAP


def id_columns(ids_t):
    tokens = ids_t.shape[1]
    eye = jnp.where(
        lax.broadcasted_iota(jnp.int32, (tokens, tokens), 0) == lax.broadcasted_iota(jnp.int32, (tokens, tokens), 1),
        1.0,
        0.0,
    )
    return columns_of(ids_t.astype(F32), eye), eye


def routing_rows(ids_t, expert_total, owners, local_count):
    top, tokens = ids_t.shape
    ids = (id_columns(ids_t)[0] + 0.5).astype(jnp.int32)
    slots = expert_total * CAP
    member = jnp.zeros((tokens, expert_total), F32)
    for k in range(top):
        lane = lax.broadcasted_iota(jnp.int32, (tokens, expert_total), 1)
        member = member + jnp.where(lane == ids[:, k : k + 1], 1.0, 0.0)
    member = member.astype(BF16)
    earlier = lax.broadcasted_iota(jnp.int32, (tokens, tokens), 0) > lax.broadcasted_iota(
        jnp.int32, (tokens, tokens), 1
    )
    rank = mm(jnp.where(earlier, 1.0, 0.0).astype(BF16), member, NN)
    row = lax.broadcasted_iota(jnp.int32, (slots, expert_total), 0)
    expert, _ = expert_of(row, owners, local_count)
    spreading = jnp.where(
        expert == lax.broadcasted_iota(jnp.int32, (slots, expert_total), 1), 1.0, 0.0
    ).astype(BF16)
    hit = mm(spreading, member, NT)
    rank_of = mm(spreading, rank.astype(BF16), NT)
    _, slot = expert_of(lax.broadcasted_iota(jnp.int32, (slots, tokens), 0), owners, local_count)
    return jnp.where(rank_of == slot.astype(F32), hit, 0.0).astype(BF16)


def slot_masks(ids_t, expert_total, owners, local_count):
    top, tokens = ids_t.shape
    ids = (id_columns(ids_t)[0] + 0.5).astype(jnp.int32)
    slots = expert_total * CAP
    lane = lax.broadcasted_iota(jnp.int32, (tokens, expert_total), 1)
    member = jnp.zeros((tokens, expert_total), F32)
    for k in range(top):
        member = member + jnp.where(lane == ids[:, k : k + 1], 1.0, 0.0)
    member = member.astype(BF16)
    earlier = lax.broadcasted_iota(jnp.int32, (tokens, tokens), 0) > lax.broadcasted_iota(
        jnp.int32, (tokens, tokens), 1
    )
    rank = mm(jnp.where(earlier, 1.0, 0.0).astype(BF16), member, NN)
    row = lax.broadcasted_iota(jnp.int32, (expert_total, slots), 1)
    expert, _ = expert_of(row, owners, local_count)
    spreading = jnp.where(
        expert == lax.broadcasted_iota(jnp.int32, (expert_total, slots), 0), 1.0, 0.0
    ).astype(BF16)
    rank_of = mm(rank.astype(BF16), spreading, NN)
    expert, slot = expert_of(lax.broadcasted_iota(jnp.int32, (tokens, slots), 1), owners, local_count)
    fits = rank_of == slot.astype(F32)
    return [fits & (expert == ids[:, k : k + 1]) for k in range(top)]


def to_tiles(scratch, rows, value, first=0):
    count = scratch.shape[0] // rows
    for i in range(value.shape[1] // LANES):
        scratch[pl.ds(first + i, rows, stride=count), :] = value[:, i * LANES : (i + 1) * LANES]


def dispatch_grads(ids, out_grad, expert_total, owners, local_count):
    tokens, width = out_grad.shape
    slots = expert_total * CAP
    count = width // LANES

    def kernel(i_ref, g_ref, o_ref, s_ref):
        pick = routing_rows(i_ref[...], expert_total, owners, local_count)
        to_tiles(s_ref, slots, mm(pick, g_ref[...], NN))
        o_ref[...] = s_ref[...].astype(BF16)

    return call(
        kernel,
        jax.ShapeDtypeStruct((slots * count, LANES), BF16),
        (pltpu.VMEM((slots * count, LANES), F32),),
    )(ids, out_grad)


def normalise(parts, residual, moe_gain, ids, inner_total, expert_total, owners, local_count):
    x_count, tokens, _ = parts.shape
    width = residual.shape[1]
    slots = expert_total * CAP
    count = width // LANES

    def kernel(p_ref, r_ref, m_ref, i_ref, o_ref, h_ref, v_ref, s_ref):
        summed = p_ref[0].astype(F32)
        for x in range(1, x_count):
            summed = summed + p_ref[x].astype(F32)
        squares = summed[:, width : width + 1] + summed[:, width + 1 : width + 2] + summed[:, width + 2 : width + 3]
        hidden = r_ref[...].astype(F32) + summed[:, :width] * lax.rsqrt(squares / inner_total + 1e-05)
        hidden = hidden.astype(BF16)
        h_ref[...] = hidden
        hidden = hidden.astype(F32)
        inv = lax.rsqrt(jnp.mean(hidden * hidden, axis=1, keepdims=True) + 1e-06)
        v_ref[...] = jnp.broadcast_to(inv, (tokens, LANES))
        normed = (hidden * inv * m_ref[...]).astype(BF16)
        pick = routing_rows(i_ref[...], expert_total, owners, local_count)
        to_tiles(s_ref, slots, mm(pick, normed, NN))
        o_ref[...] = s_ref[...].astype(BF16)

    return call(
        kernel,
        (
            jax.ShapeDtypeStruct((slots * count, LANES), BF16),
            jax.ShapeDtypeStruct((tokens, width), BF16),
            jax.ShapeDtypeStruct((tokens, LANES), F32),
        ),
        (pltpu.VMEM((slots * count, LANES), F32),),
    )(parts, residual, moe_gain, ids)


def pack_weights(core, gate_up, down):
    local_count, d_local, ff_both = gate_up.shape
    ff_width = down.shape[1]
    tiles = ff_both // LANES
    height = tiles * d_local + ff_width

    def kernel(core_ref, g_ref, d_ref, keep_ref, send_ref):
        for out_ref, e in ((keep_ref, core_ref[0]), (send_ref, 1 - core_ref[0])):
            for i in range(tiles):
                out_ref[i * d_local : (i + 1) * d_local, :] = g_ref[e, :, i * LANES : (i + 1) * LANES]
            out_ref[tiles * d_local :, :] = d_ref[e]

    vmem = pl.BlockSpec(memory_space=pltpu.VMEM)
    shape = jax.ShapeDtypeStruct((height, LANES), BF16)
    return pl.pallas_call(
        kernel,
        out_shape=(shape, shape),
        in_specs=[pl.BlockSpec(memory_space=pltpu.SMEM), vmem, vmem],
        out_specs=(vmem, vmem),
        compiler_params=pltpu.CompilerParams(vmem_limit_bytes=58 << 20),
    )(core, gate_up, down)


def experts(core, rows_in, grads_in, weights, ff_width, gu_rows):
    z_count, cores, height, _ = weights.shape
    count = z_count * cores
    slots = rows_in.shape[0] // count
    dests = slots // CAP
    ff_tiles = 2 * ff_width // LANES
    block = gu_rows // ff_tiles
    each = CAP * count

    def kernel(core_ref, x_ref, g_ref, w_hbm, o_ref, x_s, g_s, xb_s, gb_s, w_ref, sems):
        copies = [pltpu.make_async_copy(w_hbm.at[z], w_ref.at[z], sems.at[z]) for z in range(z_count)]
        for copy in copies:
            copy.start()
        core = core_ref[0]
        x_s[...] = x_ref[...].astype(F32)
        g_s[...] = g_ref[...].astype(F32)
        order = [(z, s, z * cores + (core if s == 0 else 1 - core)) for z in range(z_count) for s in range(cores)]
        for i, (z, s, c) in enumerate(order):
            xb_s[:, i * LANES : (i + 1) * LANES] = x_s[pl.ds(c, slots, stride=count), :].astype(BF16)
            gb_s[:, i * LANES : (i + 1) * LANES] = g_s[pl.ds(c, slots, stride=count), :].astype(BF16)

        def tile(z, s, i):
            return w_ref[z, s, i * block : (i + 1) * block, :]

        for copy in copies:
            copy.wait()
        projected = []
        for first in range(0, ff_tiles, 2):
            used = range(first, min(first + 2, ff_tiles))
            rhs = jnp.concatenate(
                [jnp.concatenate([tile(z, s, i) for i in used], axis=1) for z, s, _ in order], axis=0
            )
            projected.append(mm(xb_s[...], rhs, NN))
        projected = jnp.concatenate(projected, axis=1)
        hidden_grad = []
        for first in range(0, ff_width, 256):
            size = min(256, ff_width - first)
            rhs = jnp.concatenate(
                [w_ref[z, s, gu_rows + first : gu_rows + first + size, :] for z, s, _ in order], axis=1
            )
            hidden_grad.append(mm(gb_s[...], rhs, NT))
        hidden_grad = jnp.concatenate(hidden_grad, axis=1)
        pre_gate = projected[:, :ff_width]
        pre_up = projected[:, ff_width:]
        sig = 1.0 / (1.0 + jnp.exp(-pre_gate))
        act = pre_gate * sig
        activated = (act * pre_up).astype(BF16)
        grad_gate = hidden_grad * pre_up * sig * (1.0 + pre_gate * (1.0 - sig))
        grad_up = hidden_grad * act
        grad_both = jnp.concatenate([grad_gate, grad_up], axis=1).astype(BF16)
        for z in range(z_count):
            rhs = jnp.concatenate([w_ref[z, s, gu_rows:, :] for s in range(cores)], axis=1)
            out = mm(activated, rhs, NN)
            rhs = jnp.concatenate(
                [jnp.concatenate([tile(z, s, i) for i in range(ff_tiles)], axis=1) for s in range(cores)], axis=0
            )
            grad = mm(grad_both, rhs, NT)
            for s in range(cores):
                c = z * cores + (core if s == 0 else 1 - core)
                x_s[pl.ds(c, slots, stride=count), :] = out[:, s * LANES : (s + 1) * LANES]
                g_s[pl.ds(c, slots, stride=count), :] = grad[:, s * LANES : (s + 1) * LANES]
        for d in range(dests):
            o_ref[d, :each, :] = x_s[d * each : (d + 1) * each, :].astype(BF16)
            o_ref[d, each:, :] = g_s[d * each : (d + 1) * each, :].astype(BF16)

    vmem = pl.BlockSpec(memory_space=pltpu.VMEM)
    return pl.pallas_call(
        kernel,
        out_shape=jax.ShapeDtypeStruct((dests, 2 * each, LANES), BF16),
        in_specs=[pl.BlockSpec(memory_space=pltpu.SMEM), vmem, vmem, pl.BlockSpec(memory_space=pl.ANY)],
        out_specs=vmem,
        scratch_shapes=[
            pltpu.VMEM(rows_in.shape, F32),
            pltpu.VMEM(rows_in.shape, F32),
            pltpu.VMEM((slots, count * LANES), BF16),
            pltpu.VMEM((slots, count * LANES), BF16),
            pltpu.VMEM(weights.shape, BF16),
            pltpu.SemaphoreType.DMA((z_count,)),
        ],
        compiler_params=pltpu.CompilerParams(vmem_limit_bytes=58 << 20),
    )(core, rows_in, grads_in, weights)


def combine(back, hidden, inv_rms, out_grad, moe_gain, ids_t, route_t, expert_total, owners, local_count):
    tokens, width = hidden.shape
    top = ids_t.shape[0]
    count = width // LANES
    slots = expert_total * CAP
    each = CAP * count

    def kernel(r_ref, h_ref, v_ref, g_ref, m_ref, i_ref, w_ref, layer_ref, res_ref, route_ref, o_s, b_s):
        for d in range(expert_total):
            o_s[d * each : (d + 1) * each, :] = r_ref[d, :each, :].astype(F32)
            b_s[d * each : (d + 1) * each, :] = r_ref[d, each:, :].astype(F32)
        masks = slot_masks(i_ref[...], expert_total, owners, local_count)
        eye = id_columns(i_ref[...])[1]
        routes = columns_of(w_ref[...], eye)
        weight = jnp.zeros((tokens, slots), F32)
        for k in range(top):
            weight = weight + jnp.where(masks[k], routes[:, k : k + 1], 0.0)
        hi = weight.astype(BF16)
        both = jnp.concatenate([hi, (weight - hi.astype(F32)).astype(BF16)], axis=0)

        def rows_of(ref):
            return jnp.concatenate(
                [ref[pl.ds(i, slots, stride=count), :].astype(BF16) for i in range(count)], axis=1
            )

        hidden = h_ref[...].astype(F32)
        grad = g_ref[...]
        outs = rows_of(o_s)
        mixed = mm(both, outs, NN)
        layer_ref[...] = (hidden + (mixed[:tokens] + mixed[tokens:])).astype(BF16)
        dots = mm(grad, outs, NT)
        lane = lax.broadcasted_iota(jnp.int32, (tokens, top), 1)
        route = jnp.zeros((tokens, top), F32)
        for k in range(top):
            one = jnp.sum(jnp.where(masks[k], dots, 0.0), axis=1, keepdims=True)
            route = jnp.where(lane == k, one, route)
        route_ref[...] = mm(route, eye, TN, HIGH)
        mixed = mm(both, rows_of(b_s), NN)
        inv = v_ref[:, 0:1]
        unit_grad = (mixed[:tokens] + mixed[tokens:]) * m_ref[...]
        unit_rows = hidden * inv
        mean = jnp.mean(unit_grad * unit_rows, axis=1, keepdims=True)
        res_ref[...] = (grad.astype(F32) + inv * (unit_grad - unit_rows * mean)).astype(BF16)

    shape = jax.ShapeDtypeStruct((tokens, width), BF16)
    return call(
        kernel,
        (shape, shape, jax.ShapeDtypeStruct((top, tokens), F32)),
        (pltpu.VMEM((slots * count, LANES), F32), pltpu.VMEM((slots * count, LANES), F32)),
    )(back, hidden, inv_rms, out_grad, moe_gain, ids_t, route_t)


def ring_route(count, shift):
    return [(i, (i + shift) % count) for i in range(count)]


def local(
    x_inner,
    bc_input,
    gate_input,
    conv_weight,
    bc_conv_weight,
    step_size,
    log_decay,
    skip_gain,
    norm_gain,
    out_weight,
    residual,
    moe_gain,
    expert_ids,
    route_weights,
    gate_up_weight,
    down_weight,
    out_grad,
):
    ctx = ("z", "core")
    ctx_count = lax.axis_size("z") * lax.axis_size("core")
    x_count, y_count = lax.axis_size("x"), lax.axis_size("y")
    owners = x_count * y_count
    heads = step_size.shape[1]
    channels = x_inner.shape[1]
    head_width = channels // heads
    state_size = bc_input.shape[1] // 2
    local_count, d_local, ff_both = gate_up_weight.shape
    ff_width = down_weight.shape[1]
    expert_total = local_count * owners
    tokens, width = residual.shape
    exchange = ("core", "x", "y")

    ids_t, route_t = expert_ids.T, route_weights.T
    step_t, decay_t = step_size.T, log_decay.T
    core = lax.axis_index("core").astype(jnp.int32).reshape(1)

    last = jnp.concatenate([x_inner[-8:], bc_input[-8:]], axis=1)
    rim = lax.ppermute(last, ctx, [(i, i + 1) for i in range(ctx_count - 1)])

    kept, other = pack_weights(core, gate_up_weight, down_weight)
    swapped = lax.ppermute(other, "core", [(0, 1), (1, 0)])
    weights = lax.all_gather(jnp.stack([kept, swapped]), "z", axis=0, tiled=False)
    gu_rows = kept.shape[0] - ff_width

    sent_grads = dispatch_grads(ids_t, out_grad, expert_total, owners, local_count)
    rim, sent_grads = lax.optimization_barrier((rim, sent_grads))

    conv, held_in, sent = mixer_state(
        x_inner, bc_input, rim, conv_weight, bc_conv_weight, step_t, decay_t, ctx_count
    )
    received = lax.all_to_all(sent, ctx, split_axis=0, concat_axis=0, tiled=True)
    grads_in = lax.all_to_all(
        sent_grads.reshape(expert_total, -1, LANES), exchange, split_axis=0, concat_axis=0, tiled=True
    )

    folded = (out_weight.astype(F32) * norm_gain[:, None]).astype(BF16)
    folded, rim = lax.optimization_barrier((folded, rim))
    half = folded.shape[0] // 2
    from_prev = lax.ppermute(folded, "y", ring_route(y_count, 1))
    from_next = lax.ppermute(folded, "y", ring_route(y_count, -1))
    y_local, e_rows = mixer_rows(conv, held_in, step_t, decay_t, skip_gain, channels)
    received, from_prev, from_next, y_local = lax.optimization_barrier((received, from_prev, from_next, y_local))
    far_a = lax.ppermute(from_prev[:half], "y", ring_route(y_count, 1))
    far_b = lax.ppermute(from_next[half:], "y", ring_route(y_count, -1))
    y_at = lax.axis_index("y")
    where = jnp.stack([y_at, (y_at + y_count - 1) % y_count, (y_at + 1) % y_count, (y_at + 2) % y_count, (y_at + 2) % y_count]).astype(jnp.int32)

    scanned = state_scan(received, state_size // ctx_count)
    arriving = lax.all_to_all(scanned, ctx, split_axis=0, concat_axis=0, tiled=True).reshape(state_size, channels)
    arriving, grads_in = lax.optimization_barrier((arriving, grads_in))
    gated = gate_rows(y_local, conv, e_rows, arriving, gate_input, x_count, y_count)
    gated = lax.all_to_all(gated, "y", split_axis=0, concat_axis=0, tiled=True)
    parts = project(gated, [folded, from_prev, from_next, far_a, far_b], where, x_count)
    parts = lax.all_to_all(parts, "x", split_axis=0, concat_axis=0, tiled=True)
    sent_rows, hidden, inv_rms = normalise(
        parts, residual, moe_gain[None, :], ids_t, channels * owners, expert_total, owners, local_count
    )
    rows_in = lax.all_to_all(
        sent_rows.reshape(expert_total, -1, LANES), exchange, split_axis=0, concat_axis=0, tiled=True
    )
    back = experts(core, rows_in.reshape(-1, LANES), grads_in.reshape(-1, LANES), weights, ff_width, gu_rows)
    back = lax.all_to_all(back, exchange, split_axis=0, concat_axis=0, tiled=True)
    layer, res, route = combine(
        back, hidden, inv_rms, out_grad, moe_gain[None, :], ids_t, route_t, expert_total, owners, local_count
    )
    return layer, res, route.T


def solution(mesh):
    ctx_count, exp_count = mesh.devices.shape
    side = int(round(exp_count**0.5))
    devices = mesh.devices.reshape(ctx_count // 2, 2, side, exp_count // side)
    fine = Mesh(devices, ("z", "core", "x", "y"))
    ctx, exp = ("z", "core"), ("x", "y")
    token = P(ctx + exp, None)
    return jax.shard_map(
        local,
        mesh=fine,
        in_specs=(
            P(ctx, exp),
            P(ctx, None),
            P(ctx, exp),
            P(None, exp),
            P(),
            P(ctx, exp),
            P(ctx, exp),
            P(exp),
            P(exp),
            P(exp, None),
            token,
            P(),
            token,
            token,
            P(exp, ctx, None),
            P(exp, None, ctx),
            token,
        ),
        out_specs=(token, token, token),
        check_vma=False,
    )
```

```python
import jax
import jax.numpy as jnp
from jax import lax
from jax.experimental import pallas as pl
from jax.experimental.pallas import tpu as pltpu
from jax.sharding import Mesh
from jax.sharding import PartitionSpec as P


F32 = jnp.float32
BF16 = jnp.bfloat16
HIGH = lax.Precision.HIGHEST
SPAN = 128
CAP = 9
LANES = 128


def mm(a, b, dims, precision=None):
    return lax.dot_general(a, b, (dims, ((), ())), precision=precision, preferred_element_type=F32)


NN = ((1,), (0,))
NT = ((1,), (1,))
TN = ((0,), (0,))


def silu(v):
    return v * (1.0 / (1.0 + jnp.exp(-v)))


def call(kernel, outs, scratch=()):
    return pl.pallas_call(
        kernel,
        out_shape=outs,
        scratch_shapes=list(scratch),
        compiler_params=pltpu.CompilerParams(vmem_limit_bytes=58 << 20),
    )


def spread(values, first, heads, head_width):
    rows = values.shape[0]
    per = LANES // head_width
    lane = lax.broadcasted_iota(jnp.int32, (rows, LANES), 1)
    parts = []
    for group in range(heads // per):
        out = jnp.broadcast_to(values[:, first + group * per : first + group * per + 1], (rows, LANES))
        for i in range(1, per):
            col = first + group * per + i
            out = jnp.where(
                lane < i * head_width, out, jnp.broadcast_to(values[:, col : col + 1], (rows, LANES))
            )
        parts.append(out)
    return jnp.concatenate(parts, axis=1)


def columns_of(transposed, eye):
    return mm(eye, transposed, NT, HIGH)


def stack_blocks(values, blocks):
    return jnp.concatenate([values[:, j * SPAN : (j + 1) * SPAN] for j in range(blocks)], axis=0)


def three_rows(total, rows):
    hi = total.astype(BF16).astype(F32)
    mid = (total - hi).astype(BF16).astype(F32)
    low = total - hi - mid
    pick = lax.broadcasted_iota(jnp.int32, (rows, total.shape[1]), 0)
    return jnp.where(pick == 0, hi, jnp.where(pick == 1, mid, jnp.where(pick == 2, low, 0.0)))


def mixer_state(x_inner, bc_input, rim, conv_weight, bc_weight, step_t, decay_t):
    rows, channels = x_inner.shape
    heads = step_t.shape[0]
    state_size = bc_input.shape[1] // 2
    width = channels + 2 * state_size
    head_width = channels // heads
    blocks = rows // SPAN
    kernel_len = conv_weight.shape[0]

    def kernel(x_ref, bc_ref, rim_ref, wx_ref, wb_ref, step_ref, ld_ref, conv_ref, in_ref, send_ref, pad_ref):
        row_i = lax.broadcasted_iota(jnp.int32, (SPAN, SPAN), 0)
        col_i = lax.broadcasted_iota(jnp.int32, (SPAN, SPAN), 1)
        later = jnp.where(row_i < col_i, 1.0, 0.0).astype(F32)
        eye = jnp.where(row_i == col_i, 1.0, 0.0).astype(F32)
        ones = jnp.ones((8, SPAN), F32)
        ld = stack_blocks(ld_ref[...], blocks)
        left = jnp.exp(jnp.minimum(mm(later, ld, NT, HIGH), 0.0))
        tails = left * columns_of(stack_blocks(step_ref[...], blocks), eye)
        lasts = mm(ones, ld, NT, HIGH)
        decays = jnp.exp(jnp.minimum(lasts, 0.0))
        weight = jnp.concatenate([wx_ref[...], wb_ref[...]], axis=1)
        held = None
        total = None
        pad_ref[0:8, :] = rim_ref[...].astype(F32)
        for j in range(blocks):
            at = j * SPAN
            pad_ref[8 + at : 8 + at + SPAN, :channels] = x_ref[at : at + SPAN, :].astype(F32)
            pad_ref[8 + at : 8 + at + SPAN, channels:] = bc_ref[at : at + SPAN, :].astype(F32)
            summed = None
            for k in range(kernel_len):
                begin = at + 8 - kernel_len + 1 + k
                term = weight[k : k + 1, :] * pad_ref[begin : begin + SPAN, :]
                summed = term if summed is None else summed + term
            conv = silu(summed).astype(BF16)
            conv_ref[at : at + SPAN, :] = conv
            x_t = (conv[:, :channels].astype(F32) * spread(tails, j * heads, heads, head_width)).astype(BF16)
            state = mm(conv[:, channels : channels + state_size], x_t, TN)
            if j == 0:
                in_ref[at : at + SPAN, :] = jnp.zeros((state_size, channels), BF16)
                held = state
                total = lasts[:, :heads]
            else:
                in_ref[at : at + SPAN, :] = held.astype(BF16)
                held = spread(decays, j * heads, heads, head_width)[0:1, :] * held + state
                total = total + lasts[:, j * heads : (j + 1) * heads]
        send_ref[:state_size, :] = held.astype(BF16)
        extra = three_rows(spread(total, 0, heads, head_width)[0:1, :], 16)
        send_ref[state_size:, :] = extra.astype(BF16)

    return call(
        kernel,
        (
            jax.ShapeDtypeStruct((rows, width), BF16),
            jax.ShapeDtypeStruct((blocks * state_size, channels), BF16),
            jax.ShapeDtypeStruct((state_size + 16, channels), BF16),
        ),
        (pltpu.VMEM((rows + 8, width), F32),),
    )(x_inner, bc_input, rim, conv_weight, bc_weight, step_t, decay_t)


def mixer_rows(conv, entering, step_t, decay_t, skip_gain, channels):
    rows = conv.shape[0]
    heads = step_t.shape[0]
    state_size = (conv.shape[1] - channels) // 2
    head_width = channels // heads
    blocks = rows // SPAN

    def kernel(skip_ref, conv_ref, in_ref, step_ref, ld_ref, y_ref, e_ref):
        row_i = lax.broadcasted_iota(jnp.int32, (SPAN, SPAN), 0)
        col_i = lax.broadcasted_iota(jnp.int32, (SPAN, SPAN), 1)
        causal = row_i >= col_i
        lower = jnp.where(causal, 1.0, 0.0).astype(F32)
        upper = jnp.where(row_i <= col_i, 1.0, 0.0).astype(F32)
        lane = lax.broadcasted_iota(jnp.int32, (SPAN, LANES), 1)
        lane_row = lax.broadcasted_iota(jnp.int32, (1, LANES), 1)
        per = LANES // head_width
        skip = []
        for group in range(channels // LANES):
            out = jnp.full((1, LANES), skip_ref[group * per], F32)
            for i in range(1, per):
                out = jnp.where(lane_row < i * head_width, out, skip_ref[group * per + i])
            skip.append(out)
        skip = jnp.concatenate(skip, axis=1)
        ld = stack_blocks(ld_ref[...], blocks)
        ld = jnp.concatenate([ld, jnp.zeros((SPAN - blocks * heads, SPAN), F32)], axis=0)
        cum = mm(lower, ld, NT, HIGH)
        cum_t = mm(ld, upper, NN, HIGH)
        group_lane = lax.broadcasted_iota(jnp.int32, (SPAN, SPAN), 1)
        earlier = jnp.zeros((SPAN, SPAN), F32)
        total = jnp.zeros((1, heads), F32)
        for j in range(blocks):
            for h in range(heads):
                earlier = jnp.where(group_lane == j * heads + h, total[:, h : h + 1], earlier)
            total = total + cum[SPAN - 1 : SPAN, j * heads : (j + 1) * heads]
        e_ref[...] = jnp.exp(jnp.minimum(earlier + cum, 0.0))
        e_cum = jnp.exp(jnp.minimum(cum, 0.0))
        for j in range(blocks):
            at = j * SPAN
            x_b = conv_ref[at : at + SPAN, :channels]
            b_b = conv_ref[at : at + SPAN, channels : channels + state_size]
            c_b = conv_ref[at : at + SPAN, channels + state_size :]
            scores = mm(c_b, b_b, NT)
            within = []
            for group in range(channels // LANES):
                x_g = x_b[:, group * LANES : (group + 1) * LANES]
                out = None
                for i in range(per):
                    h = group * per + i
                    r = j * heads + h
                    gap = cum[:, r : r + 1] - cum_t[r : r + 1, :]
                    w = jnp.exp(jnp.where(causal, gap, -1e30)) * scores * step_ref[h : h + 1, at : at + SPAN]
                    y_h = mm(w.astype(BF16), x_g, NN)
                    out = y_h if out is None else jnp.where(lane < i * head_width, out, y_h)
                within.append(out)
            within = jnp.concatenate(within, axis=1)
            y = within + skip * x_b.astype(F32)
            if j > 0:
                y = y + mm(c_b, in_ref[at : at + SPAN, :], NN) * spread(e_cum, j * heads, heads, head_width)
            y_ref[at : at + SPAN, :] = y

    vmem = pl.BlockSpec(memory_space=pltpu.VMEM)
    return pl.pallas_call(
        kernel,
        out_shape=(
            jax.ShapeDtypeStruct((rows, channels), F32),
            jax.ShapeDtypeStruct((SPAN, SPAN), F32),
        ),
        in_specs=[pl.BlockSpec(memory_space=pltpu.SMEM)] + [vmem] * 4,
        out_specs=(vmem, vmem),
        compiler_params=pltpu.CompilerParams(vmem_limit_bytes=58 << 20),
    )(skip_gain, conv, entering, step_t, decay_t)


def total_of(ref, state_size):
    rows = ref[state_size:, :].astype(F32)
    return rows[0:1] + rows[1:2] + rows[2:3]


def join_states(parts, state_size, last):
    channels = parts[0].shape[1]

    def kernel(*refs):
        ins, o_ref = refs[:-1], refs[-1]
        out = ins[0][:state_size, :].astype(F32)
        total = total_of(ins[0], state_size)
        for ref in ins[1:]:
            out = out + jnp.exp(jnp.minimum(total, 0.0)) * ref[:state_size, :].astype(F32)
            total = total + total_of(ref, state_size)
        o_ref[:state_size, :] = out.astype(BF16)
        if not last:
            o_ref[state_size:, :] = three_rows(total, 16).astype(BF16)

    height = state_size if last else state_size + 16
    return call(kernel, jax.ShapeDtypeStruct((height, channels), BF16))(*parts)


def gate_rows(y_at, y_local, conv, e_cols, arriving, gate_input, heads, x_count, y_count):
    rows, channels = y_local.shape
    blocks = rows // SPAN
    head_width = channels // heads
    state_size = arriving.shape[0]
    own = rows // (x_count * y_count)

    def kernel(at_ref, y_ref, c_ref, e_ref, a_ref, g_ref, *refs):
        outs, s_ref = refs[:-1], refs[-1]
        state = a_ref[...]
        for j in range(blocks):
            at = j * SPAN
            carried = mm(c_ref[at : at + SPAN, channels + state_size :], state, NN) * spread(
                e_ref[...], j * heads, heads, head_width
            )
            gated = (y_ref[at : at + SPAN, :] + carried) * silu(g_ref[at : at + SPAN, :].astype(F32))
            s_ref[at : at + SPAN, :] = gated.astype(BF16)
        for k in range(y_count):
            y = lax.rem(at_ref[0] + k, y_count)
            for x in range(x_count):
                first = pl.multiple_of((x * y_count + y) * own, own)
                outs[k][x * own : (x + 1) * own, :] = s_ref[pl.ds(first, own), :]

    vmem = pl.BlockSpec(memory_space=pltpu.VMEM)
    shape = jax.ShapeDtypeStruct((x_count * own, channels), BF16)
    return pl.pallas_call(
        kernel,
        out_shape=(shape,) * y_count,
        in_specs=[pl.BlockSpec(memory_space=pltpu.SMEM)] + [vmem] * 5,
        out_specs=(vmem,) * y_count,
        scratch_shapes=[pltpu.VMEM((rows, channels), BF16)],
        compiler_params=pltpu.CompilerParams(vmem_limit_bytes=58 << 20),
    )(y_at, y_local, conv, e_cols, arriving, gate_input)


def project(x_at, gated, weights, x_count):
    rows, _ = gated[0].shape
    out_width = weights[0][0].shape[1]
    own = rows // x_count
    count = len(gated)
    sizes = [len(w) for w in weights]

    def kernel(at_ref, *refs):
        g_refs = refs[:count]
        w_refs = refs[count : count + sum(sizes)]
        outs, s_ref = refs[count + sum(sizes) : -1], refs[-1]
        squares = jnp.zeros((rows, 1), F32)
        for g_ref in g_refs:
            part = g_ref[...].astype(F32)
            squares = squares + jnp.sum(part * part, axis=1, keepdims=True)
        lhs = jnp.concatenate([g_ref[...] for g_ref in g_refs], axis=1)
        size = 512
        for first in range(0, out_width, size):
            rhs = jnp.concatenate([w_ref[:, first : first + size] for w_ref in w_refs], axis=0)
            s_ref[:, first : first + size] = mm(lhs, rhs, NN).astype(BF16)
        hi = squares.astype(BF16).astype(F32)
        mid = (squares - hi).astype(BF16).astype(F32)
        low = squares - hi - mid
        lane = lax.broadcasted_iota(jnp.int32, (rows, LANES), 1)
        extra = jnp.where(lane == 0, hi, jnp.where(lane == 1, mid, jnp.where(lane == 2, low, 0.0)))
        s_ref[:, out_width:] = extra.astype(BF16)
        for k in range(x_count):
            first = pl.multiple_of(lax.rem(at_ref[0] + k, x_count) * own, own)
            outs[k][...] = s_ref[pl.ds(first, own), :]

    flat = [w for group in weights for w in group]
    vmem = pl.BlockSpec(memory_space=pltpu.VMEM)
    shape = jax.ShapeDtypeStruct((own, out_width + LANES), BF16)
    return pl.pallas_call(
        kernel,
        out_shape=(shape,) * x_count,
        in_specs=[pl.BlockSpec(memory_space=pltpu.SMEM)] + [vmem] * (count + len(flat)),
        out_specs=(vmem,) * x_count,
        scratch_shapes=[pltpu.VMEM((rows, out_width + LANES), BF16)],
        compiler_params=pltpu.CompilerParams(vmem_limit_bytes=58 << 20),
    )(x_at, *gated, *flat)


def expert_of(row, owners, local_count):
    dest = (row * 7282) >> 16
    core = dest // owners
    return local_count * (dest - core * owners) + core, row - dest * CAP


def id_columns(ids_t):
    tokens = ids_t.shape[1]
    eye = jnp.where(
        lax.broadcasted_iota(jnp.int32, (tokens, tokens), 0) == lax.broadcasted_iota(jnp.int32, (tokens, tokens), 1),
        1.0,
        0.0,
    )
    return columns_of(ids_t.astype(F32), eye), eye


def routing_rows(ids_t, expert_total, owners, local_count):
    top, tokens = ids_t.shape
    ids = (id_columns(ids_t)[0] + 0.5).astype(jnp.int32)
    slots = expert_total * CAP
    member = jnp.zeros((tokens, expert_total), F32)
    for k in range(top):
        lane = lax.broadcasted_iota(jnp.int32, (tokens, expert_total), 1)
        member = member + jnp.where(lane == ids[:, k : k + 1], 1.0, 0.0)
    member = member.astype(BF16)
    earlier = lax.broadcasted_iota(jnp.int32, (tokens, tokens), 0) > lax.broadcasted_iota(
        jnp.int32, (tokens, tokens), 1
    )
    rank = mm(jnp.where(earlier, 1.0, 0.0).astype(BF16), member, NN)
    row = lax.broadcasted_iota(jnp.int32, (slots, expert_total), 0)
    expert, _ = expert_of(row, owners, local_count)
    spreading = jnp.where(
        expert == lax.broadcasted_iota(jnp.int32, (slots, expert_total), 1), 1.0, 0.0
    ).astype(BF16)
    hit = mm(spreading, member, NT)
    rank_of = mm(spreading, rank.astype(BF16), NT)
    _, slot = expert_of(lax.broadcasted_iota(jnp.int32, (slots, tokens), 0), owners, local_count)
    return jnp.where(rank_of == slot.astype(F32), hit, 0.0).astype(BF16)


def slot_masks(ids_t, expert_total, owners, local_count):
    top, tokens = ids_t.shape
    ids = (id_columns(ids_t)[0] + 0.5).astype(jnp.int32)
    slots = expert_total * CAP
    lane = lax.broadcasted_iota(jnp.int32, (tokens, expert_total), 1)
    member = jnp.zeros((tokens, expert_total), F32)
    for k in range(top):
        member = member + jnp.where(lane == ids[:, k : k + 1], 1.0, 0.0)
    member = member.astype(BF16)
    earlier = lax.broadcasted_iota(jnp.int32, (tokens, tokens), 0) > lax.broadcasted_iota(
        jnp.int32, (tokens, tokens), 1
    )
    rank = mm(jnp.where(earlier, 1.0, 0.0).astype(BF16), member, NN)
    row = lax.broadcasted_iota(jnp.int32, (expert_total, slots), 1)
    expert, _ = expert_of(row, owners, local_count)
    spreading = jnp.where(
        expert == lax.broadcasted_iota(jnp.int32, (expert_total, slots), 0), 1.0, 0.0
    ).astype(BF16)
    rank_of = mm(rank.astype(BF16), spreading, NN)
    expert, slot = expert_of(lax.broadcasted_iota(jnp.int32, (tokens, slots), 1), owners, local_count)
    fits = rank_of == slot.astype(F32)
    return [fits & (expert == ids[:, k : k + 1]) for k in range(top)]


def to_tiles(scratch, rows, value, first=0):
    count = scratch.shape[0] // rows
    for i in range(value.shape[1] // LANES):
        scratch[pl.ds(first + i, rows, stride=count), :] = value[:, i * LANES : (i + 1) * LANES]


def dispatch_grads(ids, out_grad, expert_total, owners, local_count):
    _, width = out_grad.shape
    slots = expert_total * CAP
    count = width // LANES

    def kernel(i_ref, g_ref, o_ref, s_ref):
        pick = routing_rows(i_ref[...], expert_total, owners, local_count)
        to_tiles(s_ref, slots, mm(pick, g_ref[...], NN))
        o_ref[...] = s_ref[...].astype(BF16)

    return call(
        kernel,
        jax.ShapeDtypeStruct((slots * count, LANES), BF16),
        (pltpu.VMEM((slots * count, LANES), F32),),
    )(ids, out_grad)


def normalise(parts, residual, moe_gain, ids, inner_total, expert_total, owners, local_count):
    tokens, width = residual.shape
    slots = expert_total * CAP
    count = width // LANES
    sources = len(parts)

    def kernel(*refs):
        r_ref, m_ref, i_ref, o_ref, h_ref, v_ref, s_ref = refs[sources:]
        summed = refs[0][...].astype(F32)
        for p_ref in refs[1:sources]:
            summed = summed + p_ref[...].astype(F32)
        squares = summed[:, width : width + 1] + summed[:, width + 1 : width + 2] + summed[:, width + 2 : width + 3]
        hidden = r_ref[...].astype(F32) + summed[:, :width] * lax.rsqrt(squares / inner_total + 1e-05)
        hidden = hidden.astype(BF16)
        h_ref[...] = hidden
        hidden = hidden.astype(F32)
        inv = lax.rsqrt(jnp.mean(hidden * hidden, axis=1, keepdims=True) + 1e-06)
        v_ref[...] = jnp.broadcast_to(inv, (tokens, LANES))
        normed = (hidden * inv * m_ref[...]).astype(BF16)
        pick = routing_rows(i_ref[...], expert_total, owners, local_count)
        to_tiles(s_ref, slots, mm(pick, normed, NN))
        o_ref[...] = s_ref[...].astype(BF16)

    return call(
        kernel,
        (
            jax.ShapeDtypeStruct((slots * count, LANES), BF16),
            jax.ShapeDtypeStruct((tokens, width), BF16),
            jax.ShapeDtypeStruct((tokens, LANES), F32),
        ),
        (pltpu.VMEM((slots * count, LANES), F32),),
    )(*parts, residual, moe_gain, ids)


def pack_weights(core, gate_up, down):
    _, d_local, ff_both = gate_up.shape
    ff_width = down.shape[1]
    tiles = ff_both // LANES
    height = tiles * d_local + ff_width

    def kernel(core_ref, g_ref, d_ref, keep_ref, send_ref):
        for out_ref, e in ((keep_ref, core_ref[0]), (send_ref, 1 - core_ref[0])):
            for i in range(tiles):
                out_ref[i * d_local : (i + 1) * d_local, :] = g_ref[e, :, i * LANES : (i + 1) * LANES]
            out_ref[tiles * d_local :, :] = d_ref[e]

    vmem = pl.BlockSpec(memory_space=pltpu.VMEM)
    shape = jax.ShapeDtypeStruct((height, LANES), BF16)
    return pl.pallas_call(
        kernel,
        out_shape=(shape, shape),
        in_specs=[pl.BlockSpec(memory_space=pltpu.SMEM), vmem, vmem],
        out_specs=(vmem, vmem),
        compiler_params=pltpu.CompilerParams(vmem_limit_bytes=58 << 20),
    )(core, gate_up, down)


def experts(core, rows_in, grads_in, weights, ff_width, gu_rows):
    z_count, cores, _, _ = weights.shape
    count = z_count * cores
    slots = rows_in.shape[0] // count
    dests = slots // CAP
    ff_tiles = 2 * ff_width // LANES
    block = gu_rows // ff_tiles
    each = CAP * count

    def kernel(core_ref, x_ref, g_ref, w_hbm, o_ref, x_s, g_s, xb_s, gb_s, w_ref, sems):
        copies = [pltpu.make_async_copy(w_hbm.at[z], w_ref.at[z], sems.at[z]) for z in range(z_count)]
        for copy in copies:
            copy.start()
        core = core_ref[0]
        x_s[...] = x_ref[...].astype(F32)
        g_s[...] = g_ref[...].astype(F32)
        order = [(z, s, z * cores + (core if s == 0 else 1 - core)) for z in range(z_count) for s in range(cores)]
        for i, (z, s, c) in enumerate(order):
            xb_s[:, i * LANES : (i + 1) * LANES] = x_s[pl.ds(c, slots, stride=count), :].astype(BF16)
            gb_s[:, i * LANES : (i + 1) * LANES] = g_s[pl.ds(c, slots, stride=count), :].astype(BF16)

        def tile(z, s, i):
            return w_ref[z, s, i * block : (i + 1) * block, :]

        for copy in copies:
            copy.wait()
        projected = []
        for first in range(0, ff_tiles, 2):
            used = range(first, min(first + 2, ff_tiles))
            rhs = jnp.concatenate(
                [jnp.concatenate([tile(z, s, i) for i in used], axis=1) for z, s, _ in order], axis=0
            )
            projected.append(mm(xb_s[...], rhs, NN))
        projected = jnp.concatenate(projected, axis=1)
        hidden_grad = []
        for first in range(0, ff_width, 256):
            size = min(256, ff_width - first)
            rhs = jnp.concatenate(
                [w_ref[z, s, gu_rows + first : gu_rows + first + size, :] for z, s, _ in order], axis=1
            )
            hidden_grad.append(mm(gb_s[...], rhs, NT))
        hidden_grad = jnp.concatenate(hidden_grad, axis=1)
        pre_gate = projected[:, :ff_width]
        pre_up = projected[:, ff_width:]
        sig = 1.0 / (1.0 + jnp.exp(-pre_gate))
        act = pre_gate * sig
        activated = (act * pre_up).astype(BF16)
        grad_gate = hidden_grad * pre_up * sig * (1.0 + pre_gate * (1.0 - sig))
        grad_up = hidden_grad * act
        grad_both = jnp.concatenate([grad_gate, grad_up], axis=1).astype(BF16)
        for z in range(z_count):
            rhs = jnp.concatenate([w_ref[z, s, gu_rows:, :] for s in range(cores)], axis=1)
            out = mm(activated, rhs, NN)
            rhs = jnp.concatenate(
                [jnp.concatenate([tile(z, s, i) for i in range(ff_tiles)], axis=1) for s in range(cores)], axis=0
            )
            grad = mm(grad_both, rhs, NT)
            for s in range(cores):
                c = z * cores + (core if s == 0 else 1 - core)
                x_s[pl.ds(c, slots, stride=count), :] = out[:, s * LANES : (s + 1) * LANES]
                g_s[pl.ds(c, slots, stride=count), :] = grad[:, s * LANES : (s + 1) * LANES]
        for d in range(dests):
            o_ref[d, :each, :] = x_s[d * each : (d + 1) * each, :].astype(BF16)
            o_ref[d, each:, :] = g_s[d * each : (d + 1) * each, :].astype(BF16)

    vmem = pl.BlockSpec(memory_space=pltpu.VMEM)
    return pl.pallas_call(
        kernel,
        out_shape=jax.ShapeDtypeStruct((dests, 2 * each, LANES), BF16),
        in_specs=[pl.BlockSpec(memory_space=pltpu.SMEM), vmem, vmem, pl.BlockSpec(memory_space=pl.ANY)],
        out_specs=vmem,
        scratch_shapes=[
            pltpu.VMEM(rows_in.shape, F32),
            pltpu.VMEM(rows_in.shape, F32),
            pltpu.VMEM((slots, count * LANES), BF16),
            pltpu.VMEM((slots, count * LANES), BF16),
            pltpu.VMEM(weights.shape, BF16),
            pltpu.SemaphoreType.DMA((z_count,)),
        ],
        compiler_params=pltpu.CompilerParams(vmem_limit_bytes=58 << 20),
    )(core, rows_in, grads_in, weights)


def combine(back, hidden, inv_rms, out_grad, moe_gain, ids_t, route_t, expert_total, owners, local_count):
    tokens, width = hidden.shape
    top = ids_t.shape[0]
    count = width // LANES
    slots = expert_total * CAP
    each = CAP * count

    def kernel(r_ref, h_ref, v_ref, g_ref, m_ref, i_ref, w_ref, layer_ref, res_ref, route_ref, o_s, b_s):
        for d in range(expert_total):
            o_s[d * each : (d + 1) * each, :] = r_ref[d, :each, :].astype(F32)
            b_s[d * each : (d + 1) * each, :] = r_ref[d, each:, :].astype(F32)
        masks = slot_masks(i_ref[...], expert_total, owners, local_count)
        eye = id_columns(i_ref[...])[1]
        routes = columns_of(w_ref[...], eye)
        weight = jnp.zeros((tokens, slots), F32)
        for k in range(top):
            weight = weight + jnp.where(masks[k], routes[:, k : k + 1], 0.0)
        hi = weight.astype(BF16)
        both = jnp.concatenate([hi, (weight - hi.astype(F32)).astype(BF16)], axis=0)

        def rows_of(ref):
            return jnp.concatenate(
                [ref[pl.ds(i, slots, stride=count), :].astype(BF16) for i in range(count)], axis=1
            )

        hidden = h_ref[...].astype(F32)
        grad = g_ref[...]
        outs = rows_of(o_s)
        mixed = mm(both, outs, NN)
        layer_ref[...] = (hidden + (mixed[:tokens] + mixed[tokens:])).astype(BF16)
        dots = mm(grad, outs, NT)
        lane = lax.broadcasted_iota(jnp.int32, (tokens, top), 1)
        route = jnp.zeros((tokens, top), F32)
        for k in range(top):
            one = jnp.sum(jnp.where(masks[k], dots, 0.0), axis=1, keepdims=True)
            route = jnp.where(lane == k, one, route)
        route_ref[...] = mm(route, eye, TN, HIGH)
        mixed = mm(both, rows_of(b_s), NN)
        inv = v_ref[:, 0:1]
        unit_grad = (mixed[:tokens] + mixed[tokens:]) * m_ref[...]
        unit_rows = hidden * inv
        mean = jnp.mean(unit_grad * unit_rows, axis=1, keepdims=True)
        res_ref[...] = (grad.astype(F32) + inv * (unit_grad - unit_rows * mean)).astype(BF16)

    shape = jax.ShapeDtypeStruct((tokens, width), BF16)
    return call(
        kernel,
        (shape, shape, jax.ShapeDtypeStruct((top, tokens), F32)),
        (pltpu.VMEM((slots * count, LANES), F32), pltpu.VMEM((slots * count, LANES), F32)),
    )(back, hidden, inv_rms, out_grad, moe_gain, ids_t, route_t)


def ring_route(count, shift):
    return [(i, (i + shift) % count) for i in range(count)]


def local(
    x_inner,
    bc_input,
    gate_input,
    conv_weight,
    bc_conv_weight,
    step_size,
    log_decay,
    skip_gain,
    norm_gain,
    out_weight,
    residual,
    moe_gain,
    expert_ids,
    route_weights,
    gate_up_weight,
    down_weight,
    out_grad,
):
    ctx = ("z", "core")
    ctx_count = lax.axis_size("z") * lax.axis_size("core")
    x_count, y_count = lax.axis_size("x"), lax.axis_size("y")
    owners = x_count * y_count
    heads = step_size.shape[1]
    channels = x_inner.shape[1]
    state_size = bc_input.shape[1] // 2
    local_count, _, _ = gate_up_weight.shape
    ff_width = down_weight.shape[1]
    expert_total = local_count * owners
    exchange = ("core", "x", "y")

    ids_t, route_t = expert_ids.T, route_weights.T
    step_t, decay_t = step_size.T, log_decay.T
    core = lax.axis_index("core").astype(jnp.int32).reshape(1)

    last = jnp.concatenate([x_inner[-8:], bc_input[-8:]], axis=1)
    rim = lax.ppermute(last, ctx, [(i, i + 1) for i in range(ctx_count - 1)])

    kept, other = pack_weights(core, gate_up_weight, down_weight)
    swapped = lax.ppermute(other, "core", [(0, 1), (1, 0)])
    weights = lax.all_gather(jnp.stack([kept, swapped]), "z", axis=0, tiled=False)
    gu_rows = kept.shape[0] - ff_width

    folded = (out_weight.astype(F32) * norm_gain[:, None]).astype(BF16)
    half = folded.shape[0] // 2
    from_prev = lax.ppermute(folded, "y", ring_route(y_count, 1))
    from_next = lax.ppermute(folded, "y", ring_route(y_count, -1))
    far_a = lax.ppermute(from_prev[:half], "y", ring_route(y_count, 1))
    far_b = lax.ppermute(from_next[half:], "y", ring_route(y_count, -1))

    sent_grads = dispatch_grads(ids_t, out_grad, expert_total, owners, local_count)
    rim, sent_grads = lax.optimization_barrier((rim, sent_grads))
    grads_in = lax.all_to_all(
        sent_grads.reshape(expert_total, -1, LANES), exchange, split_axis=0, concat_axis=0, tiled=True
    )

    conv, held_in, sent = mixer_state(x_inner, bc_input, rim, conv_weight, bc_conv_weight, step_t, decay_t)
    reach = 4

    def earlier(value, distance):
        return lax.ppermute(value, ctx, [(i, i + distance) for i in range(ctx_count - distance)])

    near = [earlier(sent, d) for d in range(1, reach + 1)]
    y_local, e_cols = mixer_rows(conv, held_in, step_t, decay_t, skip_gain, channels)
    window = join_states(near, state_size, False)
    windows = [window] + [earlier(window, d) for d in range(reach, ctx_count, reach)]
    arriving = join_states(windows, state_size, True)
    arriving, grads_in = lax.optimization_barrier((arriving, grads_in))
    y_at = lax.axis_index("y").astype(jnp.int32).reshape(1)
    x_at = lax.axis_index("x").astype(jnp.int32).reshape(1)
    gated = gate_rows(y_at, y_local, conv, e_cols, arriving, gate_input, heads, x_count, y_count)
    gated = [gated[0]] + [
        lax.ppermute(gated[k], "y", ring_route(y_count, k)) for k in range(1, y_count)
    ]
    pieces = [(folded,), (from_prev,), (far_a, far_b), (from_next,)]
    parts = project(x_at, gated, pieces, x_count)
    parts = [parts[0]] + [
        lax.ppermute(parts[k], "x", ring_route(x_count, k)) for k in range(1, x_count)
    ]
    sent_rows, hidden, inv_rms = normalise(
        parts, residual, moe_gain[None, :], ids_t, channels * owners, expert_total, owners, local_count
    )
    rows_in = lax.all_to_all(
        sent_rows.reshape(expert_total, -1, LANES), exchange, split_axis=0, concat_axis=0, tiled=True
    )
    back = experts(core, rows_in.reshape(-1, LANES), grads_in.reshape(-1, LANES), weights, ff_width, gu_rows)
    back = lax.all_to_all(back, exchange, split_axis=0, concat_axis=0, tiled=True)
    layer, res, route = combine(
        back, hidden, inv_rms, out_grad, moe_gain[None, :], ids_t, route_t, expert_total, owners, local_count
    )
    return layer, res, route.T


def solution(mesh):
    ctx_count, exp_count = mesh.devices.shape
    side = int(round(exp_count**0.5))
    devices = mesh.devices.reshape(ctx_count // 2, 2, side, exp_count // side)
    fine = Mesh(devices, ("z", "core", "x", "y"))
    ctx, exp = ("z", "core"), ("x", "y")
    token = P(ctx + exp, None)
    return jax.shard_map(
        local,
        mesh=fine,
        in_specs=(
            P(ctx, exp),
            P(ctx, None),
            P(ctx, exp),
            P(None, exp),
            P(),
            P(ctx, exp),
            P(ctx, exp),
            P(exp),
            P(exp),
            P(exp, None),
            token,
            P(),
            token,
            token,
            P(exp, ctx, None),
            P(exp, None, ctx),
            token,
        ),
        out_specs=(token, token, token),
        check_vma=False,
    )
```

```python
import jax
import jax.numpy as jnp
from jax import lax
from jax.experimental import pallas as pl
from jax.experimental.pallas import tpu as pltpu
from jax.sharding import Mesh
from jax.sharding import PartitionSpec as P


F32 = jnp.float32
BF16 = jnp.bfloat16
HIGH = lax.Precision.HIGHEST
SPAN = 128
CAP = 9
LANES = 128


def mm(a, b, dims, precision=None):
    return lax.dot_general(a, b, (dims, ((), ())), precision=precision, preferred_element_type=F32)


NN = ((1,), (0,))
NT = ((1,), (1,))
TN = ((0,), (0,))


def silu(v):
    return v * (1.0 / (1.0 + jnp.exp(-v)))


def call(kernel, outs, scratch=()):
    return pl.pallas_call(
        kernel,
        out_shape=outs,
        scratch_shapes=list(scratch),
        compiler_params=pltpu.CompilerParams(vmem_limit_bytes=58 << 20),
    )


def spread(values, first, heads, head_width):
    rows = values.shape[0]
    per = LANES // head_width
    lane = lax.broadcasted_iota(jnp.int32, (rows, LANES), 1)
    parts = []
    for group in range(heads // per):
        out = jnp.broadcast_to(values[:, first + group * per : first + group * per + 1], (rows, LANES))
        for i in range(1, per):
            col = first + group * per + i
            out = jnp.where(
                lane < i * head_width, out, jnp.broadcast_to(values[:, col : col + 1], (rows, LANES))
            )
        parts.append(out)
    return jnp.concatenate(parts, axis=1)


def columns_of(transposed, eye):
    return mm(eye, transposed, NT, HIGH)


def stack_blocks(values, blocks):
    return jnp.concatenate([values[:, j * SPAN : (j + 1) * SPAN] for j in range(blocks)], axis=0)


def three_rows(total, rows):
    hi = total.astype(BF16).astype(F32)
    mid = (total - hi).astype(BF16).astype(F32)
    low = total - hi - mid
    pick = lax.broadcasted_iota(jnp.int32, (rows, total.shape[1]), 0)
    return jnp.where(pick == 0, hi, jnp.where(pick == 1, mid, jnp.where(pick == 2, low, 0.0)))


def mixer_state(x_inner, bc_input, rim, conv_weight, bc_weight, step_t, decay_t):
    rows, channels = x_inner.shape
    heads = step_t.shape[0]
    state_size = bc_input.shape[1] // 2
    width = channels + 2 * state_size
    head_width = channels // heads
    blocks = rows // SPAN
    kernel_len = conv_weight.shape[0]

    def kernel(x_ref, bc_ref, rim_ref, wx_ref, wb_ref, step_ref, ld_ref, conv_ref, in_ref, send_ref, pad_ref):
        row_i = lax.broadcasted_iota(jnp.int32, (SPAN, SPAN), 0)
        col_i = lax.broadcasted_iota(jnp.int32, (SPAN, SPAN), 1)
        later = jnp.where(row_i < col_i, 1.0, 0.0).astype(F32)
        eye = jnp.where(row_i == col_i, 1.0, 0.0).astype(F32)
        ones = jnp.ones((8, SPAN), F32)
        ld = stack_blocks(ld_ref[...], blocks)
        left = jnp.exp(jnp.minimum(mm(later, ld, NT, HIGH), 0.0))
        tails = left * columns_of(stack_blocks(step_ref[...], blocks), eye)
        lasts = mm(ones, ld, NT, HIGH)
        decays = jnp.exp(jnp.minimum(lasts, 0.0))
        weight = jnp.concatenate([wx_ref[...], wb_ref[...]], axis=1)
        held = None
        total = None
        pad_ref[0:8, :] = rim_ref[...].astype(F32)
        for j in range(blocks):
            at = j * SPAN
            pad_ref[8 + at : 8 + at + SPAN, :channels] = x_ref[at : at + SPAN, :].astype(F32)
            pad_ref[8 + at : 8 + at + SPAN, channels:] = bc_ref[at : at + SPAN, :].astype(F32)
            summed = None
            for k in range(kernel_len):
                begin = at + 8 - kernel_len + 1 + k
                term = weight[k : k + 1, :] * pad_ref[begin : begin + SPAN, :]
                summed = term if summed is None else summed + term
            conv = silu(summed).astype(BF16)
            conv_ref[at : at + SPAN, :] = conv
            x_t = (conv[:, :channels].astype(F32) * spread(tails, j * heads, heads, head_width)).astype(BF16)
            state = mm(conv[:, channels : channels + state_size], x_t, TN)
            if j == 0:
                in_ref[at : at + SPAN, :] = jnp.zeros((state_size, channels), BF16)
                held = state
                total = lasts[:, :heads]
            else:
                in_ref[at : at + SPAN, :] = held.astype(BF16)
                held = spread(decays, j * heads, heads, head_width)[0:1, :] * held + state
                total = total + lasts[:, j * heads : (j + 1) * heads]
        send_ref[:state_size, :] = held.astype(BF16)
        extra = three_rows(spread(total, 0, heads, head_width)[0:1, :], 16)
        send_ref[state_size:, :] = extra.astype(BF16)

    return call(
        kernel,
        (
            jax.ShapeDtypeStruct((rows, width), BF16),
            jax.ShapeDtypeStruct((blocks * state_size, channels), BF16),
            jax.ShapeDtypeStruct((state_size + 16, channels), BF16),
        ),
        (pltpu.VMEM((rows + 8, width), F32),),
    )(x_inner, bc_input, rim, conv_weight, bc_weight, step_t, decay_t)


def mixer_rows(conv, entering, step_t, decay_t, skip_gain, channels):
    rows = conv.shape[0]
    heads = step_t.shape[0]
    state_size = (conv.shape[1] - channels) // 2
    head_width = channels // heads
    blocks = rows // SPAN

    def kernel(skip_ref, conv_ref, in_ref, step_ref, ld_ref, y_ref, e_ref):
        row_i = lax.broadcasted_iota(jnp.int32, (SPAN, SPAN), 0)
        col_i = lax.broadcasted_iota(jnp.int32, (SPAN, SPAN), 1)
        causal = row_i >= col_i
        lower = jnp.where(causal, 1.0, 0.0).astype(F32)
        upper = jnp.where(row_i <= col_i, 1.0, 0.0).astype(F32)
        lane = lax.broadcasted_iota(jnp.int32, (SPAN, LANES), 1)
        lane_row = lax.broadcasted_iota(jnp.int32, (1, LANES), 1)
        per = LANES // head_width
        skip = []
        for group in range(channels // LANES):
            out = jnp.full((1, LANES), skip_ref[group * per], F32)
            for i in range(1, per):
                out = jnp.where(lane_row < i * head_width, out, skip_ref[group * per + i])
            skip.append(out)
        skip = jnp.concatenate(skip, axis=1)
        ld = stack_blocks(ld_ref[...], blocks)
        ld = jnp.concatenate([ld, jnp.zeros((SPAN - blocks * heads, SPAN), F32)], axis=0)
        cum = mm(lower, ld, NT, HIGH)
        cum_t = mm(ld, upper, NN, HIGH)
        group_lane = lax.broadcasted_iota(jnp.int32, (SPAN, SPAN), 1)
        earlier = jnp.zeros((SPAN, SPAN), F32)
        total = jnp.zeros((1, heads), F32)
        for j in range(blocks):
            for h in range(heads):
                earlier = jnp.where(group_lane == j * heads + h, total[:, h : h + 1], earlier)
            total = total + cum[SPAN - 1 : SPAN, j * heads : (j + 1) * heads]
        e_ref[...] = jnp.exp(jnp.minimum(earlier + cum, 0.0))
        e_cum = jnp.exp(jnp.minimum(cum, 0.0))
        for j in range(blocks):
            at = j * SPAN
            x_b = conv_ref[at : at + SPAN, :channels]
            b_b = conv_ref[at : at + SPAN, channels : channels + state_size]
            c_b = conv_ref[at : at + SPAN, channels + state_size :]
            scores = mm(c_b, b_b, NT)
            within = []
            for group in range(channels // LANES):
                x_g = x_b[:, group * LANES : (group + 1) * LANES]
                out = None
                for i in range(per):
                    h = group * per + i
                    r = j * heads + h
                    gap = cum[:, r : r + 1] - cum_t[r : r + 1, :]
                    w = jnp.exp(jnp.where(causal, gap, -1e30)) * scores * step_ref[h : h + 1, at : at + SPAN]
                    y_h = mm(w.astype(BF16), x_g, NN)
                    out = y_h if out is None else jnp.where(lane < i * head_width, out, y_h)
                within.append(out)
            within = jnp.concatenate(within, axis=1)
            y = within + skip * x_b.astype(F32)
            if j > 0:
                y = y + mm(c_b, in_ref[at : at + SPAN, :], NN) * spread(e_cum, j * heads, heads, head_width)
            y_ref[at : at + SPAN, :] = y

    vmem = pl.BlockSpec(memory_space=pltpu.VMEM)
    return pl.pallas_call(
        kernel,
        out_shape=(
            jax.ShapeDtypeStruct((rows, channels), F32),
            jax.ShapeDtypeStruct((SPAN, SPAN), F32),
        ),
        in_specs=[pl.BlockSpec(memory_space=pltpu.SMEM)] + [vmem] * 4,
        out_specs=(vmem, vmem),
        compiler_params=pltpu.CompilerParams(vmem_limit_bytes=58 << 20),
    )(skip_gain, conv, entering, step_t, decay_t)


def total_of(ref, state_size):
    rows = ref[state_size:, :].astype(F32)
    return rows[0:1] + rows[1:2] + rows[2:3]


def join_states(parts, state_size, last):
    channels = parts[0].shape[1]

    def kernel(*refs):
        ins, o_ref = refs[:-1], refs[-1]
        out = ins[0][:state_size, :].astype(F32)
        total = total_of(ins[0], state_size)
        for ref in ins[1:]:
            out = out + jnp.exp(jnp.minimum(total, 0.0)) * ref[:state_size, :].astype(F32)
            total = total + total_of(ref, state_size)
        o_ref[:state_size, :] = out.astype(BF16)
        if not last:
            o_ref[state_size:, :] = three_rows(total, 16).astype(BF16)

    height = state_size if last else state_size + 16
    return call(kernel, jax.ShapeDtypeStruct((height, channels), BF16))(*parts)


def gate_rows(y_at, y_local, conv, e_cols, arriving, gate_input, heads, x_count, y_count):
    rows, channels = y_local.shape
    blocks = rows // SPAN
    head_width = channels // heads
    state_size = arriving.shape[0]
    own = rows // (x_count * y_count)

    def kernel(at_ref, y_ref, c_ref, e_ref, a_ref, g_ref, *refs):
        outs, s_ref = refs[:-1], refs[-1]
        state = a_ref[...]
        for j in range(blocks):
            at = j * SPAN
            carried = mm(c_ref[at : at + SPAN, channels + state_size :], state, NN) * spread(
                e_ref[...], j * heads, heads, head_width
            )
            gated = (y_ref[at : at + SPAN, :] + carried) * silu(g_ref[at : at + SPAN, :].astype(F32))
            s_ref[at : at + SPAN, :] = gated.astype(BF16)
        for k in range(y_count):
            y = lax.rem(at_ref[0] + k, y_count)
            for x in range(x_count):
                first = pl.multiple_of((x * y_count + y) * own, own)
                outs[k][x * own : (x + 1) * own, :] = s_ref[pl.ds(first, own), :]

    vmem = pl.BlockSpec(memory_space=pltpu.VMEM)
    shape = jax.ShapeDtypeStruct((x_count * own, channels), BF16)
    return pl.pallas_call(
        kernel,
        out_shape=(shape,) * y_count,
        in_specs=[pl.BlockSpec(memory_space=pltpu.SMEM)] + [vmem] * 5,
        out_specs=(vmem,) * y_count,
        scratch_shapes=[pltpu.VMEM((rows, channels), BF16)],
        compiler_params=pltpu.CompilerParams(vmem_limit_bytes=58 << 20),
    )(y_at, y_local, conv, e_cols, arriving, gate_input)


def project(x_at, gated, weights, x_count):
    rows, _ = gated[0].shape
    out_width = weights[0][0].shape[1]
    own = rows // x_count
    count = len(gated)
    sizes = [len(w) for w in weights]

    def kernel(at_ref, *refs):
        g_refs = refs[:count]
        w_refs = refs[count : count + sum(sizes)]
        outs, s_ref = refs[count + sum(sizes) : -1], refs[-1]
        squares = jnp.zeros((rows, 1), F32)
        for g_ref in g_refs:
            part = g_ref[...].astype(F32)
            squares = squares + jnp.sum(part * part, axis=1, keepdims=True)
        lhs = jnp.concatenate([g_ref[...] for g_ref in g_refs], axis=1)
        size = 512
        for first in range(0, out_width, size):
            rhs = jnp.concatenate([w_ref[:, first : first + size] for w_ref in w_refs], axis=0)
            s_ref[:, first : first + size] = mm(lhs, rhs, NN).astype(BF16)
        hi = squares.astype(BF16).astype(F32)
        mid = (squares - hi).astype(BF16).astype(F32)
        low = squares - hi - mid
        lane = lax.broadcasted_iota(jnp.int32, (rows, LANES), 1)
        extra = jnp.where(lane == 0, hi, jnp.where(lane == 1, mid, jnp.where(lane == 2, low, 0.0)))
        s_ref[:, out_width:] = extra.astype(BF16)
        for k in range(x_count):
            first = pl.multiple_of(lax.rem(at_ref[0] + k, x_count) * own, own)
            outs[k][...] = s_ref[pl.ds(first, own), :]

    flat = [w for group in weights for w in group]
    vmem = pl.BlockSpec(memory_space=pltpu.VMEM)
    shape = jax.ShapeDtypeStruct((own, out_width + LANES), BF16)
    return pl.pallas_call(
        kernel,
        out_shape=(shape,) * x_count,
        in_specs=[pl.BlockSpec(memory_space=pltpu.SMEM)] + [vmem] * (count + len(flat)),
        out_specs=(vmem,) * x_count,
        scratch_shapes=[pltpu.VMEM((rows, out_width + LANES), BF16)],
        compiler_params=pltpu.CompilerParams(vmem_limit_bytes=58 << 20),
    )(x_at, *gated, *flat)


def expert_of(row, owners, local_count):
    dest = (row * 7282) >> 16
    core = dest // owners
    return local_count * (dest - core * owners) + core, row - dest * CAP


def id_columns(ids_t):
    tokens = ids_t.shape[1]
    eye = jnp.where(
        lax.broadcasted_iota(jnp.int32, (tokens, tokens), 0) == lax.broadcasted_iota(jnp.int32, (tokens, tokens), 1),
        1.0,
        0.0,
    )
    return columns_of(ids_t.astype(F32), eye), eye


def routing_rows(ids_t, expert_total, owners, local_count):
    top, tokens = ids_t.shape
    ids = (id_columns(ids_t)[0] + 0.5).astype(jnp.int32)
    slots = expert_total * CAP
    member = jnp.zeros((tokens, expert_total), F32)
    for k in range(top):
        lane = lax.broadcasted_iota(jnp.int32, (tokens, expert_total), 1)
        member = member + jnp.where(lane == ids[:, k : k + 1], 1.0, 0.0)
    member = member.astype(BF16)
    earlier = lax.broadcasted_iota(jnp.int32, (tokens, tokens), 0) > lax.broadcasted_iota(
        jnp.int32, (tokens, tokens), 1
    )
    rank = mm(jnp.where(earlier, 1.0, 0.0).astype(BF16), member, NN)
    row = lax.broadcasted_iota(jnp.int32, (slots, expert_total), 0)
    expert, _ = expert_of(row, owners, local_count)
    spreading = jnp.where(
        expert == lax.broadcasted_iota(jnp.int32, (slots, expert_total), 1), 1.0, 0.0
    ).astype(BF16)
    hit = mm(spreading, member, NT)
    rank_of = mm(spreading, rank.astype(BF16), NT)
    _, slot = expert_of(lax.broadcasted_iota(jnp.int32, (slots, tokens), 0), owners, local_count)
    return jnp.where(rank_of == slot.astype(F32), hit, 0.0).astype(BF16)


def slot_masks(ids_t, expert_total, owners, local_count):
    top, tokens = ids_t.shape
    ids = (id_columns(ids_t)[0] + 0.5).astype(jnp.int32)
    slots = expert_total * CAP
    lane = lax.broadcasted_iota(jnp.int32, (tokens, expert_total), 1)
    member = jnp.zeros((tokens, expert_total), F32)
    for k in range(top):
        member = member + jnp.where(lane == ids[:, k : k + 1], 1.0, 0.0)
    member = member.astype(BF16)
    earlier = lax.broadcasted_iota(jnp.int32, (tokens, tokens), 0) > lax.broadcasted_iota(
        jnp.int32, (tokens, tokens), 1
    )
    rank = mm(jnp.where(earlier, 1.0, 0.0).astype(BF16), member, NN)
    row = lax.broadcasted_iota(jnp.int32, (expert_total, slots), 1)
    expert, _ = expert_of(row, owners, local_count)
    spreading = jnp.where(
        expert == lax.broadcasted_iota(jnp.int32, (expert_total, slots), 0), 1.0, 0.0
    ).astype(BF16)
    rank_of = mm(rank.astype(BF16), spreading, NN)
    expert, slot = expert_of(lax.broadcasted_iota(jnp.int32, (tokens, slots), 1), owners, local_count)
    fits = rank_of == slot.astype(F32)
    return [fits & (expert == ids[:, k : k + 1]) for k in range(top)]


def to_tiles(scratch, rows, value, first=0):
    count = scratch.shape[0] // rows
    for i in range(value.shape[1] // LANES):
        scratch[pl.ds(first + i, rows, stride=count), :] = value[:, i * LANES : (i + 1) * LANES]


def dispatch_grads(ids, out_grad, expert_total, owners, local_count):
    _, width = out_grad.shape
    slots = expert_total * CAP
    count = width // LANES

    def kernel(i_ref, g_ref, o_ref, s_ref):
        pick = routing_rows(i_ref[...], expert_total, owners, local_count)
        to_tiles(s_ref, slots, mm(pick, g_ref[...], NN))
        o_ref[...] = s_ref[...].astype(BF16)

    return call(
        kernel,
        jax.ShapeDtypeStruct((slots * count, LANES), BF16),
        (pltpu.VMEM((slots * count, LANES), F32),),
    )(ids, out_grad)


def normalise(parts, residual, moe_gain, ids, inner_total, expert_total, owners, local_count):
    tokens, width = residual.shape
    slots = expert_total * CAP
    count = width // LANES
    sources = len(parts)

    def kernel(*refs):
        r_ref, m_ref, i_ref, o_ref, h_ref, v_ref, s_ref = refs[sources:]
        summed = refs[0][...].astype(F32)
        for p_ref in refs[1:sources]:
            summed = summed + p_ref[...].astype(F32)
        squares = summed[:, width : width + 1] + summed[:, width + 1 : width + 2] + summed[:, width + 2 : width + 3]
        hidden = r_ref[...].astype(F32) + summed[:, :width] * lax.rsqrt(squares / inner_total + 1e-05)
        hidden = hidden.astype(BF16)
        h_ref[...] = hidden
        hidden = hidden.astype(F32)
        inv = lax.rsqrt(jnp.mean(hidden * hidden, axis=1, keepdims=True) + 1e-06)
        v_ref[...] = jnp.broadcast_to(inv, (tokens, LANES))
        normed = (hidden * inv * m_ref[...]).astype(BF16)
        pick = routing_rows(i_ref[...], expert_total, owners, local_count)
        to_tiles(s_ref, slots, mm(pick, normed, NN))
        o_ref[...] = s_ref[...].astype(BF16)

    return call(
        kernel,
        (
            jax.ShapeDtypeStruct((slots * count, LANES), BF16),
            jax.ShapeDtypeStruct((tokens, width), BF16),
            jax.ShapeDtypeStruct((tokens, LANES), F32),
        ),
        (pltpu.VMEM((slots * count, LANES), F32),),
    )(*parts, residual, moe_gain, ids)


def pack_weights(core, gate_up, down):
    _, d_local, ff_both = gate_up.shape
    ff_width = down.shape[1]
    tiles = ff_both // LANES
    height = tiles * d_local + ff_width

    def kernel(core_ref, g_ref, d_ref, keep_ref, send_ref):
        for out_ref, e in ((keep_ref, core_ref[0]), (send_ref, 1 - core_ref[0])):
            for i in range(tiles):
                out_ref[i * d_local : (i + 1) * d_local, :] = g_ref[e, :, i * LANES : (i + 1) * LANES]
            out_ref[tiles * d_local :, :] = d_ref[e]

    vmem = pl.BlockSpec(memory_space=pltpu.VMEM)
    shape = jax.ShapeDtypeStruct((height, LANES), BF16)
    return pl.pallas_call(
        kernel,
        out_shape=(shape, shape),
        in_specs=[pl.BlockSpec(memory_space=pltpu.SMEM), vmem, vmem],
        out_specs=(vmem, vmem),
        compiler_params=pltpu.CompilerParams(vmem_limit_bytes=58 << 20),
    )(core, gate_up, down)


def weight_copies(w_hbm, w_ref, sems):
    return [pltpu.make_async_copy(w_hbm.at[z], w_ref.at[z], sems.at[z]) for z in range(w_hbm.shape[0])]


def columns_in_order(z_count, cores, core):
    return [(z, s, z * cores + (core if s == 0 else 1 - core)) for z in range(z_count) for s in range(cores)]


def experts(core, rows_in, grads_in, weights, ff_width, gu_rows):
    z_count, cores, _, _ = weights.shape
    count = z_count * cores
    slots = rows_in.shape[0] // count
    ff_tiles = 2 * ff_width // LANES
    block = gu_rows // ff_tiles

    def kernel(core_ref, x_ref, g_ref, w_hbm, o_ref, b_ref, x_s, g_s, xb_s, gb_s, w_ref, sems):
        copies = weight_copies(w_hbm, w_ref, sems)
        for copy in copies:
            copy.start()
        order = columns_in_order(z_count, cores, core_ref[0])
        x_s[...] = x_ref[...].astype(F32)
        g_s[...] = g_ref[...].astype(F32)
        for i, (z, s, c) in enumerate(order):
            xb_s[:, i * LANES : (i + 1) * LANES] = x_s[pl.ds(c, slots, stride=count), :].astype(BF16)
            gb_s[:, i * LANES : (i + 1) * LANES] = g_s[pl.ds(c, slots, stride=count), :].astype(BF16)

        def tile(z, s, i):
            return w_ref[z, s, i * block : (i + 1) * block, :]

        for copy in copies:
            copy.wait()
        projected = []
        for first in range(0, ff_tiles, 2):
            used = range(first, min(first + 2, ff_tiles))
            rhs = jnp.concatenate(
                [jnp.concatenate([tile(z, s, i) for i in used], axis=1) for z, s, _ in order], axis=0
            )
            projected.append(mm(xb_s[...], rhs, NN))
        projected = jnp.concatenate(projected, axis=1)
        hidden_grad = []
        for first in range(0, ff_width, 256):
            size = min(256, ff_width - first)
            rhs = jnp.concatenate(
                [w_ref[z, s, gu_rows + first : gu_rows + first + size, :] for z, s, _ in order], axis=1
            )
            hidden_grad.append(mm(gb_s[...], rhs, NT))
        hidden_grad = jnp.concatenate(hidden_grad, axis=1)
        pre_gate = projected[:, :ff_width]
        pre_up = projected[:, ff_width:]
        sig = 1.0 / (1.0 + jnp.exp(-pre_gate))
        act = pre_gate * sig
        activated = (act * pre_up).astype(BF16)
        grad_gate = hidden_grad * pre_up * sig * (1.0 + pre_gate * (1.0 - sig))
        grad_up = hidden_grad * act
        b_ref[...] = jnp.concatenate([grad_gate, grad_up], axis=1).astype(BF16)
        for z in range(z_count):
            rhs = jnp.concatenate([w_ref[z, s, gu_rows:, :] for s in range(cores)], axis=1)
            out = mm(activated, rhs, NN)
            for s in range(cores):
                c = order[z * cores + s][2]
                x_s[pl.ds(c, slots, stride=count), :] = out[:, s * LANES : (s + 1) * LANES]
        o_ref[...] = x_s[...].astype(BF16)

    vmem = pl.BlockSpec(memory_space=pltpu.VMEM)
    return pl.pallas_call(
        kernel,
        out_shape=(
            jax.ShapeDtypeStruct(rows_in.shape, BF16),
            jax.ShapeDtypeStruct((slots, 2 * ff_width), BF16),
        ),
        in_specs=[pl.BlockSpec(memory_space=pltpu.SMEM), vmem, vmem, pl.BlockSpec(memory_space=pl.ANY)],
        out_specs=(vmem, vmem),
        scratch_shapes=[
            pltpu.VMEM(rows_in.shape, F32),
            pltpu.VMEM(rows_in.shape, F32),
            pltpu.VMEM((slots, count * LANES), BF16),
            pltpu.VMEM((slots, count * LANES), BF16),
            pltpu.VMEM(weights.shape, BF16),
            pltpu.SemaphoreType.DMA((z_count,)),
        ],
        compiler_params=pltpu.CompilerParams(vmem_limit_bytes=58 << 20),
    )(core, rows_in, grads_in, weights)


def expert_inputs(core, grad_both, weights, gu_rows):
    z_count, cores, _, _ = weights.shape
    count = z_count * cores
    slots, ff_both = grad_both.shape
    ff_tiles = ff_both // LANES
    block = gu_rows // ff_tiles

    def kernel(core_ref, b_ref, w_hbm, o_ref, s_ref, w_ref, sems):
        copies = [
            pltpu.make_async_copy(w_hbm.at[z, :, pl.ds(0, gu_rows), :], w_ref.at[z], sems.at[z])
            for z in range(z_count)
        ]
        for copy in copies:
            copy.start()
        order = columns_in_order(z_count, cores, core_ref[0])
        for z in range(z_count):
            copies[z].wait()
            rhs = jnp.concatenate(
                [
                    jnp.concatenate([w_ref[z, s, i * block : (i + 1) * block, :] for i in range(ff_tiles)], axis=1)
                    for s in range(cores)
                ],
                axis=0,
            )
            grad = mm(b_ref[...], rhs, NT)
            for s in range(cores):
                c = order[z * cores + s][2]
                s_ref[pl.ds(c, slots, stride=count), :] = grad[:, s * LANES : (s + 1) * LANES]
        o_ref[...] = s_ref[...].astype(BF16)

    vmem = pl.BlockSpec(memory_space=pltpu.VMEM)
    return pl.pallas_call(
        kernel,
        out_shape=jax.ShapeDtypeStruct((slots * count, LANES), BF16),
        in_specs=[pl.BlockSpec(memory_space=pltpu.SMEM), vmem, pl.BlockSpec(memory_space=pl.ANY)],
        out_specs=vmem,
        scratch_shapes=[
            pltpu.VMEM((slots * count, LANES), F32),
            pltpu.VMEM((z_count, cores, gu_rows, LANES), BF16),
            pltpu.SemaphoreType.DMA((z_count,)),
        ],
        compiler_params=pltpu.CompilerParams(vmem_limit_bytes=58 << 20),
    )(core, grad_both, weights)


def gathered_rows(ref, slots, count):
    return jnp.concatenate(
        [ref[pl.ds(i, slots, stride=count), :].astype(BF16) for i in range(count)], axis=1
    )


def combine_outputs(outs, hidden, out_grad, ids_t, route_t, expert_total, owners, local_count):
    tokens, width = hidden.shape
    top = ids_t.shape[0]
    count = width // LANES
    slots = expert_total * CAP

    def kernel(r_ref, h_ref, g_ref, i_ref, w_ref, layer_ref, route_ref, both_ref, o_s):
        o_s[...] = r_ref[...].astype(F32)
        masks = slot_masks(i_ref[...], expert_total, owners, local_count)
        eye = id_columns(i_ref[...])[1]
        routes = columns_of(w_ref[...], eye)
        weight = jnp.zeros((tokens, slots), F32)
        for k in range(top):
            weight = weight + jnp.where(masks[k], routes[:, k : k + 1], 0.0)
        hi = weight.astype(BF16)
        both = jnp.concatenate([hi, (weight - hi.astype(F32)).astype(BF16)], axis=0)
        both_ref[...] = both
        outs = gathered_rows(o_s, slots, count)
        mixed = mm(both, outs, NN)
        layer_ref[...] = (h_ref[...].astype(F32) + (mixed[:tokens] + mixed[tokens:])).astype(BF16)
        dots = mm(g_ref[...], outs, NT)
        lane = lax.broadcasted_iota(jnp.int32, (tokens, top), 1)
        route = jnp.zeros((tokens, top), F32)
        for k in range(top):
            one = jnp.sum(jnp.where(masks[k], dots, 0.0), axis=1, keepdims=True)
            route = jnp.where(lane == k, one, route)
        route_ref[...] = mm(route, eye, TN, HIGH)

    return call(
        kernel,
        (
            jax.ShapeDtypeStruct((tokens, width), BF16),
            jax.ShapeDtypeStruct((top, tokens), F32),
            jax.ShapeDtypeStruct((2 * tokens, slots), BF16),
        ),
        (pltpu.VMEM((slots * count, LANES), F32),),
    )(outs, hidden, out_grad, ids_t, route_t)


def combine_grads(grads, both, hidden, inv_rms, out_grad, moe_gain):
    tokens, width = hidden.shape
    count = width // LANES
    slots = both.shape[1]

    def kernel(r_ref, both_ref, h_ref, v_ref, g_ref, m_ref, res_ref, b_s):
        b_s[...] = r_ref[...].astype(F32)
        mixed = mm(both_ref[...], gathered_rows(b_s, slots, count), NN)
        inv = v_ref[:, 0:1]
        unit_grad = (mixed[:tokens] + mixed[tokens:]) * m_ref[...]
        unit_rows = h_ref[...].astype(F32) * inv
        mean = jnp.mean(unit_grad * unit_rows, axis=1, keepdims=True)
        res_ref[...] = (g_ref[...].astype(F32) + inv * (unit_grad - unit_rows * mean)).astype(BF16)

    return call(
        kernel,
        jax.ShapeDtypeStruct((tokens, width), BF16),
        (pltpu.VMEM((slots * count, LANES), F32),),
    )(grads, both, hidden, inv_rms, out_grad, moe_gain)


def ring_route(count, shift):
    return [(i, (i + shift) % count) for i in range(count)]


def local(
    x_inner,
    bc_input,
    gate_input,
    conv_weight,
    bc_conv_weight,
    step_size,
    log_decay,
    skip_gain,
    norm_gain,
    out_weight,
    residual,
    moe_gain,
    expert_ids,
    route_weights,
    gate_up_weight,
    down_weight,
    out_grad,
):
    ctx = ("z", "core")
    ctx_count = lax.axis_size("z") * lax.axis_size("core")
    x_count, y_count = lax.axis_size("x"), lax.axis_size("y")
    owners = x_count * y_count
    heads = step_size.shape[1]
    channels = x_inner.shape[1]
    state_size = bc_input.shape[1] // 2
    local_count, _, _ = gate_up_weight.shape
    ff_width = down_weight.shape[1]
    expert_total = local_count * owners
    exchange = ("core", "x", "y")

    ids_t, route_t = expert_ids.T, route_weights.T
    step_t, decay_t = step_size.T, log_decay.T
    core = lax.axis_index("core").astype(jnp.int32).reshape(1)

    last = jnp.concatenate([x_inner[-8:], bc_input[-8:]], axis=1)
    rim = lax.ppermute(last, ctx, [(i, i + 1) for i in range(ctx_count - 1)])

    folded = (out_weight.astype(F32) * norm_gain[:, None]).astype(BF16)
    half = folded.shape[0] // 2
    from_prev = lax.ppermute(folded, "y", ring_route(y_count, 1))
    from_next = lax.ppermute(folded, "y", ring_route(y_count, -1))
    far_a = lax.ppermute(from_prev[:half], "y", ring_route(y_count, 1))
    far_b = lax.ppermute(from_next[half:], "y", ring_route(y_count, -1))

    kept, other = pack_weights(core, gate_up_weight, down_weight)
    swapped = lax.ppermute(other, "core", [(0, 1), (1, 0)])

    conv, held_in, sent = mixer_state(x_inner, bc_input, rim, conv_weight, bc_conv_weight, step_t, decay_t)
    reach = 4

    def earlier(value, distance):
        return lax.ppermute(value, ctx, [(i, i + distance) for i in range(ctx_count - distance)])

    near = [earlier(sent, d) for d in range(1, reach + 1)]
    kept, swapped, conv = lax.optimization_barrier((kept, swapped, conv))
    stacked = jnp.stack([kept, swapped])
    weights = lax.all_gather(stacked, "z", axis=0, tiled=False)
    gu_rows = kept.shape[0] - ff_width
    y_local, e_cols = mixer_rows(conv, held_in, step_t, decay_t, skip_gain, channels)
    window = join_states(near, state_size, False)
    windows = [window] + [earlier(window, d) for d in range(reach, ctx_count, reach)]

    sent_grads = dispatch_grads(ids_t, out_grad, expert_total, owners, local_count)
    grads_in = lax.all_to_all(
        sent_grads.reshape(expert_total, -1, LANES), exchange, split_axis=0, concat_axis=0, tiled=True
    )

    arriving = join_states(windows, state_size, True)
    y_at = lax.axis_index("y").astype(jnp.int32).reshape(1)
    x_at = lax.axis_index("x").astype(jnp.int32).reshape(1)
    gated = gate_rows(y_at, y_local, conv, e_cols, arriving, gate_input, heads, x_count, y_count)
    gated = [gated[0]] + [
        lax.ppermute(gated[k], "y", ring_route(y_count, k)) for k in range(1, y_count)
    ]
    gated, grads_in = lax.optimization_barrier((gated, grads_in))
    pieces = [(folded,), (from_prev,), (far_a, far_b), (from_next,)]
    parts = project(x_at, gated, pieces, x_count)
    parts = [parts[0]] + [
        lax.ppermute(parts[k], "x", ring_route(x_count, k)) for k in range(1, x_count)
    ]
    sent_rows, hidden, inv_rms = normalise(
        parts, residual, moe_gain[None, :], ids_t, channels * owners, expert_total, owners, local_count
    )
    rows_in = lax.all_to_all(
        sent_rows.reshape(expert_total, -1, LANES), exchange, split_axis=0, concat_axis=0, tiled=True
    )
    outs, grad_both = experts(
        core, rows_in.reshape(-1, LANES), grads_in.reshape(-1, LANES), weights, ff_width, gu_rows
    )
    outs = lax.all_to_all(
        outs.reshape(expert_total, -1, LANES), exchange, split_axis=0, concat_axis=0, tiled=True
    )
    grads = expert_inputs(core, grad_both, weights, gu_rows)
    grads = lax.all_to_all(grads.reshape(expert_total, -1, LANES), exchange, split_axis=0, concat_axis=0, tiled=True)
    layer, route, both = combine_outputs(
        outs.reshape(-1, LANES), hidden, out_grad, ids_t, route_t, expert_total, owners, local_count
    )
    res = combine_grads(grads.reshape(-1, LANES), both, hidden, inv_rms, out_grad, moe_gain[None, :])
    return layer, res, route.T


def solution(mesh):
    ctx_count, exp_count = mesh.devices.shape
    side = int(round(exp_count**0.5))
    devices = mesh.devices.reshape(ctx_count // 2, 2, side, exp_count // side)
    fine = Mesh(devices, ("z", "core", "x", "y"))
    ctx, exp = ("z", "core"), ("x", "y")
    token = P(ctx + exp, None)
    return jax.shard_map(
        local,
        mesh=fine,
        in_specs=(
            P(ctx, exp),
            P(ctx, None),
            P(ctx, exp),
            P(None, exp),
            P(),
            P(ctx, exp),
            P(ctx, exp),
            P(exp),
            P(exp),
            P(exp, None),
            token,
            P(),
            token,
            token,
            P(exp, ctx, None),
            P(exp, None, ctx),
            token,
        ),
        out_specs=(token, token, token),
        check_vma=False,
    )
```

```python
import jax
import jax.numpy as jnp
from jax import lax
from jax.experimental import pallas as pl
from jax.experimental.pallas import tpu as pltpu
from jax.sharding import Mesh
from jax.sharding import PartitionSpec as P


F32 = jnp.float32
BF16 = jnp.bfloat16
HIGH = lax.Precision.HIGHEST
SPAN = 128
CAP = 9
LANES = 128


def mm(a, b, dims, precision=None):
    return lax.dot_general(a, b, (dims, ((), ())), precision=precision, preferred_element_type=F32)


NN = ((1,), (0,))
NT = ((1,), (1,))
TN = ((0,), (0,))


def silu(v):
    return v * (1.0 / (1.0 + jnp.exp(-v)))


def call(kernel, outs, scratch=()):
    return pl.pallas_call(
        kernel,
        out_shape=outs,
        scratch_shapes=list(scratch),
        compiler_params=pltpu.CompilerParams(vmem_limit_bytes=58 << 20),
    )


def spread(values, first, heads, head_width):
    rows = values.shape[0]
    per = LANES // head_width
    lane = lax.broadcasted_iota(jnp.int32, (rows, LANES), 1)
    parts = []
    for group in range(heads // per):
        out = jnp.broadcast_to(values[:, first + group * per : first + group * per + 1], (rows, LANES))
        for i in range(1, per):
            col = first + group * per + i
            out = jnp.where(
                lane < i * head_width, out, jnp.broadcast_to(values[:, col : col + 1], (rows, LANES))
            )
        parts.append(out)
    return jnp.concatenate(parts, axis=1)


def columns_of(transposed, eye):
    return mm(eye, transposed, NT, HIGH)


def stack_blocks(values, blocks):
    return jnp.concatenate([values[:, j * SPAN : (j + 1) * SPAN] for j in range(blocks)], axis=0)


def three_rows(total, rows):
    hi = total.astype(BF16).astype(F32)
    mid = (total - hi).astype(BF16).astype(F32)
    low = total - hi - mid
    pick = lax.broadcasted_iota(jnp.int32, (rows, total.shape[1]), 0)
    return jnp.where(pick == 0, hi, jnp.where(pick == 1, mid, jnp.where(pick == 2, low, 0.0)))


def mixer_state(x_inner, bc_input, rim, conv_weight, bc_weight, step_t, decay_t):
    rows, channels = x_inner.shape
    heads = step_t.shape[0]
    state_size = bc_input.shape[1] // 2
    width = channels + 2 * state_size
    head_width = channels // heads
    blocks = rows // SPAN
    kernel_len = conv_weight.shape[0]

    def kernel(x_ref, bc_ref, rim_ref, wx_ref, wb_ref, step_ref, ld_ref, conv_ref, in_ref, send_ref, pad_ref):
        row_i = lax.broadcasted_iota(jnp.int32, (SPAN, SPAN), 0)
        col_i = lax.broadcasted_iota(jnp.int32, (SPAN, SPAN), 1)
        later = jnp.where(row_i < col_i, 1.0, 0.0).astype(F32)
        eye = jnp.where(row_i == col_i, 1.0, 0.0).astype(F32)
        ones = jnp.ones((8, SPAN), F32)
        ld = stack_blocks(ld_ref[...], blocks)
        left = jnp.exp(jnp.minimum(mm(later, ld, NT, HIGH), 0.0))
        tails = left * columns_of(stack_blocks(step_ref[...], blocks), eye)
        lasts = mm(ones, ld, NT, HIGH)
        decays = jnp.exp(jnp.minimum(lasts, 0.0))
        weight = jnp.concatenate([wx_ref[...], wb_ref[...]], axis=1)
        held = None
        total = None
        pad_ref[0:8, :] = rim_ref[...].astype(F32)
        for j in range(blocks):
            at = j * SPAN
            pad_ref[8 + at : 8 + at + SPAN, :channels] = x_ref[at : at + SPAN, :].astype(F32)
            pad_ref[8 + at : 8 + at + SPAN, channels:] = bc_ref[at : at + SPAN, :].astype(F32)
            summed = None
            for k in range(kernel_len):
                begin = at + 8 - kernel_len + 1 + k
                term = weight[k : k + 1, :] * pad_ref[begin : begin + SPAN, :]
                summed = term if summed is None else summed + term
            conv = silu(summed).astype(BF16)
            conv_ref[at : at + SPAN, :] = conv
            x_t = (conv[:, :channels].astype(F32) * spread(tails, j * heads, heads, head_width)).astype(BF16)
            state = mm(conv[:, channels : channels + state_size], x_t, TN)
            if j == 0:
                in_ref[at : at + SPAN, :] = jnp.zeros((state_size, channels), BF16)
                held = state
                total = lasts[:, :heads]
            else:
                in_ref[at : at + SPAN, :] = held.astype(BF16)
                held = spread(decays, j * heads, heads, head_width)[0:1, :] * held + state
                total = total + lasts[:, j * heads : (j + 1) * heads]
        send_ref[:state_size, :] = held.astype(BF16)
        extra = three_rows(spread(total, 0, heads, head_width)[0:1, :], 16)
        send_ref[state_size:, :] = extra.astype(BF16)

    return call(
        kernel,
        (
            jax.ShapeDtypeStruct((rows, width), BF16),
            jax.ShapeDtypeStruct((blocks * state_size, channels), BF16),
            jax.ShapeDtypeStruct((state_size + 16, channels), BF16),
        ),
        (pltpu.VMEM((rows + 8, width), F32),),
    )(x_inner, bc_input, rim, conv_weight, bc_weight, step_t, decay_t)


def mixer_rows(conv, entering, step_t, decay_t, skip_gain, channels):
    rows = conv.shape[0]
    heads = step_t.shape[0]
    state_size = (conv.shape[1] - channels) // 2
    head_width = channels // heads
    blocks = rows // SPAN

    def kernel(skip_ref, conv_ref, in_ref, step_ref, ld_ref, y_ref, e_ref):
        row_i = lax.broadcasted_iota(jnp.int32, (SPAN, SPAN), 0)
        col_i = lax.broadcasted_iota(jnp.int32, (SPAN, SPAN), 1)
        causal = row_i >= col_i
        lower = jnp.where(causal, 1.0, 0.0).astype(F32)
        upper = jnp.where(row_i <= col_i, 1.0, 0.0).astype(F32)
        lane = lax.broadcasted_iota(jnp.int32, (SPAN, LANES), 1)
        lane_row = lax.broadcasted_iota(jnp.int32, (1, LANES), 1)
        per = LANES // head_width
        skip = []
        for group in range(channels // LANES):
            out = jnp.full((1, LANES), skip_ref[group * per], F32)
            for i in range(1, per):
                out = jnp.where(lane_row < i * head_width, out, skip_ref[group * per + i])
            skip.append(out)
        skip = jnp.concatenate(skip, axis=1)
        ld = stack_blocks(ld_ref[...], blocks)
        ld = jnp.concatenate([ld, jnp.zeros((SPAN - blocks * heads, SPAN), F32)], axis=0)
        cum = mm(lower, ld, NT, HIGH)
        cum_t = mm(ld, upper, NN, HIGH)
        group_lane = lax.broadcasted_iota(jnp.int32, (SPAN, SPAN), 1)
        earlier = jnp.zeros((SPAN, SPAN), F32)
        total = jnp.zeros((1, heads), F32)
        for j in range(blocks):
            for h in range(heads):
                earlier = jnp.where(group_lane == j * heads + h, total[:, h : h + 1], earlier)
            total = total + cum[SPAN - 1 : SPAN, j * heads : (j + 1) * heads]
        e_ref[...] = jnp.exp(jnp.minimum(earlier + cum, 0.0))
        e_cum = jnp.exp(jnp.minimum(cum, 0.0))
        for j in range(blocks):
            at = j * SPAN
            x_b = conv_ref[at : at + SPAN, :channels]
            b_b = conv_ref[at : at + SPAN, channels : channels + state_size]
            c_b = conv_ref[at : at + SPAN, channels + state_size :]
            scores = mm(c_b, b_b, NT)
            within = []
            for group in range(channels // LANES):
                x_g = x_b[:, group * LANES : (group + 1) * LANES]
                out = None
                for i in range(per):
                    h = group * per + i
                    r = j * heads + h
                    gap = cum[:, r : r + 1] - cum_t[r : r + 1, :]
                    w = jnp.exp(jnp.where(causal, gap, -1e30)) * scores * step_ref[h : h + 1, at : at + SPAN]
                    y_h = mm(w.astype(BF16), x_g, NN)
                    out = y_h if out is None else jnp.where(lane < i * head_width, out, y_h)
                within.append(out)
            within = jnp.concatenate(within, axis=1)
            y = within + skip * x_b.astype(F32)
            if j > 0:
                y = y + mm(c_b, in_ref[at : at + SPAN, :], NN) * spread(e_cum, j * heads, heads, head_width)
            y_ref[at : at + SPAN, :] = y

    vmem = pl.BlockSpec(memory_space=pltpu.VMEM)
    return pl.pallas_call(
        kernel,
        out_shape=(
            jax.ShapeDtypeStruct((rows, channels), F32),
            jax.ShapeDtypeStruct((SPAN, SPAN), F32),
        ),
        in_specs=[pl.BlockSpec(memory_space=pltpu.SMEM)] + [vmem] * 4,
        out_specs=(vmem, vmem),
        compiler_params=pltpu.CompilerParams(vmem_limit_bytes=58 << 20),
    )(skip_gain, conv, entering, step_t, decay_t)


def total_of(ref, state_size):
    rows = ref[state_size:, :].astype(F32)
    return rows[0:1] + rows[1:2] + rows[2:3]


def join_states(parts, state_size, last):
    channels = parts[0].shape[1]

    def kernel(*refs):
        ins, o_ref = refs[:-1], refs[-1]
        out = ins[0][:state_size, :].astype(F32)
        total = total_of(ins[0], state_size)
        for ref in ins[1:]:
            out = out + jnp.exp(jnp.minimum(total, 0.0)) * ref[:state_size, :].astype(F32)
            total = total + total_of(ref, state_size)
        o_ref[:state_size, :] = out.astype(BF16)
        if not last:
            o_ref[state_size:, :] = three_rows(total, 16).astype(BF16)

    height = state_size if last else state_size + 16
    return call(kernel, jax.ShapeDtypeStruct((height, channels), BF16))(*parts)


def gate_rows(y_at, y_local, conv, e_cols, arriving, gate_input, heads, x_count, y_count):
    rows, channels = y_local.shape
    blocks = rows // SPAN
    head_width = channels // heads
    state_size = arriving.shape[0]
    own = rows // (x_count * y_count)

    def kernel(at_ref, y_ref, c_ref, e_ref, a_ref, g_ref, *refs):
        outs, s_ref = refs[:-1], refs[-1]
        state = a_ref[...]
        for j in range(blocks):
            at = j * SPAN
            carried = mm(c_ref[at : at + SPAN, channels + state_size :], state, NN) * spread(
                e_ref[...], j * heads, heads, head_width
            )
            gated = (y_ref[at : at + SPAN, :] + carried) * silu(g_ref[at : at + SPAN, :].astype(F32))
            s_ref[at : at + SPAN, :] = gated.astype(BF16)
        for k in range(y_count):
            y = lax.rem(at_ref[0] + k, y_count)
            for x in range(x_count):
                first = pl.multiple_of((x * y_count + y) * own, own)
                outs[k][x * own : (x + 1) * own, :] = s_ref[pl.ds(first, own), :]

    vmem = pl.BlockSpec(memory_space=pltpu.VMEM)
    shape = jax.ShapeDtypeStruct((x_count * own, channels), BF16)
    return pl.pallas_call(
        kernel,
        out_shape=(shape,) * y_count,
        in_specs=[pl.BlockSpec(memory_space=pltpu.SMEM)] + [vmem] * 5,
        out_specs=(vmem,) * y_count,
        scratch_shapes=[pltpu.VMEM((rows, channels), BF16)],
        compiler_params=pltpu.CompilerParams(vmem_limit_bytes=58 << 20),
    )(y_at, y_local, conv, e_cols, arriving, gate_input)


def project(x_at, gated, weights, x_count):
    rows, _ = gated[0].shape
    out_width = weights[0][0].shape[1]
    own = rows // x_count
    count = len(gated)
    sizes = [len(w) for w in weights]

    def kernel(at_ref, *refs):
        g_refs = refs[:count]
        w_refs = refs[count : count + sum(sizes)]
        outs, s_ref = refs[count + sum(sizes) : -1], refs[-1]
        squares = jnp.zeros((rows, 1), F32)
        for g_ref in g_refs:
            part = g_ref[...].astype(F32)
            squares = squares + jnp.sum(part * part, axis=1, keepdims=True)
        lhs = jnp.concatenate([g_ref[...] for g_ref in g_refs], axis=1)
        size = 512
        for first in range(0, out_width, size):
            rhs = jnp.concatenate([w_ref[:, first : first + size] for w_ref in w_refs], axis=0)
            s_ref[:, first : first + size] = mm(lhs, rhs, NN).astype(BF16)
        hi = squares.astype(BF16).astype(F32)
        mid = (squares - hi).astype(BF16).astype(F32)
        low = squares - hi - mid
        lane = lax.broadcasted_iota(jnp.int32, (rows, LANES), 1)
        extra = jnp.where(lane == 0, hi, jnp.where(lane == 1, mid, jnp.where(lane == 2, low, 0.0)))
        s_ref[:, out_width:] = extra.astype(BF16)
        for k in range(x_count):
            first = pl.multiple_of(lax.rem(at_ref[0] + k, x_count) * own, own)
            outs[k][...] = s_ref[pl.ds(first, own), :]

    flat = [w for group in weights for w in group]
    vmem = pl.BlockSpec(memory_space=pltpu.VMEM)
    shape = jax.ShapeDtypeStruct((own, out_width + LANES), BF16)
    return pl.pallas_call(
        kernel,
        out_shape=(shape,) * x_count,
        in_specs=[pl.BlockSpec(memory_space=pltpu.SMEM)] + [vmem] * (count + len(flat)),
        out_specs=(vmem,) * x_count,
        scratch_shapes=[pltpu.VMEM((rows, out_width + LANES), BF16)],
        compiler_params=pltpu.CompilerParams(vmem_limit_bytes=58 << 20),
    )(x_at, *gated, *flat)


def expert_of(row, expert_total, owners, local_count):
    main = 8 * expert_total
    dest = jnp.where(row < main, row >> 3, row - main)
    slot = jnp.where(row < main, row & 7, 8)
    core = dest // owners
    return local_count * (dest - core * owners) + core, slot


def put_tiles(ref, value, dests, columns):
    height = ref.shape[0] // dests
    count = height // CAP
    main = 8 * dests
    wide = ref.reshape(dests, height, LANES)
    for i, c in enumerate(columns):
        part = value[:, i * LANES : (i + 1) * LANES]
        start = 8 * c if isinstance(c, int) else pl.multiple_of(8 * c, 8)
        wide[:, pl.ds(start, 8), :] = part[:main].reshape(dests, 8, LANES)
        ref[pl.ds(8 * count + c, dests, stride=height), :] = part[main:]


def take_tile(ref, dests, c):
    height = ref.shape[0] // dests
    count = height // CAP
    start = 8 * c if isinstance(c, int) else pl.multiple_of(8 * c, 8)
    wide = ref.reshape(dests, height, LANES)
    main = wide[:, pl.ds(start, 8), :].reshape(8 * dests, LANES)
    return jnp.concatenate([main, ref[pl.ds(8 * count + c, dests, stride=height), :]], axis=0)


def id_columns(ids_t):
    tokens = ids_t.shape[1]
    eye = jnp.where(
        lax.broadcasted_iota(jnp.int32, (tokens, tokens), 0) == lax.broadcasted_iota(jnp.int32, (tokens, tokens), 1),
        1.0,
        0.0,
    )
    return columns_of(ids_t.astype(F32), eye), eye


def routing_rows(ids_t, expert_total, owners, local_count):
    top, tokens = ids_t.shape
    ids = (id_columns(ids_t)[0] + 0.5).astype(jnp.int32)
    slots = expert_total * CAP
    member = jnp.zeros((tokens, expert_total), F32)
    for k in range(top):
        lane = lax.broadcasted_iota(jnp.int32, (tokens, expert_total), 1)
        member = member + jnp.where(lane == ids[:, k : k + 1], 1.0, 0.0)
    member = member.astype(BF16)
    earlier = lax.broadcasted_iota(jnp.int32, (tokens, tokens), 0) > lax.broadcasted_iota(
        jnp.int32, (tokens, tokens), 1
    )
    rank = mm(jnp.where(earlier, 1.0, 0.0).astype(BF16), member, NN)
    row = lax.broadcasted_iota(jnp.int32, (slots, expert_total), 0)
    expert, _ = expert_of(row, expert_total, owners, local_count)
    spreading = jnp.where(
        expert == lax.broadcasted_iota(jnp.int32, (slots, expert_total), 1), 1.0, 0.0
    ).astype(BF16)
    hit = mm(spreading, member, NT)
    rank_of = mm(spreading, rank.astype(BF16), NT)
    _, slot = expert_of(
        lax.broadcasted_iota(jnp.int32, (slots, tokens), 0), expert_total, owners, local_count
    )
    return jnp.where(rank_of == slot.astype(F32), hit, 0.0).astype(BF16)


def slot_masks(ids_t, expert_total, owners, local_count):
    top, tokens = ids_t.shape
    ids = (id_columns(ids_t)[0] + 0.5).astype(jnp.int32)
    slots = expert_total * CAP
    lane = lax.broadcasted_iota(jnp.int32, (tokens, expert_total), 1)
    member = jnp.zeros((tokens, expert_total), F32)
    for k in range(top):
        member = member + jnp.where(lane == ids[:, k : k + 1], 1.0, 0.0)
    member = member.astype(BF16)
    earlier = lax.broadcasted_iota(jnp.int32, (tokens, tokens), 0) > lax.broadcasted_iota(
        jnp.int32, (tokens, tokens), 1
    )
    rank = mm(jnp.where(earlier, 1.0, 0.0).astype(BF16), member, NN)
    row = lax.broadcasted_iota(jnp.int32, (expert_total, slots), 1)
    expert, _ = expert_of(row, expert_total, owners, local_count)
    spreading = jnp.where(
        expert == lax.broadcasted_iota(jnp.int32, (expert_total, slots), 0), 1.0, 0.0
    ).astype(BF16)
    rank_of = mm(rank.astype(BF16), spreading, NN)
    expert, slot = expert_of(
        lax.broadcasted_iota(jnp.int32, (tokens, slots), 1), expert_total, owners, local_count
    )
    fits = rank_of == slot.astype(F32)
    return [fits & (expert == ids[:, k : k + 1]) for k in range(top)]


def dispatch_grads(ids, out_grad, expert_total, owners, local_count):
    _, width = out_grad.shape
    slots = expert_total * CAP
    count = width // LANES
    each = CAP * count

    def kernel(i_ref, g_ref, o_hbm, s_ref, b_ref, sem):
        pick = routing_rows(i_ref[...], expert_total, owners, local_count)
        put_tiles(s_ref, mm(pick, g_ref[...], NN), expert_total, range(count))
        b_ref[...] = s_ref[...].astype(BF16).reshape(expert_total, each, LANES)
        copy = pltpu.make_async_copy(b_ref, o_hbm.at[:, pl.ds(each, each), :], sem.at[0])
        copy.start()
        copy.wait()

    vmem = pl.BlockSpec(memory_space=pltpu.VMEM)
    return pl.pallas_call(
        kernel,
        out_shape=jax.ShapeDtypeStruct((expert_total, 2 * each, LANES), BF16),
        in_specs=[vmem, vmem],
        out_specs=pl.BlockSpec(memory_space=pl.ANY),
        scratch_shapes=[
            pltpu.VMEM((slots * count, LANES), F32),
            pltpu.VMEM((expert_total, each, LANES), BF16),
            pltpu.SemaphoreType.DMA((1,)),
        ],
        compiler_params=pltpu.CompilerParams(vmem_limit_bytes=58 << 20),
    )(ids, out_grad)


def normalise(buffer, parts, residual, moe_gain, ids, inner_total, expert_total, owners, local_count):
    tokens, width = residual.shape
    slots = expert_total * CAP
    count = width // LANES
    sources = len(parts)

    each = CAP * count

    def kernel(*refs):
        r_ref, m_ref, i_ref, _, o_hbm, h_ref, v_ref, s_ref, b_ref, sem = refs[sources:]
        summed = refs[0][...].astype(F32)
        for p_ref in refs[1:sources]:
            summed = summed + p_ref[...].astype(F32)
        squares = summed[:, width : width + 1] + summed[:, width + 1 : width + 2] + summed[:, width + 2 : width + 3]
        hidden = r_ref[...].astype(F32) + summed[:, :width] * lax.rsqrt(squares / inner_total + 1e-05)
        hidden = hidden.astype(BF16)
        h_ref[...] = hidden
        hidden = hidden.astype(F32)
        inv = lax.rsqrt(jnp.mean(hidden * hidden, axis=1, keepdims=True) + 1e-06)
        v_ref[...] = jnp.broadcast_to(inv, (tokens, LANES))
        normed = (hidden * inv * m_ref[...]).astype(BF16)
        pick = routing_rows(i_ref[...], expert_total, owners, local_count)
        put_tiles(s_ref, mm(pick, normed, NN), expert_total, range(count))
        b_ref[...] = s_ref[...].astype(BF16).reshape(expert_total, each, LANES)
        copy = pltpu.make_async_copy(b_ref, o_hbm.at[:, pl.ds(0, each), :], sem.at[0])
        copy.start()
        copy.wait()

    vmem = pl.BlockSpec(memory_space=pltpu.VMEM)
    anywhere = pl.BlockSpec(memory_space=pl.ANY)
    return pl.pallas_call(
        kernel,
        out_shape=(
            jax.ShapeDtypeStruct(buffer.shape, BF16),
            jax.ShapeDtypeStruct((tokens, width), BF16),
            jax.ShapeDtypeStruct((tokens, LANES), F32),
        ),
        in_specs=[vmem] * (sources + 3) + [anywhere],
        out_specs=(anywhere, vmem, vmem),
        scratch_shapes=[
            pltpu.VMEM((slots * count, LANES), F32),
            pltpu.VMEM((expert_total, each, LANES), BF16),
            pltpu.SemaphoreType.DMA((1,)),
        ],
        input_output_aliases={sources + 3: 0},
        compiler_params=pltpu.CompilerParams(vmem_limit_bytes=58 << 20),
    )(*parts, residual, moe_gain, ids, buffer)


def pack_weights(core, gate_up, down):
    _, d_local, ff_both = gate_up.shape
    ff_width = down.shape[1]
    tiles = ff_both // LANES
    height = tiles * d_local + ff_width

    def kernel(core_ref, g_ref, d_ref, keep_ref, send_ref):
        for out_ref, e in ((keep_ref, core_ref[0]), (send_ref, 1 - core_ref[0])):
            for i in range(tiles):
                out_ref[i * d_local : (i + 1) * d_local, :] = g_ref[e, :, i * LANES : (i + 1) * LANES]
            out_ref[tiles * d_local :, :] = d_ref[e]

    vmem = pl.BlockSpec(memory_space=pltpu.VMEM)
    shape = jax.ShapeDtypeStruct((height, LANES), BF16)
    return pl.pallas_call(
        kernel,
        out_shape=(shape, shape),
        in_specs=[pl.BlockSpec(memory_space=pltpu.SMEM), vmem, vmem],
        out_specs=(vmem, vmem),
        compiler_params=pltpu.CompilerParams(vmem_limit_bytes=58 << 20),
    )(core, gate_up, down)


def experts(core, rows_in, weights, ff_width, gu_rows):
    z_count, cores, _, _ = weights.shape
    count = z_count * cores
    dests = rows_in.shape[0]
    slots = dests * CAP
    ff_tiles = 2 * ff_width // LANES
    block = gu_rows // ff_tiles
    each = CAP * count

    def kernel(core_ref, x_ref, w_hbm, o_ref, x_s, g_s, xb_s, gb_s, w_ref, sems):
        copies = [pltpu.make_async_copy(w_hbm.at[z], w_ref.at[z], sems.at[z]) for z in range(z_count)]
        for copy in copies:
            copy.start()
        core = core_ref[0]
        x_s[...] = x_ref[:, :each, :].astype(F32).reshape(dests * each, LANES)
        g_s[...] = x_ref[:, each:, :].astype(F32).reshape(dests * each, LANES)
        order = [(z, s, z * cores + (core if s == 0 else 1 - core)) for z in range(z_count) for s in range(cores)]
        for i, (z, s, c) in enumerate(order):
            xb_s[:, i * LANES : (i + 1) * LANES] = take_tile(x_s, dests, c).astype(BF16)
            gb_s[:, i * LANES : (i + 1) * LANES] = take_tile(g_s, dests, c).astype(BF16)

        def tile(z, s, i):
            return w_ref[z, s, i * block : (i + 1) * block, :]

        for copy in copies:
            copy.wait()
        projected = []
        for first in range(0, ff_tiles, 2):
            used = range(first, min(first + 2, ff_tiles))
            rhs = jnp.concatenate(
                [jnp.concatenate([tile(z, s, i) for i in used], axis=1) for z, s, _ in order], axis=0
            )
            projected.append(mm(xb_s[...], rhs, NN))
        projected = jnp.concatenate(projected, axis=1)
        hidden_grad = []
        for first in range(0, ff_width, 256):
            size = min(256, ff_width - first)
            rhs = jnp.concatenate(
                [w_ref[z, s, gu_rows + first : gu_rows + first + size, :] for z, s, _ in order], axis=1
            )
            hidden_grad.append(mm(gb_s[...], rhs, NT))
        hidden_grad = jnp.concatenate(hidden_grad, axis=1)
        pre_gate = projected[:, :ff_width]
        pre_up = projected[:, ff_width:]
        sig = 1.0 / (1.0 + jnp.exp(-pre_gate))
        act = pre_gate * sig
        activated = (act * pre_up).astype(BF16)
        grad_gate = hidden_grad * pre_up * sig * (1.0 + pre_gate * (1.0 - sig))
        grad_up = hidden_grad * act
        grad_both = jnp.concatenate([grad_gate, grad_up], axis=1).astype(BF16)
        for z in range(z_count):
            rhs = jnp.concatenate([w_ref[z, s, gu_rows:, :] for s in range(cores)], axis=1)
            out = mm(activated, rhs, NN)
            rhs = jnp.concatenate(
                [jnp.concatenate([tile(z, s, i) for i in range(ff_tiles)], axis=1) for s in range(cores)], axis=0
            )
            grad = mm(grad_both, rhs, NT)
            places = [z * cores + core, z * cores + 1 - core]
            put_tiles(x_s, out, dests, places)
            put_tiles(g_s, grad, dests, places)
        o_ref[:, :each, :] = x_s[...].astype(BF16).reshape(dests, each, LANES)
        o_ref[:, each:, :] = g_s[...].astype(BF16).reshape(dests, each, LANES)

    vmem = pl.BlockSpec(memory_space=pltpu.VMEM)
    return pl.pallas_call(
        kernel,
        out_shape=jax.ShapeDtypeStruct((dests, 2 * each, LANES), BF16),
        in_specs=[pl.BlockSpec(memory_space=pltpu.SMEM), vmem, pl.BlockSpec(memory_space=pl.ANY)],
        out_specs=vmem,
        scratch_shapes=[
            pltpu.VMEM((dests * each, LANES), F32),
            pltpu.VMEM((dests * each, LANES), F32),
            pltpu.VMEM((slots, count * LANES), BF16),
            pltpu.VMEM((slots, count * LANES), BF16),
            pltpu.VMEM(weights.shape, BF16),
            pltpu.SemaphoreType.DMA((z_count,)),
        ],
        compiler_params=pltpu.CompilerParams(vmem_limit_bytes=58 << 20),
    )(core, rows_in, weights)


def combine(back, hidden, inv_rms, out_grad, moe_gain, ids_t, route_t, expert_total, owners, local_count):
    tokens, width = hidden.shape
    top = ids_t.shape[0]
    count = width // LANES
    slots = expert_total * CAP
    each = CAP * count

    def kernel(r_ref, h_ref, v_ref, g_ref, m_ref, i_ref, w_ref, layer_ref, res_ref, route_ref, o_s, b_s):
        o_s[...] = r_ref[:, :each, :].astype(F32).reshape(slots * count, LANES)
        b_s[...] = r_ref[:, each:, :].astype(F32).reshape(slots * count, LANES)
        masks = slot_masks(i_ref[...], expert_total, owners, local_count)
        eye = id_columns(i_ref[...])[1]
        routes = columns_of(w_ref[...], eye)
        weight = jnp.zeros((tokens, slots), F32)
        for k in range(top):
            weight = weight + jnp.where(masks[k], routes[:, k : k + 1], 0.0)
        hi = weight.astype(BF16)
        both = jnp.concatenate([hi, (weight - hi.astype(F32)).astype(BF16)], axis=0)

        def rows_of(ref):
            return jnp.concatenate(
                [take_tile(ref, expert_total, i).astype(BF16) for i in range(count)], axis=1
            )

        hidden = h_ref[...].astype(F32)
        grad = g_ref[...]
        outs = rows_of(o_s)
        mixed = mm(both, outs, NN)
        layer_ref[...] = (hidden + (mixed[:tokens] + mixed[tokens:])).astype(BF16)
        dots = mm(grad, outs, NT)
        lane = lax.broadcasted_iota(jnp.int32, (tokens, top), 1)
        route = jnp.zeros((tokens, top), F32)
        for k in range(top):
            one = jnp.sum(jnp.where(masks[k], dots, 0.0), axis=1, keepdims=True)
            route = jnp.where(lane == k, one, route)
        route_ref[...] = mm(route, eye, TN, HIGH)
        mixed = mm(both, rows_of(b_s), NN)
        inv = v_ref[:, 0:1]
        unit_grad = (mixed[:tokens] + mixed[tokens:]) * m_ref[...]
        unit_rows = hidden * inv
        mean = jnp.mean(unit_grad * unit_rows, axis=1, keepdims=True)
        res_ref[...] = (grad.astype(F32) + inv * (unit_grad - unit_rows * mean)).astype(BF16)

    shape = jax.ShapeDtypeStruct((tokens, width), BF16)
    return call(
        kernel,
        (shape, shape, jax.ShapeDtypeStruct((top, tokens), F32)),
        (pltpu.VMEM((slots * count, LANES), F32), pltpu.VMEM((slots * count, LANES), F32)),
    )(back, hidden, inv_rms, out_grad, moe_gain, ids_t, route_t)


def ring_route(count, shift):
    return [(i, (i + shift) % count) for i in range(count)]


def local(
    x_inner,
    bc_input,
    gate_input,
    conv_weight,
    bc_conv_weight,
    step_size,
    log_decay,
    skip_gain,
    norm_gain,
    out_weight,
    residual,
    moe_gain,
    expert_ids,
    route_weights,
    gate_up_weight,
    down_weight,
    out_grad,
):
    ctx = ("z", "core")
    ctx_count = lax.axis_size("z") * lax.axis_size("core")
    x_count, y_count = lax.axis_size("x"), lax.axis_size("y")
    owners = x_count * y_count
    heads = step_size.shape[1]
    channels = x_inner.shape[1]
    state_size = bc_input.shape[1] // 2
    local_count, _, _ = gate_up_weight.shape
    ff_width = down_weight.shape[1]
    expert_total = local_count * owners
    exchange = ("core", "x", "y")

    ids_t, route_t = expert_ids.T, route_weights.T
    step_t, decay_t = step_size.T, log_decay.T
    core = lax.axis_index("core").astype(jnp.int32).reshape(1)

    last = jnp.concatenate([x_inner[-8:], bc_input[-8:]], axis=1)
    rim = lax.ppermute(last, ctx, [(i, i + 1) for i in range(ctx_count - 1)])

    folded = (out_weight.astype(F32) * norm_gain[:, None]).astype(BF16)
    half = folded.shape[0] // 2
    from_prev = lax.ppermute(folded, "y", ring_route(y_count, 1))
    from_next = lax.ppermute(folded, "y", ring_route(y_count, -1))
    far_a = lax.ppermute(from_prev[:half], "y", ring_route(y_count, 1))
    far_b = lax.ppermute(from_next[half:], "y", ring_route(y_count, -1))

    kept, other = pack_weights(core, gate_up_weight, down_weight)
    swapped = lax.ppermute(other, "core", [(0, 1), (1, 0)])

    conv, held_in, sent = mixer_state(x_inner, bc_input, rim, conv_weight, bc_conv_weight, step_t, decay_t)
    reach = 4

    def earlier(value, distance):
        return lax.ppermute(value, ctx, [(i, i + distance) for i in range(ctx_count - distance)])

    near = [earlier(sent, d) for d in range(1, reach + 1)]
    kept, swapped, conv = lax.optimization_barrier((kept, swapped, conv))
    stacked = jnp.stack([kept, swapped])
    weights = lax.all_gather(stacked, "z", axis=0, tiled=False)
    gu_rows = kept.shape[0] - ff_width
    y_local, e_cols = mixer_rows(conv, held_in, step_t, decay_t, skip_gain, channels)
    window = join_states(near, state_size, False)
    windows = [window] + [earlier(window, d) for d in range(reach, ctx_count, reach)]

    buffer = dispatch_grads(ids_t, out_grad, expert_total, owners, local_count)
    arriving = join_states(windows, state_size, True)
    y_at = lax.axis_index("y").astype(jnp.int32).reshape(1)
    x_at = lax.axis_index("x").astype(jnp.int32).reshape(1)
    gated = gate_rows(y_at, y_local, conv, e_cols, arriving, gate_input, heads, x_count, y_count)
    gated = [gated[0]] + [
        lax.ppermute(gated[k], "y", ring_route(y_count, k)) for k in range(1, y_count)
    ]
    pieces = [(folded,), (from_prev,), (far_a, far_b), (from_next,)]
    parts = project(x_at, gated, pieces, x_count)
    parts = [parts[0]] + [
        lax.ppermute(parts[k], "x", ring_route(x_count, k)) for k in range(1, x_count)
    ]
    sent_rows, hidden, inv_rms = normalise(
        buffer, parts, residual, moe_gain[None, :], ids_t, channels * owners, expert_total, owners, local_count
    )
    rows_in = lax.all_to_all(sent_rows, exchange, split_axis=0, concat_axis=0, tiled=True)
    back = experts(core, rows_in, weights, ff_width, gu_rows)
    back = lax.all_to_all(back, exchange, split_axis=0, concat_axis=0, tiled=True)
    layer, res, route = combine(
        back, hidden, inv_rms, out_grad, moe_gain[None, :], ids_t, route_t, expert_total, owners, local_count
    )
    return layer, res, route.T


def solution(mesh):
    ctx_count, exp_count = mesh.devices.shape
    side = int(round(exp_count**0.5))
    devices = mesh.devices.reshape(ctx_count // 2, 2, side, exp_count // side)
    fine = Mesh(devices, ("z", "core", "x", "y"))
    ctx, exp = ("z", "core"), ("x", "y")
    token = P(ctx + exp, None)
    return jax.shard_map(
        local,
        mesh=fine,
        in_specs=(
            P(ctx, exp),
            P(ctx, None),
            P(ctx, exp),
            P(None, exp),
            P(),
            P(ctx, exp),
            P(ctx, exp),
            P(exp),
            P(exp),
            P(exp, None),
            token,
            P(),
            token,
            token,
            P(exp, ctx, None),
            P(exp, None, ctx),
            token,
        ),
        out_specs=(token, token, token),
        check_vma=False,
    )
```

```python
import jax
import jax.numpy as jnp
from jax import lax
from jax.experimental import pallas as pl
from jax.experimental.pallas import tpu as pltpu
from jax.sharding import Mesh
from jax.sharding import PartitionSpec as P


F32 = jnp.float32
BF16 = jnp.bfloat16
HIGH = lax.Precision.HIGHEST
SPAN = 128
CAP = 9
LANES = 128


def mm(a, b, dims, precision=None):
    return lax.dot_general(a, b, (dims, ((), ())), precision=precision, preferred_element_type=F32)


NN = ((1,), (0,))
NT = ((1,), (1,))
TN = ((0,), (0,))


def silu(v):
    return v * (1.0 / (1.0 + jnp.exp(-v)))


def call(kernel, outs, scratch=()):
    return pl.pallas_call(
        kernel,
        out_shape=outs,
        scratch_shapes=list(scratch),
        compiler_params=pltpu.CompilerParams(vmem_limit_bytes=58 << 20),
    )


def spread(values, first, heads, head_width):
    rows = values.shape[0]
    per = LANES // head_width
    lane = lax.broadcasted_iota(jnp.int32, (rows, LANES), 1)
    parts = []
    for group in range(heads // per):
        out = jnp.broadcast_to(values[:, first + group * per : first + group * per + 1], (rows, LANES))
        for i in range(1, per):
            col = first + group * per + i
            out = jnp.where(
                lane < i * head_width, out, jnp.broadcast_to(values[:, col : col + 1], (rows, LANES))
            )
        parts.append(out)
    return jnp.concatenate(parts, axis=1)


def columns_of(transposed, eye):
    return mm(eye, transposed, NT, HIGH)


def stack_blocks(values, blocks):
    return jnp.concatenate([values[:, j * SPAN : (j + 1) * SPAN] for j in range(blocks)], axis=0)


def three_rows(total, rows):
    hi = total.astype(BF16).astype(F32)
    mid = (total - hi).astype(BF16).astype(F32)
    low = total - hi - mid
    pick = lax.broadcasted_iota(jnp.int32, (rows, total.shape[1]), 0)
    return jnp.where(pick == 0, hi, jnp.where(pick == 1, mid, jnp.where(pick == 2, low, 0.0)))


def mixer_state(x_inner, bc_input, rim, conv_weight, bc_weight, step_t, decay_t, copies):
    rows, channels = x_inner.shape
    heads = step_t.shape[0]
    state_size = bc_input.shape[1] // 2
    width = channels + 2 * state_size
    head_width = channels // heads
    blocks = rows // SPAN
    kernel_len = conv_weight.shape[0]

    def kernel(x_ref, bc_ref, rim_ref, wx_ref, wb_ref, step_ref, ld_ref, conv_ref, in_ref, send_ref, pad_ref):
        row_i = lax.broadcasted_iota(jnp.int32, (SPAN, SPAN), 0)
        col_i = lax.broadcasted_iota(jnp.int32, (SPAN, SPAN), 1)
        later = jnp.where(row_i < col_i, 1.0, 0.0).astype(F32)
        eye = jnp.where(row_i == col_i, 1.0, 0.0).astype(F32)
        ones = jnp.ones((8, SPAN), F32)
        ld = stack_blocks(ld_ref[...], blocks)
        left = jnp.exp(jnp.minimum(mm(later, ld, NT, HIGH), 0.0))
        tails = left * columns_of(stack_blocks(step_ref[...], blocks), eye)
        lasts = mm(ones, ld, NT, HIGH)
        decays = jnp.exp(jnp.minimum(lasts, 0.0))
        weight = jnp.concatenate([wx_ref[...], wb_ref[...]], axis=1)
        held = None
        total = None
        pad_ref[0:8, :] = rim_ref[...].astype(F32)
        for j in range(blocks):
            at = j * SPAN
            pad_ref[8 + at : 8 + at + SPAN, :channels] = x_ref[at : at + SPAN, :].astype(F32)
            pad_ref[8 + at : 8 + at + SPAN, channels:] = bc_ref[at : at + SPAN, :].astype(F32)
            summed = None
            for k in range(kernel_len):
                begin = at + 8 - kernel_len + 1 + k
                term = weight[k : k + 1, :] * pad_ref[begin : begin + SPAN, :]
                summed = term if summed is None else summed + term
            conv = silu(summed).astype(BF16)
            conv_ref[at : at + SPAN, :] = conv
            x_t = (conv[:, :channels].astype(F32) * spread(tails, j * heads, heads, head_width)).astype(BF16)
            state = mm(conv[:, channels : channels + state_size], x_t, TN)
            if j == 0:
                in_ref[at : at + SPAN, :] = jnp.zeros((state_size, channels), BF16)
                held = state
                total = lasts[:, :heads]
            else:
                in_ref[at : at + SPAN, :] = held.astype(BF16)
                held = spread(decays, j * heads, heads, head_width)[0:1, :] * held + state
                total = total + lasts[:, j * heads : (j + 1) * heads]
        state = held.astype(BF16)
        extra = three_rows(spread(total, 0, heads, head_width)[0:1, :], 16).astype(BF16)
        for i in range(copies):
            send_ref[i, :state_size, :] = state
            send_ref[i, state_size:, :] = extra

    return call(
        kernel,
        (
            jax.ShapeDtypeStruct((rows, width), BF16),
            jax.ShapeDtypeStruct((blocks * state_size, channels), BF16),
            jax.ShapeDtypeStruct((copies, state_size + 16, channels), BF16),
        ),
        (pltpu.VMEM((rows + 8, width), F32),),
    )(x_inner, bc_input, rim, conv_weight, bc_weight, step_t, decay_t)


def mixer_rows(conv, entering, step_t, decay_t, skip_gain, channels):
    rows = conv.shape[0]
    heads = step_t.shape[0]
    state_size = (conv.shape[1] - channels) // 2
    head_width = channels // heads
    blocks = rows // SPAN

    def kernel(skip_ref, conv_ref, in_ref, step_ref, ld_ref, y_ref, e_ref):
        row_i = lax.broadcasted_iota(jnp.int32, (SPAN, SPAN), 0)
        col_i = lax.broadcasted_iota(jnp.int32, (SPAN, SPAN), 1)
        causal = row_i >= col_i
        lower = jnp.where(causal, 1.0, 0.0).astype(F32)
        upper = jnp.where(row_i <= col_i, 1.0, 0.0).astype(F32)
        lane = lax.broadcasted_iota(jnp.int32, (SPAN, LANES), 1)
        lane_row = lax.broadcasted_iota(jnp.int32, (1, LANES), 1)
        per = LANES // head_width
        skip = []
        for group in range(channels // LANES):
            out = jnp.full((1, LANES), skip_ref[group * per], F32)
            for i in range(1, per):
                out = jnp.where(lane_row < i * head_width, out, skip_ref[group * per + i])
            skip.append(out)
        skip = jnp.concatenate(skip, axis=1)
        ld = stack_blocks(ld_ref[...], blocks)
        ld = jnp.concatenate([ld, jnp.zeros((SPAN - blocks * heads, SPAN), F32)], axis=0)
        cum = mm(lower, ld, NT, HIGH)
        cum_t = mm(ld, upper, NN, HIGH)
        group_lane = lax.broadcasted_iota(jnp.int32, (SPAN, SPAN), 1)
        earlier = jnp.zeros((SPAN, SPAN), F32)
        total = jnp.zeros((1, heads), F32)
        for j in range(blocks):
            for h in range(heads):
                earlier = jnp.where(group_lane == j * heads + h, total[:, h : h + 1], earlier)
            total = total + cum[SPAN - 1 : SPAN, j * heads : (j + 1) * heads]
        e_ref[...] = jnp.exp(jnp.minimum(earlier + cum, 0.0))
        e_cum = jnp.exp(jnp.minimum(cum, 0.0))
        for j in range(blocks):
            at = j * SPAN
            x_b = conv_ref[at : at + SPAN, :channels]
            b_b = conv_ref[at : at + SPAN, channels : channels + state_size]
            c_b = conv_ref[at : at + SPAN, channels + state_size :]
            scores = mm(c_b, b_b, NT)
            within = []
            for group in range(channels // LANES):
                x_g = x_b[:, group * LANES : (group + 1) * LANES]
                out = None
                for i in range(per):
                    h = group * per + i
                    r = j * heads + h
                    gap = cum[:, r : r + 1] - cum_t[r : r + 1, :]
                    w = jnp.exp(jnp.where(causal, gap, -1e30)) * scores * step_ref[h : h + 1, at : at + SPAN]
                    y_h = mm(w.astype(BF16), x_g, NN)
                    out = y_h if out is None else jnp.where(lane < i * head_width, out, y_h)
                within.append(out)
            within = jnp.concatenate(within, axis=1)
            y = within + skip * x_b.astype(F32)
            if j > 0:
                y = y + mm(c_b, in_ref[at : at + SPAN, :], NN) * spread(e_cum, j * heads, heads, head_width)
            y_ref[at : at + SPAN, :] = y

    vmem = pl.BlockSpec(memory_space=pltpu.VMEM)
    return pl.pallas_call(
        kernel,
        out_shape=(
            jax.ShapeDtypeStruct((rows, channels), F32),
            jax.ShapeDtypeStruct((SPAN, SPAN), F32),
        ),
        in_specs=[pl.BlockSpec(memory_space=pltpu.SMEM)] + [vmem] * 4,
        out_specs=(vmem, vmem),
        compiler_params=pltpu.CompilerParams(vmem_limit_bytes=58 << 20),
    )(skip_gain, conv, entering, step_t, decay_t)


def total_of(ref, i, state_size):
    rows = ref[i, state_size:, :].astype(F32)
    return rows[0:1] + rows[1:2] + rows[2:3]


def join_near(place, received, state_size, copies):
    count, height, channels = received.shape

    def kernel(at_ref, r_ref, own_ref, log_ref, send_ref):
        whole = jnp.zeros((state_size, channels), F32)
        total = jnp.zeros((1, channels), F32)
        own_ref[...] = whole
        log_ref[...] = jnp.zeros((8, channels), F32)
        for i in range(count):
            log = total_of(r_ref, i, state_size)
            whole = jnp.exp(jnp.minimum(log, 0.0)) * whole + r_ref[i, :state_size, :].astype(F32)
            total = total + log

            @pl.when(at_ref[0] == i + 1)
            def _(whole=whole, total=total):
                own_ref[...] = whole
                log_ref[...] = jnp.broadcast_to(total, (8, channels))

        state = whole.astype(BF16)
        extra = three_rows(total, 16).astype(BF16)
        for i in range(copies):
            send_ref[i, :state_size, :] = state
            send_ref[i, state_size:, :] = extra

    vmem = pl.BlockSpec(memory_space=pltpu.VMEM)
    return pl.pallas_call(
        kernel,
        out_shape=(
            jax.ShapeDtypeStruct((state_size, channels), F32),
            jax.ShapeDtypeStruct((8, channels), F32),
            jax.ShapeDtypeStruct((copies, height, channels), BF16),
        ),
        in_specs=[pl.BlockSpec(memory_space=pltpu.SMEM), vmem],
        out_specs=(vmem, vmem, vmem),
        compiler_params=pltpu.CompilerParams(vmem_limit_bytes=58 << 20),
    )(place, received)


def join_far(place, received, own, log):
    count, _, channels = received.shape
    state_size = own.shape[0]

    def kernel(at_ref, r_ref, own_ref, log_ref, o_ref):
        whole = jnp.zeros((state_size, channels), F32)
        o_ref[...] = own_ref[...].astype(BF16)
        for i in range(count - 1):
            step = jnp.exp(jnp.minimum(total_of(r_ref, i, state_size), 0.0))
            whole = step * whole + r_ref[i, :state_size, :].astype(F32)

            @pl.when(at_ref[0] == i + 1)
            def _(whole=whole):
                o_ref[...] = (jnp.exp(jnp.minimum(log_ref[0:1, :], 0.0)) * whole + own_ref[...]).astype(BF16)

    vmem = pl.BlockSpec(memory_space=pltpu.VMEM)
    return pl.pallas_call(
        kernel,
        out_shape=jax.ShapeDtypeStruct((state_size, channels), BF16),
        in_specs=[pl.BlockSpec(memory_space=pltpu.SMEM), vmem, vmem, vmem],
        out_specs=vmem,
        compiler_params=pltpu.CompilerParams(vmem_limit_bytes=58 << 20),
    )(place, received, own, log)


def gate_rows(y_at, y_local, conv, e_cols, arriving, gate_input, heads, x_count, y_count):
    rows, channels = y_local.shape
    blocks = rows // SPAN
    head_width = channels // heads
    state_size = arriving.shape[0]
    own = rows // (x_count * y_count)

    def kernel(at_ref, y_ref, c_ref, e_ref, a_ref, g_ref, *refs):
        outs, s_ref = refs[:-1], refs[-1]
        state = a_ref[...]
        for j in range(blocks):
            at = j * SPAN
            carried = mm(c_ref[at : at + SPAN, channels + state_size :], state, NN) * spread(
                e_ref[...], j * heads, heads, head_width
            )
            gated = (y_ref[at : at + SPAN, :] + carried) * silu(g_ref[at : at + SPAN, :].astype(F32))
            s_ref[at : at + SPAN, :] = gated.astype(BF16)
        for k in range(y_count):
            y = lax.rem(at_ref[0] + k, y_count)
            for x in range(x_count):
                first = pl.multiple_of((x * y_count + y) * own, own)
                outs[k][x * own : (x + 1) * own, :] = s_ref[pl.ds(first, own), :]

    vmem = pl.BlockSpec(memory_space=pltpu.VMEM)
    shape = jax.ShapeDtypeStruct((x_count * own, channels), BF16)
    return pl.pallas_call(
        kernel,
        out_shape=(shape,) * y_count,
        in_specs=[pl.BlockSpec(memory_space=pltpu.SMEM)] + [vmem] * 5,
        out_specs=(vmem,) * y_count,
        scratch_shapes=[pltpu.VMEM((rows, channels), BF16)],
        compiler_params=pltpu.CompilerParams(vmem_limit_bytes=58 << 20),
    )(y_at, y_local, conv, e_cols, arriving, gate_input)


def project(x_at, gated, weights, x_count):
    rows, _ = gated[0].shape
    out_width = weights[0][0].shape[1]
    own = rows // x_count
    count = len(gated)
    sizes = [len(w) for w in weights]

    def kernel(at_ref, *refs):
        g_refs = refs[:count]
        w_refs = refs[count : count + sum(sizes)]
        outs, s_ref = refs[count + sum(sizes) : -1], refs[-1]
        squares = jnp.zeros((rows, 1), F32)
        for g_ref in g_refs:
            part = g_ref[...].astype(F32)
            squares = squares + jnp.sum(part * part, axis=1, keepdims=True)
        lhs = jnp.concatenate([g_ref[...] for g_ref in g_refs], axis=1)
        size = 512
        for first in range(0, out_width, size):
            rhs = jnp.concatenate([w_ref[:, first : first + size] for w_ref in w_refs], axis=0)
            s_ref[:, first : first + size] = mm(lhs, rhs, NN).astype(BF16)
        hi = squares.astype(BF16).astype(F32)
        mid = (squares - hi).astype(BF16).astype(F32)
        low = squares - hi - mid
        lane = lax.broadcasted_iota(jnp.int32, (rows, LANES), 1)
        extra = jnp.where(lane == 0, hi, jnp.where(lane == 1, mid, jnp.where(lane == 2, low, 0.0)))
        s_ref[:, out_width:] = extra.astype(BF16)
        for k in range(x_count):
            first = pl.multiple_of(lax.rem(at_ref[0] + k, x_count) * own, own)
            outs[k][...] = s_ref[pl.ds(first, own), :]

    flat = [w for group in weights for w in group]
    vmem = pl.BlockSpec(memory_space=pltpu.VMEM)
    shape = jax.ShapeDtypeStruct((own, out_width + LANES), BF16)
    return pl.pallas_call(
        kernel,
        out_shape=(shape,) * x_count,
        in_specs=[pl.BlockSpec(memory_space=pltpu.SMEM)] + [vmem] * (count + len(flat)),
        out_specs=(vmem,) * x_count,
        scratch_shapes=[pltpu.VMEM((rows, out_width + LANES), BF16)],
        compiler_params=pltpu.CompilerParams(vmem_limit_bytes=58 << 20),
    )(x_at, *gated, *flat)


def expert_of(row, expert_total, owners, local_count):
    main = 8 * expert_total
    dest = jnp.where(row < main, row >> 3, row - main)
    slot = jnp.where(row < main, row & 7, 8)
    core = dest // owners
    return local_count * (dest - core * owners) + core, slot


def put_tiles(ref, value, dests, columns):
    height = ref.shape[0] // dests
    count = height // CAP
    main = 8 * dests
    wide = ref.reshape(dests, height, LANES)
    for i, c in enumerate(columns):
        part = value[:, i * LANES : (i + 1) * LANES]
        start = 8 * c if isinstance(c, int) else pl.multiple_of(8 * c, 8)
        wide[:, pl.ds(start, 8), :] = part[:main].reshape(dests, 8, LANES)
        ref[pl.ds(8 * count + c, dests, stride=height), :] = part[main:]


def take_tile(ref, dests, c):
    height = ref.shape[0] // dests
    count = height // CAP
    start = 8 * c if isinstance(c, int) else pl.multiple_of(8 * c, 8)
    wide = ref.reshape(dests, height, LANES)
    main = wide[:, pl.ds(start, 8), :].reshape(8 * dests, LANES)
    return jnp.concatenate([main, ref[pl.ds(8 * count + c, dests, stride=height), :]], axis=0)


def id_columns(ids_t):
    tokens = ids_t.shape[1]
    eye = jnp.where(
        lax.broadcasted_iota(jnp.int32, (tokens, tokens), 0) == lax.broadcasted_iota(jnp.int32, (tokens, tokens), 1),
        1.0,
        0.0,
    )
    return columns_of(ids_t.astype(F32), eye), eye


def routing_rows(ids_t, expert_total, owners, local_count):
    top, tokens = ids_t.shape
    ids = (id_columns(ids_t)[0] + 0.5).astype(jnp.int32)
    slots = expert_total * CAP
    member = jnp.zeros((tokens, expert_total), F32)
    for k in range(top):
        lane = lax.broadcasted_iota(jnp.int32, (tokens, expert_total), 1)
        member = member + jnp.where(lane == ids[:, k : k + 1], 1.0, 0.0)
    member = member.astype(BF16)
    earlier = lax.broadcasted_iota(jnp.int32, (tokens, tokens), 0) > lax.broadcasted_iota(
        jnp.int32, (tokens, tokens), 1
    )
    rank = mm(jnp.where(earlier, 1.0, 0.0).astype(BF16), member, NN)
    row = lax.broadcasted_iota(jnp.int32, (slots, expert_total), 0)
    expert, _ = expert_of(row, expert_total, owners, local_count)
    spreading = jnp.where(
        expert == lax.broadcasted_iota(jnp.int32, (slots, expert_total), 1), 1.0, 0.0
    ).astype(BF16)
    hit = mm(spreading, member, NT)
    rank_of = mm(spreading, rank.astype(BF16), NT)
    _, slot = expert_of(
        lax.broadcasted_iota(jnp.int32, (slots, tokens), 0), expert_total, owners, local_count
    )
    return jnp.where(rank_of == slot.astype(F32), hit, 0.0).astype(BF16)


def slot_masks(ids_t, expert_total, owners, local_count):
    top, tokens = ids_t.shape
    ids = (id_columns(ids_t)[0] + 0.5).astype(jnp.int32)
    slots = expert_total * CAP
    lane = lax.broadcasted_iota(jnp.int32, (tokens, expert_total), 1)
    member = jnp.zeros((tokens, expert_total), F32)
    for k in range(top):
        member = member + jnp.where(lane == ids[:, k : k + 1], 1.0, 0.0)
    member = member.astype(BF16)
    earlier = lax.broadcasted_iota(jnp.int32, (tokens, tokens), 0) > lax.broadcasted_iota(
        jnp.int32, (tokens, tokens), 1
    )
    rank = mm(jnp.where(earlier, 1.0, 0.0).astype(BF16), member, NN)
    row = lax.broadcasted_iota(jnp.int32, (expert_total, slots), 1)
    expert, _ = expert_of(row, expert_total, owners, local_count)
    spreading = jnp.where(
        expert == lax.broadcasted_iota(jnp.int32, (expert_total, slots), 0), 1.0, 0.0
    ).astype(BF16)
    rank_of = mm(rank.astype(BF16), spreading, NN)
    expert, slot = expert_of(
        lax.broadcasted_iota(jnp.int32, (tokens, slots), 1), expert_total, owners, local_count
    )
    fits = rank_of == slot.astype(F32)
    return [fits & (expert == ids[:, k : k + 1]) for k in range(top)]


def dispatch_grads(ids, out_grad, expert_total, owners, local_count):
    _, width = out_grad.shape
    slots = expert_total * CAP
    count = width // LANES
    each = CAP * count

    def kernel(i_ref, g_ref, o_hbm, s_ref, b_ref, sem):
        pick = routing_rows(i_ref[...], expert_total, owners, local_count)
        put_tiles(s_ref, mm(pick, g_ref[...], NN), expert_total, range(count))
        b_ref[...] = s_ref[...].astype(BF16).reshape(expert_total, each, LANES)
        copy = pltpu.make_async_copy(b_ref, o_hbm.at[:, pl.ds(each, each), :], sem.at[0])
        copy.start()
        copy.wait()

    vmem = pl.BlockSpec(memory_space=pltpu.VMEM)
    return pl.pallas_call(
        kernel,
        out_shape=jax.ShapeDtypeStruct((expert_total, 2 * each, LANES), BF16),
        in_specs=[vmem, vmem],
        out_specs=pl.BlockSpec(memory_space=pl.ANY),
        scratch_shapes=[
            pltpu.VMEM((slots * count, LANES), F32),
            pltpu.VMEM((expert_total, each, LANES), BF16),
            pltpu.SemaphoreType.DMA((1,)),
        ],
        compiler_params=pltpu.CompilerParams(vmem_limit_bytes=58 << 20),
    )(ids, out_grad)


def normalise(buffer, parts, residual, moe_gain, ids, inner_total, expert_total, owners, local_count):
    tokens, width = residual.shape
    slots = expert_total * CAP
    count = width // LANES
    sources = len(parts)

    each = CAP * count

    def kernel(*refs):
        r_ref, m_ref, i_ref, _, o_hbm, h_ref, v_ref, s_ref, b_ref, sem = refs[sources:]
        summed = refs[0][...].astype(F32)
        for p_ref in refs[1:sources]:
            summed = summed + p_ref[...].astype(F32)
        squares = summed[:, width : width + 1] + summed[:, width + 1 : width + 2] + summed[:, width + 2 : width + 3]
        hidden = r_ref[...].astype(F32) + summed[:, :width] * lax.rsqrt(squares / inner_total + 1e-05)
        hidden = hidden.astype(BF16)
        h_ref[...] = hidden
        hidden = hidden.astype(F32)
        inv = lax.rsqrt(jnp.mean(hidden * hidden, axis=1, keepdims=True) + 1e-06)
        v_ref[...] = jnp.broadcast_to(inv, (tokens, LANES))
        normed = (hidden * inv * m_ref[...]).astype(BF16)
        pick = routing_rows(i_ref[...], expert_total, owners, local_count)
        put_tiles(s_ref, mm(pick, normed, NN), expert_total, range(count))
        b_ref[...] = s_ref[...].astype(BF16).reshape(expert_total, each, LANES)
        copy = pltpu.make_async_copy(b_ref, o_hbm.at[:, pl.ds(0, each), :], sem.at[0])
        copy.start()
        copy.wait()

    vmem = pl.BlockSpec(memory_space=pltpu.VMEM)
    anywhere = pl.BlockSpec(memory_space=pl.ANY)
    return pl.pallas_call(
        kernel,
        out_shape=(
            jax.ShapeDtypeStruct(buffer.shape, BF16),
            jax.ShapeDtypeStruct((tokens, width), BF16),
            jax.ShapeDtypeStruct((tokens, LANES), F32),
        ),
        in_specs=[vmem] * (sources + 3) + [anywhere],
        out_specs=(anywhere, vmem, vmem),
        scratch_shapes=[
            pltpu.VMEM((slots * count, LANES), F32),
            pltpu.VMEM((expert_total, each, LANES), BF16),
            pltpu.SemaphoreType.DMA((1,)),
        ],
        input_output_aliases={sources + 3: 0},
        compiler_params=pltpu.CompilerParams(vmem_limit_bytes=58 << 20),
    )(*parts, residual, moe_gain, ids, buffer)


def pack_weights(core, gate_up, down):
    _, d_local, ff_both = gate_up.shape
    ff_width = down.shape[1]
    tiles = ff_both // LANES
    height = tiles * d_local + ff_width

    def kernel(core_ref, g_ref, d_ref, keep_ref, send_ref):
        for out_ref, e in ((keep_ref, core_ref[0]), (send_ref, 1 - core_ref[0])):
            for i in range(tiles):
                out_ref[i * d_local : (i + 1) * d_local, :] = g_ref[e, :, i * LANES : (i + 1) * LANES]
            out_ref[tiles * d_local :, :] = d_ref[e]

    vmem = pl.BlockSpec(memory_space=pltpu.VMEM)
    shape = jax.ShapeDtypeStruct((height, LANES), BF16)
    return pl.pallas_call(
        kernel,
        out_shape=(shape, shape),
        in_specs=[pl.BlockSpec(memory_space=pltpu.SMEM), vmem, vmem],
        out_specs=(vmem, vmem),
        compiler_params=pltpu.CompilerParams(vmem_limit_bytes=58 << 20),
    )(core, gate_up, down)


def experts(core, rows_in, weights, ff_width, gu_rows):
    z_count, cores, _, _ = weights.shape
    count = z_count * cores
    dests = rows_in.shape[0]
    slots = dests * CAP
    ff_tiles = 2 * ff_width // LANES
    block = gu_rows // ff_tiles
    each = CAP * count

    def kernel(core_ref, x_ref, w_hbm, o_ref, x_s, g_s, xb_s, gb_s, w_ref, sems):
        copies = [pltpu.make_async_copy(w_hbm.at[z], w_ref.at[z], sems.at[z]) for z in range(z_count)]
        for copy in copies:
            copy.start()
        core = core_ref[0]
        x_s[...] = x_ref[:, :each, :].astype(F32).reshape(dests * each, LANES)
        g_s[...] = x_ref[:, each:, :].astype(F32).reshape(dests * each, LANES)
        order = [(z, s, z * cores + (core if s == 0 else 1 - core)) for z in range(z_count) for s in range(cores)]
        for i, (z, s, c) in enumerate(order):
            xb_s[:, i * LANES : (i + 1) * LANES] = take_tile(x_s, dests, c).astype(BF16)
            gb_s[:, i * LANES : (i + 1) * LANES] = take_tile(g_s, dests, c).astype(BF16)

        def tile(z, s, i):
            return w_ref[z, s, i * block : (i + 1) * block, :]

        for copy in copies:
            copy.wait()
        projected = []
        for first in range(0, ff_tiles, 2):
            used = range(first, min(first + 2, ff_tiles))
            rhs = jnp.concatenate(
                [jnp.concatenate([tile(z, s, i) for i in used], axis=1) for z, s, _ in order], axis=0
            )
            projected.append(mm(xb_s[...], rhs, NN))
        projected = jnp.concatenate(projected, axis=1)
        hidden_grad = []
        for first in range(0, ff_width, 256):
            size = min(256, ff_width - first)
            rhs = jnp.concatenate(
                [w_ref[z, s, gu_rows + first : gu_rows + first + size, :] for z, s, _ in order], axis=1
            )
            hidden_grad.append(mm(gb_s[...], rhs, NT))
        hidden_grad = jnp.concatenate(hidden_grad, axis=1)
        pre_gate = projected[:, :ff_width]
        pre_up = projected[:, ff_width:]
        sig = 1.0 / (1.0 + jnp.exp(-pre_gate))
        act = pre_gate * sig
        activated = (act * pre_up).astype(BF16)
        grad_gate = hidden_grad * pre_up * sig * (1.0 + pre_gate * (1.0 - sig))
        grad_up = hidden_grad * act
        grad_both = jnp.concatenate([grad_gate, grad_up], axis=1).astype(BF16)
        for z in range(z_count):
            rhs = jnp.concatenate([w_ref[z, s, gu_rows:, :] for s in range(cores)], axis=1)
            out = mm(activated, rhs, NN)
            rhs = jnp.concatenate(
                [jnp.concatenate([tile(z, s, i) for i in range(ff_tiles)], axis=1) for s in range(cores)], axis=0
            )
            grad = mm(grad_both, rhs, NT)
            places = [z * cores + core, z * cores + 1 - core]
            put_tiles(x_s, out, dests, places)
            put_tiles(g_s, grad, dests, places)
        o_ref[:, :each, :] = x_s[...].astype(BF16).reshape(dests, each, LANES)
        o_ref[:, each:, :] = g_s[...].astype(BF16).reshape(dests, each, LANES)

    vmem = pl.BlockSpec(memory_space=pltpu.VMEM)
    return pl.pallas_call(
        kernel,
        out_shape=jax.ShapeDtypeStruct((dests, 2 * each, LANES), BF16),
        in_specs=[pl.BlockSpec(memory_space=pltpu.SMEM), vmem, pl.BlockSpec(memory_space=pl.ANY)],
        out_specs=vmem,
        scratch_shapes=[
            pltpu.VMEM((dests * each, LANES), F32),
            pltpu.VMEM((dests * each, LANES), F32),
            pltpu.VMEM((slots, count * LANES), BF16),
            pltpu.VMEM((slots, count * LANES), BF16),
            pltpu.VMEM(weights.shape, BF16),
            pltpu.SemaphoreType.DMA((z_count,)),
        ],
        compiler_params=pltpu.CompilerParams(vmem_limit_bytes=58 << 20),
    )(core, rows_in, weights)


def combine(back, hidden, inv_rms, out_grad, moe_gain, ids_t, route_t, expert_total, owners, local_count):
    tokens, width = hidden.shape
    top = ids_t.shape[0]
    count = width // LANES
    slots = expert_total * CAP
    each = CAP * count

    def kernel(r_ref, h_ref, v_ref, g_ref, m_ref, i_ref, w_ref, layer_ref, res_ref, route_ref, o_s, b_s):
        o_s[...] = r_ref[:, :each, :].astype(F32).reshape(slots * count, LANES)
        b_s[...] = r_ref[:, each:, :].astype(F32).reshape(slots * count, LANES)
        masks = slot_masks(i_ref[...], expert_total, owners, local_count)
        eye = id_columns(i_ref[...])[1]
        routes = columns_of(w_ref[...], eye)
        weight = jnp.zeros((tokens, slots), F32)
        for k in range(top):
            weight = weight + jnp.where(masks[k], routes[:, k : k + 1], 0.0)
        hi = weight.astype(BF16)
        both = jnp.concatenate([hi, (weight - hi.astype(F32)).astype(BF16)], axis=0)

        def rows_of(ref):
            return jnp.concatenate(
                [take_tile(ref, expert_total, i).astype(BF16) for i in range(count)], axis=1
            )

        hidden = h_ref[...].astype(F32)
        grad = g_ref[...]
        outs = rows_of(o_s)
        mixed = mm(both, outs, NN)
        layer_ref[...] = (hidden + (mixed[:tokens] + mixed[tokens:])).astype(BF16)
        dots = mm(grad, outs, NT)
        lane = lax.broadcasted_iota(jnp.int32, (tokens, top), 1)
        route = jnp.zeros((tokens, top), F32)
        for k in range(top):
            one = jnp.sum(jnp.where(masks[k], dots, 0.0), axis=1, keepdims=True)
            route = jnp.where(lane == k, one, route)
        route_ref[...] = mm(route, eye, TN, HIGH)
        mixed = mm(both, rows_of(b_s), NN)
        inv = v_ref[:, 0:1]
        unit_grad = (mixed[:tokens] + mixed[tokens:]) * m_ref[...]
        unit_rows = hidden * inv
        mean = jnp.mean(unit_grad * unit_rows, axis=1, keepdims=True)
        res_ref[...] = (grad.astype(F32) + inv * (unit_grad - unit_rows * mean)).astype(BF16)

    shape = jax.ShapeDtypeStruct((tokens, width), BF16)
    return call(
        kernel,
        (shape, shape, jax.ShapeDtypeStruct((top, tokens), F32)),
        (pltpu.VMEM((slots * count, LANES), F32), pltpu.VMEM((slots * count, LANES), F32)),
    )(back, hidden, inv_rms, out_grad, moe_gain, ids_t, route_t)


def ring_route(count, shift):
    return [(i, (i + shift) % count) for i in range(count)]


def local(
    x_inner,
    bc_input,
    gate_input,
    conv_weight,
    bc_conv_weight,
    step_size,
    log_decay,
    skip_gain,
    norm_gain,
    out_weight,
    residual,
    moe_gain,
    expert_ids,
    route_weights,
    gate_up_weight,
    down_weight,
    out_grad,
):
    chips = ("zq", "zp")
    ctx = chips + ("core",)
    group = lax.axis_size("zp") * lax.axis_size("core")
    ctx_count = lax.axis_size("zq") * group
    x_count, y_count = lax.axis_size("x"), lax.axis_size("y")
    owners = x_count * y_count
    heads = step_size.shape[1]
    channels = x_inner.shape[1]
    state_size = bc_input.shape[1] // 2
    local_count, _, _ = gate_up_weight.shape
    ff_width = down_weight.shape[1]
    expert_total = local_count * owners
    exchange = ("core", "x", "y")

    ids_t, route_t = expert_ids.T, route_weights.T
    step_t, decay_t = step_size.T, log_decay.T
    core = lax.axis_index("core").astype(jnp.int32).reshape(1)

    last = jnp.concatenate([x_inner[-8:], bc_input[-8:]], axis=1)
    rim = lax.ppermute(last, ctx, [(i, i + 1) for i in range(ctx_count - 1)])

    folded = (out_weight.astype(F32) * norm_gain[:, None]).astype(BF16)
    half = folded.shape[0] // 2
    from_prev = lax.ppermute(folded, "y", ring_route(y_count, 1))
    from_next = lax.ppermute(folded, "y", ring_route(y_count, -1))
    far_a = lax.ppermute(from_prev[:half], "y", ring_route(y_count, 1))
    far_b = lax.ppermute(from_next[half:], "y", ring_route(y_count, -1))

    kept, other = pack_weights(core, gate_up_weight, down_weight)
    swapped = lax.ppermute(other, "core", [(0, 1), (1, 0)])

    conv, held_in, sent = mixer_state(x_inner, bc_input, rim, conv_weight, bc_conv_weight, step_t, decay_t, group)
    near = lax.all_to_all(sent, ("zp", "core"), split_axis=0, concat_axis=0, tiled=True)
    kept, swapped, conv = lax.optimization_barrier((kept, swapped, conv))
    stacked = jnp.stack([kept, swapped])
    weights = lax.all_gather(stacked, chips, axis=0, tiled=False)
    gu_rows = kept.shape[0] - ff_width
    y_local, e_cols = mixer_rows(conv, held_in, step_t, decay_t, skip_gain, channels)
    place = (lax.axis_index("zp") * lax.axis_size("core") + lax.axis_index("core")).astype(jnp.int32).reshape(1)
    far_place = lax.axis_index("zq").astype(jnp.int32).reshape(1)
    own_state, own_log, window = join_near(place, near, state_size, lax.axis_size("zq"))
    windows = lax.all_to_all(window, "zq", split_axis=0, concat_axis=0, tiled=True)

    buffer = dispatch_grads(ids_t, out_grad, expert_total, owners, local_count)
    arriving = join_far(far_place, windows, own_state, own_log)
    y_at = lax.axis_index("y").astype(jnp.int32).reshape(1)
    x_at = lax.axis_index("x").astype(jnp.int32).reshape(1)
    gated = gate_rows(y_at, y_local, conv, e_cols, arriving, gate_input, heads, x_count, y_count)
    gated = [gated[0]] + [
        lax.ppermute(gated[k], "y", ring_route(y_count, k)) for k in range(1, y_count)
    ]
    pieces = [(folded,), (from_prev,), (far_a, far_b), (from_next,)]
    parts = project(x_at, gated, pieces, x_count)
    parts = [parts[0]] + [
        lax.ppermute(parts[k], "x", ring_route(x_count, k)) for k in range(1, x_count)
    ]
    sent_rows, hidden, inv_rms = normalise(
        buffer, parts, residual, moe_gain[None, :], ids_t, channels * owners, expert_total, owners, local_count
    )
    rows_in = lax.all_to_all(sent_rows, exchange, split_axis=0, concat_axis=0, tiled=True)
    back = experts(core, rows_in, weights, ff_width, gu_rows)
    back = lax.all_to_all(back, exchange, split_axis=0, concat_axis=0, tiled=True)
    layer, res, route = combine(
        back, hidden, inv_rms, out_grad, moe_gain[None, :], ids_t, route_t, expert_total, owners, local_count
    )
    return layer, res, route.T


def solution(mesh):
    ctx_count, exp_count = mesh.devices.shape
    side = int(round(exp_count**0.5))
    devices = mesh.devices.reshape(ctx_count // 4, 2, 2, side, exp_count // side)
    fine = Mesh(devices, ("zq", "zp", "core", "x", "y"))
    ctx, exp = ("zq", "zp", "core"), ("x", "y")
    token = P(ctx + exp, None)
    return jax.shard_map(
        local,
        mesh=fine,
        in_specs=(
            P(ctx, exp),
            P(ctx, None),
            P(ctx, exp),
            P(None, exp),
            P(),
            P(ctx, exp),
            P(ctx, exp),
            P(exp),
            P(exp),
            P(exp, None),
            token,
            P(),
            token,
            token,
            P(exp, ctx, None),
            P(exp, None, ctx),
            token,
        ),
        out_specs=(token, token, token),
        check_vma=False,
    )
```
